32 devices in a mesh: seq: 16 (over z, x, core), tp: 2 (over y).
Axes of the slice: x: 2, y: 2, z: 4, core: 2. Of those that a mesh axis runs over, the one named last changes fastest.
Arguments:
- tokens: bfloat16 [4, 1024, 2048], P(None, 'seq'), may hold values from -6 to 6
- cotangent: bfloat16 [4, 1024, 2048], P(None, 'seq'), may hold values from -6 to 6
- head_groups: int32 [4, 1024], P(None, 'seq'), may hold values from 1 to 4
- ffn_widths: int32 [4, 1024], P(None, 'seq'), may hold values from 1 to 4
- doc_lengths: int32 [4, 6], replicated, may hold values from 1 to 576, 1024 in all within a row
- first_gain: bfloat16 [2048], P('seq'), may hold values from 0.5 to 1.5
- first_shift: bfloat16 [2048], P('seq'), may hold values from -2 to 2
- router_weight: bfloat16 [8, 2048], P(None, 'seq'), may hold values from -0.125 to 0.125
- in_weight: bfloat16 [2048, 3, 16, 128], P('seq', None, 'tp'), may hold values from -0.125 to 0.125
- in_bias: bfloat16 [3, 16, 128], P(None, 'tp', 'seq'), may hold values from -2 to 2
- out_weight: bfloat16 [16, 128, 2048], P('tp', None, 'seq'), may hold values from -1 to 1
- out_bias: bfloat16 [2048], P('seq'), may hold values from -2 to 2
- second_gain: bfloat16 [2048], P('seq'), may hold values from 0.5 to 1.5
- second_shift: bfloat16 [2048], P('seq'), may hold values from -2 to 2
- up_weight: bfloat16 [2048, 8192], P('seq', 'tp'), may hold values from -0.125 to 0.125
- up_bias: bfloat16 [4, 2048], P('tp', 'seq'), may hold values from -3 to 3
- down_weight: bfloat16 [8192, 2048], P('tp', 'seq'), may hold values from -0.0625 to 0.0625
- down_bias: bfloat16 [2048], P('seq'), may hold values from -2 to 2
Outputs:
- block_out: bfloat16 [4, 1024, 2048], P(None, 'seq')
- tokens_grad: float32 [4, 1024, 2048], P(None, 'seq')
- grad_first_gain: float32 [2048], P('seq')
- grad_first_shift: float32 [2048], P('seq')
- grad_router: float32 [8, 2048], P(None, 'seq')
- grad_in_weight: float32 [2048, 3, 16, 128], P('seq', None, 'tp')
- grad_in_bias: float32 [3, 16, 128], P(None, 'tp', 'seq')
- grad_out_weight: float32 [16, 128, 2048], P('tp', None, 'seq')
- grad_out_bias: float32 [2048], P('seq')
- grad_second_gain: float32 [2048], P('seq')
- grad_second_shift: float32 [2048], P('seq')
- grad_up_weight: float32 [2048, 8192], P('seq', 'tp')
- grad_up_bias: float32 [4, 2048], P('tp', 'seq')
- grad_down_weight: float32 [8192, 2048], P('tp', 'seq')
- grad_down_bias: float32 [2048], P('seq')
The draws below stay inside these ranges and needn't reach their ends.
Inputs may be any that keep to these rules, and one draw needn't show every extreme that they name: `doc_lengths`: each row holds the lengths of the 6 documents of one packed sequence in order; they sum to 1024, and the longest is exactly 576.
All inputs are finite; a program needn't handle non-finite values.
Results may differ from the reference program's by a relative error of at most 0.0095.
The reference program's roundings to bfloat16 on the way count: a program that leaves them out, or rounds other values in their place, can miss the bound.
Values may be sent and summed in bfloat16 or wider, within the bound.
No kernel may reach another device: no remote copies, remote signals or barrier semaphores. Data moves between devices by JAX's collectives and lax.ppermute only.
A program may use at most 640 MiB of HBM per device.

```python
import math
import jax
import jax.numpy as jnp
import numpy as np
from jax import lax

D = 2048
HEADS = 16
HEAD_DIM = 128
FF = 8192
GROUPS = 4
DOCS = 6
MICRO = 4
TOK_DEV = 64
LENGTH = 1024


def plant(values, rng, least, high):
    extent = values.shape
    spot = [jax.random.randint(jax.random.fold_in(rng, axis), (), 0, extent[axis]) for axis in range(len(extent))]
    values = values.at[tuple(spot)].set(least)
    longest = extent.index(max(extent))
    spot[longest] = (spot[longest] + 1) % extent[longest]
    return values.at[tuple(spot)].set(high)


def raised(values, own_key, source, target, shards_of, factor):
    def block_of(dim):
        return (jnp.arange(values.shape[dim]) // (values.shape[dim] // shards_of)).reshape((-1,) + (1,) * (values.ndim - 1 - dim))

    first = jax.random.permutation(own_key, shards_of)[block_of(target)]
    far = (block_of(target) + shards_of // 2) % shards_of
    return jnp.where((block_of(source) == first) | (block_of(source) == far), factor * values, values)


def steps_of(rng, dims, shards, low, high):
    factor_of = 1.0
    for dim, shards_of in shards:
        steps = jax.random.uniform(jax.random.fold_in(jax.random.fold_in(rng, 6), dim), (shards_of,), jnp.float32, low / len(shards), high / len(shards))
        factor_of = factor_of * jnp.repeat(jnp.exp(steps), dims[dim] // shards_of).reshape((-1,) + (1,) * (len(dims) - 1 - dim))
    return factor_of


def length_profile(count, total, bound, skew):
    portions = [(1 << 20) // math.isqrt(grade ** skew) + 1 for grade in range(2, count + 1)]
    surplus, holding = total - bound - (count - 1), [1] * (count - 1)
    while surplus > 0:
        movable = [i for i in range(count - 1) if holding[i] < bound]
        pool, remaining = sum([portions[i] for i in movable]), surplus
        for i in movable:
            extra = min(bound - holding[i], max(1, remaining * portions[i] // pool), surplus)
            holding[i] = holding[i] + extra
            surplus = surplus - extra
    return np.array([bound] + holding)


def ragged(key, number_of, total, bound, lean):
    if number_of == 2:
        one = jax.random.randint(key, (), max(1, total - bound), min(bound, total - 1) + 1)
        return jnp.stack([one, total - one])
    tallies = jnp.asarray(length_profile(number_of, total, bound, lean), jnp.int32)
    couples = (number_of - 1) // 2
    donor, sink = tallies[1:1 + 2 * couples:2], tallies[2:2 + 2 * couples:2]
    margin = jnp.minimum(donor - 1, bound - sink)
    moved = jax.random.randint(jax.random.fold_in(key, 1), (couples,), 0, 1 << 20) % (margin + 1)
    tallies = tallies.at[1:1 + 2 * couples:2].set(donor - moved).at[2:2 + 2 * couples:2].set(sink + moved)
    return tallies[jax.random.permutation(jax.random.fold_in(key, 2), number_of)]


def normal_values(stream_key, shape, width, bound, pieces=(), kind=jnp.bfloat16):
    array = jax.random.normal(stream_key, shape, jnp.float32) * width
    if len(pieces) > 0:
        array = steps_of(stream_key, shape, pieces, -0.22, 0.18) * array
    return jnp.clip(array, min=-bound, max=bound).astype(kind)


def heavy_noise(stream_key, dims, width, limit, pieces, heavy, held_as=jnp.bfloat16):
    result = width * jax.random.normal(stream_key, dims, jnp.float32)
    if pieces:
        result = result * steps_of(stream_key, dims, pieces, -0.22, 0.18)
    return jnp.clip(raised(result, jax.random.fold_in(stream_key, 3), *heavy), -limit, limit).astype(held_as)


def setup_inputs(seed: int = 0) -> dict:
    splits = jax.random.split(jax.random.key(seed), 19)
    return {
        "tokens": normal_values(splits[0], (MICRO, LENGTH, D), 1.0, 6.0, ((1, 16),)),
        "cotangent": heavy_noise(splits[1], (MICRO, LENGTH, D), 1.0, 6.0, ((1, 16),), (1, 2, 16, 2.0)),
        "head_groups": plant(jax.random.randint(splits[2], (MICRO, LENGTH), 1, GROUPS + 1), jax.random.fold_in(splits[2], 1), 1, GROUPS).astype(jnp.int32),
        "ffn_widths": plant(jax.random.randint(splits[3], (MICRO, LENGTH), 1, GROUPS + 1), jax.random.fold_in(splits[3], 1), 1, GROUPS).astype(jnp.int32),
        "doc_lengths": jax.vmap(lambda own: ragged(own, DOCS, LENGTH, LENGTH // 2 + TOK_DEV, 1))(jax.random.split(splits[4], MICRO)).reshape((MICRO, DOCS)).astype(jnp.int32),
        "first_gain": jnp.clip(1.0 + 0.1 * jax.random.normal(splits[5], (D,), jnp.float32), 0.5, 1.5).astype(jnp.bfloat16),
        "first_shift": normal_values(splits[6], (D,), 0.3, 2.0, ((0, 16),)),
        "router_weight": normal_values(splits[7], (2 * GROUPS, D), D ** -0.5, 0.125, ((1, 16),)),
        "in_weight": normal_values(splits[8], (D, 3, HEADS, HEAD_DIM), D ** -0.5, 0.125, ((0, 16), (2, 2))),
        "in_bias": normal_values(splits[9], (3, HEADS, HEAD_DIM), 0.3, 2.0, ((1, 2), (2, 16))),
        "out_weight": normal_values(splits[10], (HEADS, HEAD_DIM, D), (max(1, HEADS * HEAD_DIM // 64)) ** -0.5, 1.0, ((0, 2), (2, 16))),
        "out_bias": normal_values(splits[11], (D,), 0.3, 2.0, ((0, 16),)),
        "second_gain": jnp.clip(1.0 + 0.1 * jax.random.normal(splits[12], (D,), jnp.float32), 0.5, 1.5).astype(jnp.bfloat16),
        "second_shift": normal_values(splits[13], (D,), 0.3, 2.0, ((0, 16),)),
        "up_weight": normal_values(splits[14], (D, FF), D ** -0.5, 0.125, ((0, 16), (1, 2))),
        "up_bias": normal_values(splits[15], (GROUPS, FF // GROUPS), 0.5, 3.0, ((0, 2), (1, 16))),
        "down_weight": normal_values(splits[16], (FF, D), FF ** -0.5, 0.0625, ((0, 2), (1, 16))),
        "down_bias": normal_values(splits[17], (D,), 0.3, 2.0, ((0, 16),)),
    }


HIGHEST = lax.Precision.HIGHEST

@jax.custom_vjp
def low(v):
    return lax.optimization_barrier(v.astype(jnp.bfloat16)).astype(jnp.float32)

@jax.custom_vjp
def low_back(v):
    return v

def low_keep(v):
    return (low(v), None)

def low_pass(kept, grad):
    return (grad,)

def back_keep(v):
    return (v, None)

def back_low(kept, grad):
    return (low(grad),)
low.defvjp(low_keep, low_pass)
low_back.defvjp(back_keep, back_low)

def norm_rows(rows, gain, shift):
    center = rows - lax.optimization_barrier(jnp.mean(rows, axis=-1, keepdims=True))
    inverse = lax.rsqrt(lax.optimization_barrier(jnp.mean(center * center, axis=-1, keepdims=True)) + 1e-05)
    return center * inverse * gain + shift

def rotary_tables(positions):
    half_dim = HEAD_DIM // 2
    steps_up = jnp.arange(half_dim, dtype=jnp.float32) * (2.0 / HEAD_DIM)
    inverse = jnp.exp(-math.log(10000.0) * steps_up)
    angles = positions.astype(jnp.float32)[:, None] * inverse[None, :]
    angles = jnp.concatenate([angles, angles], axis=1)
    return (jnp.cos(angles), jnp.sin(angles))

def rotate(vectors, cosine, sine):
    half_dim = vectors.shape[-1] // 2
    turned = jnp.concatenate([-vectors[..., half_dim:], vectors[..., :half_dim]], axis=-1)
    return vectors * cosine[:, None, :] + turned * sine[:, None, :]

def doc_index(lengths, positions):
    ends = jnp.cumsum(lengths)
    return lax.optimization_barrier(jnp.sum((positions[:, None] >= ends[None, :]).astype(jnp.int32), axis=1))

def layer(params, rows, heads_row, widths_row, doc_ids):
    first_gain, first_shift, router_weight, in_weight, in_bias, out_weight, out_bias, second_gain, second_shift, up_weight, up_bias, down_weight, down_bias = params
    length = rows.shape[0]
    positions = jnp.arange(length, dtype=jnp.int32)
    cosine, sine = rotary_tables(positions)
    normed = low(norm_rows(rows, first_gain, first_shift))
    logits = jnp.dot(normed, router_weight.T, precision=HIGHEST)
    attn_prob = jax.nn.softmax(logits[:, :GROUPS], axis=-1)
    ffn_prob = jax.nn.softmax(logits[:, GROUPS:], axis=-1)
    options = jnp.arange(GROUPS, dtype=jnp.int32)
    attn_pick = (options[None, :] == heads_row[:, None] - 1).astype(jnp.float32)
    ffn_pick = (options[None, :] == widths_row[:, None] - 1).astype(jnp.float32)
    attn_gate = GROUPS * lax.optimization_barrier(jnp.sum(attn_prob * attn_pick, axis=-1))
    ffn_gate = GROUPS * lax.optimization_barrier(jnp.sum(ffn_prob * ffn_pick, axis=-1))
    projected = jnp.dot(normed, in_weight.reshape(D, 3 * HEADS * HEAD_DIM), precision=HIGHEST)
    projected = low_back(projected.reshape(length, 3, HEADS, HEAD_DIM) + in_bias)
    queries = low(rotate(projected[:, 0], cosine, sine))
    keys = low(rotate(projected[:, 1], cosine, sine))
    values = low(projected[:, 2])
    scale = HEAD_DIM ** (-0.5)
    block_rows = min(512, length)
    block_count = length // block_rows

    def attend(block):
        query_block, block_pos, block_doc = block
        raw_scores = low_back(jnp.einsum('qhd,khd->hqk', query_block, keys, precision=HIGHEST))
        allowed = (positions[None, :] <= block_pos[:, None]) & (doc_ids[None, :] == block_doc[:, None])
        scores = jnp.where(allowed[None], raw_scores * scale, -jnp.inf)
        row_max = lax.optimization_barrier(jnp.max(scores, axis=-1, keepdims=True))
        weights = jnp.exp(scores - row_max)
        probs = low(weights / lax.optimization_barrier(jnp.sum(weights, axis=-1, keepdims=True)))
        return low_back(jnp.einsum('hqk,khd->qhd', probs, values, precision=HIGHEST))
    attended = lax.map(jax.checkpoint(attend), (queries.reshape(block_count, block_rows, HEADS, HEAD_DIM), positions.reshape(block_count, block_rows), doc_ids.reshape(block_count, block_rows)))
    attended = attended.reshape(length, HEADS, HEAD_DIM)
    head_ids = jnp.arange(HEADS, dtype=jnp.int32)
    head_active = (head_ids[None, :] // (HEADS // GROUPS) < heads_row[:, None]).astype(jnp.float32)
    mixed_heads = low(attended * head_active[:, :, None])
    attn_sum = low_back(jnp.dot(mixed_heads.reshape(length, HEADS * HEAD_DIM), out_weight.reshape(HEADS * HEAD_DIM, D), precision=HIGHEST))
    resid = rows + attn_gate[:, None] * (attn_sum + out_bias)
    normed_two = low(norm_rows(resid, second_gain, second_shift))
    up_pre = low_back(jnp.dot(normed_two, up_weight, precision=HIGHEST) + up_bias.reshape(FF))
    unit_ids = jnp.arange(FF, dtype=jnp.int32)
    unit_active = (unit_ids[None, :] // (FF // GROUPS) < widths_row[:, None]).astype(jnp.float32)
    hidden = low(unit_active * jnp.square(jnp.maximum(up_pre, 0.0)))
    down_sum = low_back(jnp.dot(hidden, down_weight, precision=HIGHEST))
    return resid + ffn_gate[:, None] * (down_sum + down_bias)

def reference(tokens, cotangent, head_groups, ffn_widths, doc_lengths, first_gain, first_shift, router_weight, in_weight, in_bias, out_weight, out_bias, second_gain, second_shift, up_weight, up_bias, down_weight, down_bias):
    params = (first_gain.astype(jnp.float32), first_shift.astype(jnp.float32), router_weight.astype(jnp.float32), in_weight.astype(jnp.float32), in_bias.astype(jnp.float32), out_weight.astype(jnp.float32), out_bias.astype(jnp.float32), second_gain.astype(jnp.float32), second_shift.astype(jnp.float32), up_weight.astype(jnp.float32), up_bias.astype(jnp.float32), down_weight.astype(jnp.float32), down_bias.astype(jnp.float32))

    def one_batch(totals, batch):
        rows, upstream, heads_row, widths_row, lengths_row = batch
        doc_ids = doc_index(lengths_row, jnp.arange(rows.shape[0], dtype=jnp.int32))

        def forward(param_list, inputs):
            return layer(param_list, inputs, heads_row, widths_row, doc_ids)
        output, pullback = jax.vjp(forward, params, rows.astype(jnp.float32))
        param_grads, input_grad = pullback(upstream.astype(jnp.float32))
        totals = jax.tree.map(jnp.add, totals, param_grads)
        return (totals, (output.astype(jnp.bfloat16), input_grad))
    zeros = jax.tree.map(jnp.zeros_like, params)
    totals, outputs = lax.scan(one_batch, zeros, (tokens, cotangent, head_groups, ffn_widths, doc_lengths))
    return (outputs[0], outputs[1], totals[0], totals[1], totals[2], totals[3], totals[4], totals[5], totals[6], totals[7], totals[8], totals[9], totals[10], totals[11], totals[12])
```

```python
import math

import jax
import jax.numpy as jnp
from jax import lax
from jax.sharding import Mesh
from jax.sharding import PartitionSpec as P

HEADS = 16
HEAD_DIM = 128
FF = 8192
GROUPS = 4


EPSILON = 1e-05
HIGHEST = lax.Precision.HIGHEST


def norm_forward(rows, gain, shift):
    center = rows - jnp.mean(rows, axis=-1, keepdims=True)
    inverse = lax.rsqrt(jnp.mean(center * center, axis=-1, keepdims=True) + EPSILON)
    scaled = center * inverse
    return (scaled * gain + shift, scaled, inverse)


def norm_backward(upstream, scaled, inverse, gain):
    through = upstream * gain
    return inverse * (
        through
        - jnp.mean(through, axis=-1, keepdims=True)
        - scaled * jnp.mean(through * scaled, axis=-1, keepdims=True)
    )


def rotary_tables(positions):
    half_dim = HEAD_DIM // 2
    steps_up = jnp.arange(half_dim, dtype=jnp.float32) * (2.0 / HEAD_DIM)
    inverse = jnp.exp(-math.log(10000.0) * steps_up)
    angles = positions.astype(jnp.float32)[:, None] * inverse[None, :]
    angles = jnp.concatenate([angles, angles], axis=1)
    return (jnp.cos(angles), jnp.sin(angles))


def rotate(vectors, cosine, sine):
    half_dim = vectors.shape[-1] // 2
    turned = jnp.concatenate([-vectors[..., half_dim:], vectors[..., :half_dim]], axis=-1)
    return vectors * cosine[:, None, :] + turned * sine[:, None, :]


def rotate_back(grads, cosine, sine):
    half_dim = grads.shape[-1] // 2
    moved = grads * sine[:, None, :]
    turned = jnp.concatenate([moved[..., half_dim:], -moved[..., :half_dim]], axis=-1)
    return grads * cosine[:, None, :] + turned


def doc_index(lengths, positions):
    ends = jnp.cumsum(lengths)
    return jnp.sum((positions[:, None] >= ends[None, :]).astype(jnp.int32), axis=1)


def gate_logit_grad(prob, pick, gate_grad):
    chosen = jnp.sum(prob * pick, axis=-1, keepdims=True)
    return GROUPS * chosen * (pick - prob) * gate_grad[:, None]


def local(
    tokens,
    cotangent,
    head_groups,
    ffn_widths,
    doc_lengths,
    first_gain,
    first_shift,
    router_weight,
    in_weight,
    in_bias,
    out_weight,
    out_bias,
    second_gain,
    second_shift,
    up_weight,
    up_bias,
    down_weight,
    down_bias,
):
    seq_count = lax.axis_size("seq")
    seq_index = lax.axis_index("seq")
    tp_index = lax.axis_index("tp")
    gathered = (
        lax.all_gather(first_gain, "seq", axis=0, tiled=True),
        lax.all_gather(first_shift, "seq", axis=0, tiled=True),
        lax.all_gather(router_weight, "seq", axis=1, tiled=True),
        lax.all_gather(in_weight, "seq", axis=0, tiled=True),
        lax.all_gather(in_bias, "seq", axis=2, tiled=True),
        lax.all_gather(out_weight, "seq", axis=2, tiled=True),
        lax.all_gather(out_bias, "seq", axis=0, tiled=True),
        lax.all_gather(second_gain, "seq", axis=0, tiled=True),
        lax.all_gather(second_shift, "seq", axis=0, tiled=True),
        lax.all_gather(up_weight, "seq", axis=0, tiled=True),
        lax.all_gather(up_bias, "seq", axis=1, tiled=True),
        lax.all_gather(down_weight, "seq", axis=1, tiled=True),
        lax.all_gather(down_bias, "seq", axis=0, tiled=True),
    )
    (
        gain_one,
        shift_one,
        router_full,
        in_full,
        in_bias_full,
        out_full,
        out_bias_full,
        gain_two,
        shift_two,
        up_full,
        up_bias_full,
        down_full,
        down_bias_full,
    ) = gathered
    micro, tok_dev, width = tokens.shape
    local_heads = in_full.shape[2]
    head_dim = in_full.shape[3]
    inner = local_heads * head_dim
    local_units = up_full.shape[1]
    length = tok_dev * seq_count
    scale = HEAD_DIM ** (-0.5)
    gain_one_f = gain_one.astype(jnp.float32)
    shift_one_f = shift_one.astype(jnp.float32)
    gain_two_f = gain_two.astype(jnp.float32)
    shift_two_f = shift_two.astype(jnp.float32)
    out_bias_f = out_bias_full.astype(jnp.float32)
    down_bias_f = down_bias_full.astype(jnp.float32)
    router_wide = router_full.astype(jnp.float32)
    bias_in = in_bias_full.astype(jnp.float32)
    up_bias_vec = up_bias_full.reshape(local_units).astype(jnp.float32)
    in_matrix = in_full.reshape(width, 3 * inner)
    out_matrix = out_full.reshape(inner, width)
    positions_all = jnp.arange(length, dtype=jnp.int32)
    positions_local = seq_index * tok_dev + jnp.arange(tok_dev, dtype=jnp.int32)
    cosine, sine = rotary_tables(positions_local)
    head_ids = tp_index * local_heads + jnp.arange(local_heads, dtype=jnp.int32)
    unit_ids = tp_index * local_units + jnp.arange(local_units, dtype=jnp.int32)
    options = jnp.arange(GROUPS, dtype=jnp.int32)
    grad_gain_one = jnp.zeros((width,), jnp.float32)
    grad_shift_one = jnp.zeros((width,), jnp.float32)
    grad_router = jnp.zeros(router_full.shape, jnp.float32)
    grad_in = jnp.zeros((width, 3 * inner), jnp.float32)
    grad_in_bias = jnp.zeros(in_bias_full.shape, jnp.float32)
    grad_out = jnp.zeros((inner, width), jnp.float32)
    grad_out_bias = jnp.zeros((width,), jnp.float32)
    grad_gain_two = jnp.zeros((width,), jnp.float32)
    grad_shift_two = jnp.zeros((width,), jnp.float32)
    grad_up = jnp.zeros(up_full.shape, jnp.float32)
    grad_up_bias = jnp.zeros((local_units,), jnp.float32)
    grad_down = jnp.zeros(down_full.shape, jnp.float32)
    grad_down_bias = jnp.zeros((width,), jnp.float32)
    outputs = []
    input_grads = []
    for batch in range(micro):
        rows = tokens[batch].astype(jnp.float32)
        doc_all = doc_index(doc_lengths[batch], positions_all)
        doc_local = lax.dynamic_slice_in_dim(doc_all, seq_index * tok_dev, tok_dev, 0)
        allowed = (positions_all[None, :] <= positions_local[:, None]) & (
            doc_all[None, :] == doc_local[:, None]
        )
        head_active = (head_ids[None, :] // (HEADS // GROUPS) < head_groups[batch][:, None]).astype(
            jnp.float32
        )
        unit_active = (unit_ids[None, :] // (FF // GROUPS) < ffn_widths[batch][:, None]).astype(
            jnp.float32
        )
        normed, scaled_one, inverse_one = norm_forward(rows, gain_one_f, shift_one_f)
        normed_low = normed.astype(jnp.bfloat16)
        logits = jnp.dot(normed_low, router_full.T, preferred_element_type=jnp.float32)
        attn_prob = jax.nn.softmax(logits[:, :GROUPS], axis=-1)
        ffn_prob = jax.nn.softmax(logits[:, GROUPS:], axis=-1)
        attn_pick = (options[None, :] == head_groups[batch][:, None] - 1).astype(jnp.float32)
        ffn_pick = (options[None, :] == ffn_widths[batch][:, None] - 1).astype(jnp.float32)
        attn_gate = GROUPS * jnp.sum(attn_prob * attn_pick, axis=-1)
        ffn_gate = GROUPS * jnp.sum(ffn_prob * ffn_pick, axis=-1)
        projected = jnp.dot(normed_low, in_matrix, preferred_element_type=jnp.float32)
        projected = projected.reshape(tok_dev, 3, local_heads, head_dim) + bias_in
        queries = rotate(projected[:, 0], cosine, sine).astype(jnp.bfloat16)
        keys_low = rotate(projected[:, 1], cosine, sine).astype(jnp.bfloat16)
        values_low = projected[:, 2].astype(jnp.bfloat16)
        keys_all, values_all = (
            lax.all_gather(keys_low, "seq", axis=0, tiled=True),
            lax.all_gather(values_low, "seq", axis=0, tiled=True),
        )
        raw_scores = jnp.einsum(
            "qhd,khd->hqk", queries, keys_all, preferred_element_type=jnp.float32
        )
        scores = jnp.where(allowed[None], raw_scores * scale, -jnp.inf)
        row_max = jnp.max(scores, axis=-1, keepdims=True)
        weights = jnp.exp(scores - row_max)
        row_total = jnp.sum(weights, axis=-1, keepdims=True)
        log_total = row_max + jnp.log(row_total)
        probs = weights / row_total
        attended = jnp.einsum(
            "hqk,khd->qhd",
            probs.astype(jnp.bfloat16),
            values_all,
            preferred_element_type=jnp.float32,
        )
        mixed_heads = (attended * head_active[:, :, None]).astype(jnp.bfloat16)
        mixed_flat = mixed_heads.reshape(tok_dev, inner)
        attn_part = jnp.dot(mixed_flat, out_matrix, preferred_element_type=jnp.float32)
        attn_sum = lax.psum(attn_part, "tp")
        attn_branch = attn_sum + out_bias_f
        resid = rows + attn_gate[:, None] * attn_branch
        normed_two, scaled_two, inverse_two = norm_forward(resid, gain_two_f, shift_two_f)
        normed_two_low = normed_two.astype(jnp.bfloat16)
        up_pre = jnp.dot(normed_two_low, up_full, preferred_element_type=jnp.float32) + up_bias_vec
        relu_part = jnp.maximum(up_pre, 0.0)
        hidden = (unit_active * jnp.square(relu_part)).astype(jnp.bfloat16)
        down_part = jnp.dot(hidden, down_full, preferred_element_type=jnp.float32)
        down_sum = lax.psum(down_part.astype(jnp.bfloat16), "tp").astype(jnp.float32)
        ffn_branch = down_sum + down_bias_f
        outputs.append((resid + ffn_gate[:, None] * ffn_branch).astype(jnp.bfloat16))
        upstream = cotangent[batch].astype(jnp.float32)
        ffn_gate_grad = jnp.sum(upstream * ffn_branch, axis=-1)
        gated_up = ffn_gate[:, None] * upstream
        grad_down_bias = grad_down_bias + jnp.sum(gated_up, axis=0)
        down_grad = gated_up.astype(jnp.bfloat16)
        grad_down = grad_down + jnp.einsum(
            "tf,td->fd", hidden, down_grad, preferred_element_type=jnp.float32
        )
        hidden_grad = jnp.einsum(
            "td,fd->tf", down_grad, down_full, preferred_element_type=jnp.float32
        )
        up_grad = (hidden_grad * unit_active * 2.0 * relu_part).astype(jnp.bfloat16)
        grad_up_bias = grad_up_bias + jnp.sum(up_grad.astype(jnp.float32), axis=0)
        grad_up = grad_up + jnp.einsum(
            "td,tf->df", normed_two_low, up_grad, preferred_element_type=jnp.float32
        )
        normed_two_part = jnp.einsum(
            "tf,df->td", up_grad, up_full, preferred_element_type=jnp.float32
        )
        normed_two_grad = lax.psum(normed_two_part, "tp")
        grad_gain_two = grad_gain_two + jnp.sum(normed_two_grad * scaled_two, axis=0)
        grad_shift_two = grad_shift_two + jnp.sum(normed_two_grad, axis=0)
        resid_grad = upstream + norm_backward(normed_two_grad, scaled_two, inverse_two, gain_two_f)
        attn_gate_grad = jnp.sum(resid_grad * attn_branch, axis=-1)
        gated_attn = attn_gate[:, None] * resid_grad
        grad_out_bias = grad_out_bias + jnp.sum(gated_attn, axis=0)
        attn_out_grad = gated_attn.astype(jnp.bfloat16)
        grad_out = grad_out + jnp.einsum(
            "ti,td->id", mixed_flat, attn_out_grad, preferred_element_type=jnp.float32
        )
        mixed_grad = jnp.einsum(
            "td,id->ti", attn_out_grad, out_matrix, preferred_element_type=jnp.float32
        )
        attended_grad = (
            mixed_grad.reshape(tok_dev, local_heads, head_dim) * head_active[:, :, None]
        ).astype(jnp.bfloat16)
        again_raw = jnp.einsum(
            "qhd,khd->hqk", queries, keys_all, preferred_element_type=jnp.float32
        )
        again_scores = jnp.where(allowed[None], again_raw * scale, -jnp.inf)
        probs_again = jnp.exp(again_scores - log_total)
        prob_grad = jnp.einsum(
            "qhd,khd->hqk", attended_grad, values_all, preferred_element_type=jnp.float32
        )
        row_dot = jnp.sum(probs_again * prob_grad, axis=-1, keepdims=True)
        score_grad = (probs_again * (prob_grad - row_dot) * scale).astype(jnp.bfloat16)
        query_rot_grad = jnp.einsum(
            "hqk,khd->qhd", score_grad, keys_all, preferred_element_type=jnp.float32
        )
        probs_low = probs_again.astype(jnp.bfloat16)
        key_part = jnp.einsum(
            "hqk,qhd->khd", score_grad, queries, preferred_element_type=jnp.float32
        )
        value_part = jnp.einsum(
            "hqk,qhd->khd", probs_low, attended_grad, preferred_element_type=jnp.float32
        )
        combined = lax.psum_scatter(
            jnp.concatenate([key_part, value_part], axis=1).reshape(
                lax.axis_size("seq") * tok_dev, 2 * inner
            ),
            "seq",
            scatter_dimension=0,
            tiled=True,
        )
        combined = combined.reshape(tok_dev, 2 * local_heads, head_dim)
        key_rot_grad = combined[:, :local_heads]
        value_grad = combined[:, local_heads:]
        query_grad = rotate_back(query_rot_grad, cosine, sine)
        key_grad = rotate_back(key_rot_grad, cosine, sine)
        proj_grad = jnp.stack([query_grad, key_grad, value_grad], axis=1).astype(jnp.bfloat16)
        grad_in_bias = grad_in_bias + jnp.sum(proj_grad.astype(jnp.float32), axis=0)
        proj_flat = proj_grad.reshape(tok_dev, 3 * inner)
        grad_in = grad_in + jnp.einsum(
            "tw,tc->wc", normed_low, proj_flat, preferred_element_type=jnp.float32
        )
        normed_part = jnp.einsum(
            "tc,wc->tw", proj_flat, in_matrix, preferred_element_type=jnp.float32
        )
        logit_grad = jnp.concatenate(
            [
                gate_logit_grad(attn_prob, attn_pick, attn_gate_grad),
                gate_logit_grad(ffn_prob, ffn_pick, ffn_gate_grad),
            ],
            axis=-1,
        )
        grad_router = grad_router + jnp.dot(
            logit_grad.T, normed_low.astype(jnp.float32), precision=HIGHEST
        )
        router_part = jnp.dot(logit_grad, router_wide, precision=HIGHEST)
        normed_grad = lax.psum(normed_part, "tp") + router_part
        grad_gain_one = grad_gain_one + jnp.sum(normed_grad * scaled_one, axis=0)
        grad_shift_one = grad_shift_one + jnp.sum(normed_grad, axis=0)
        input_grads.append(
            resid_grad + norm_backward(normed_grad, scaled_one, inverse_one, gain_one_f)
        )
    reduced = (
        lax.psum_scatter(grad_gain_one, "seq", scatter_dimension=0, tiled=True),
        lax.psum_scatter(grad_shift_one, "seq", scatter_dimension=0, tiled=True),
        lax.psum_scatter(grad_router, "seq", scatter_dimension=1, tiled=True),
        lax.psum_scatter(
            grad_in.reshape(width, 3, local_heads, head_dim), "seq", scatter_dimension=0, tiled=True
        ),
        lax.psum_scatter(grad_in_bias, "seq", scatter_dimension=2, tiled=True),
        lax.psum_scatter(
            grad_out.reshape(local_heads, head_dim, width), "seq", scatter_dimension=2, tiled=True
        ),
        lax.psum_scatter(grad_out_bias, "seq", scatter_dimension=0, tiled=True),
        lax.psum_scatter(grad_gain_two, "seq", scatter_dimension=0, tiled=True),
        lax.psum_scatter(grad_shift_two, "seq", scatter_dimension=0, tiled=True),
        lax.psum_scatter(grad_up, "seq", scatter_dimension=0, tiled=True),
        lax.psum_scatter(
            grad_up_bias.reshape(up_bias_full.shape), "seq", scatter_dimension=1, tiled=True
        ),
        lax.psum_scatter(grad_down, "seq", scatter_dimension=1, tiled=True),
        lax.psum_scatter(grad_down_bias, "seq", scatter_dimension=0, tiled=True),
    )
    return (
        jnp.stack(outputs),
        jnp.stack(input_grads),
        reduced[0],
        reduced[1],
        reduced[2],
        reduced[3],
        reduced[4],
        reduced[5],
        reduced[6],
        reduced[7],
        reduced[8],
        reduced[9],
        reduced[10],
        reduced[11],
        reduced[12],
    )


ROWS = ("zh", "zl", "x", "c")
GROUP = ("zl", "y", "c")
PARTS = ("zh", "x")
LOW = jnp.bfloat16
WIDE = jnp.float32


def swap(value, axis):
    return lax.ppermute(value, axis, [(0, 1), (1, 0)])


def flip_where(bit, value, axis):
    return jnp.where(bit == 1, jnp.flip(value, axis), value)


def to_own_order(value, zh, x):
    lead, width = value.shape[:-1], value.shape[-1]
    value = value.reshape(lead + (2, 2, 2, 2, width // 16))
    value = jnp.swapaxes(value, -4, -3)
    value = flip_where(zh, value, -5)
    value = flip_where(x, value, -4)
    return value.reshape(lead + (width,))


def from_own_order(value, zh, x):
    lead, width = value.shape[:-1], value.shape[-1]
    value = value.reshape(lead + (2, 2, 2, 2, width // 16))
    value = flip_where(zh, value, -5)
    value = flip_where(x, value, -4)
    value = jnp.swapaxes(value, -4, -3)
    return value.reshape(lead + (width,))


def gather_parts(piece, axis):
    over_x = swap(piece, "x")
    over_z = swap(piece, "zh")
    over_both = swap(over_z, "x")
    return jnp.concatenate([piece, over_x, over_z, over_both], axis=axis)


def scatter_parts(pieces):
    stay, send = pieces[0], pieces[1]
    got = [swap(p.astype(LOW), "x") for p in send]
    first = stay[1] + got[1].astype(WIDE)
    over_z = swap(first.astype(LOW), "zh")
    return stay[0] + got[0].astype(WIDE) + over_z.astype(WIDE)


def dot_to(left, right, dims):
    return lax.dot_general(left, right, (dims, ((), ())), preferred_element_type=WIDE)


def grouped(
    tokens,
    cotangent,
    head_groups,
    ffn_widths,
    doc_lengths,
    first_gain,
    first_shift,
    router_weight,
    in_weight,
    in_bias,
    out_weight,
    out_bias,
    second_gain,
    second_shift,
    up_weight,
    up_bias,
    down_weight,
    down_bias,
):
    zh, zl, x, c, y = (lax.axis_index(a) for a in ("zh", "zl", "x", "c", "y"))
    micro, tok_dev, width = tokens.shape
    half = tok_dev // 2
    own = 4 * half
    length = 16 * tok_dev
    block = width // 16
    tp_heads, head_dim = in_weight.shape[2:]
    heads = tp_heads // 4
    inner = heads * head_dim
    tp_units = up_weight.shape[1]
    units = tp_units // 4
    batch = zh * 2 + x
    part = zl * 2 + c
    place = (zl * 2 + y) * 2 + c
    scale = HEAD_DIM ** (-0.5)

    small = jnp.concatenate(
        [
            first_gain,
            first_shift,
            second_gain,
            second_shift,
            out_bias,
            down_bias,
            router_weight.reshape(-1),
            in_bias.reshape(-1),
            up_bias.reshape(-1),
            head_groups.astype(LOW).reshape(-1),
            ffn_widths.astype(LOW).reshape(-1),
        ]
    )
    small_all = lax.all_gather(small, ROWS, axis=0)
    n_vec = 6 + 2 * GROUPS
    vectors = small_all[:, : n_vec * block].reshape(16, n_vec, block)
    vectors = jnp.swapaxes(vectors, 0, 1).reshape(n_vec, width)
    vectors = to_own_order(vectors, zh, x)
    vectors_f = vectors.astype(WIDE)
    gain_one, shift_one, gain_two, shift_two, bias_out, bias_down = (
        vectors_f[i : i + 1] for i in range(6)
    )
    router = vectors[6:]
    at = n_vec * block
    size = in_bias.size
    bias_in = small_all[:, at : at + size].reshape((16,) + in_bias.shape)
    bias_in = jnp.moveaxis(bias_in, 0, 2).reshape(3, 4, heads, head_dim)
    bias_in = lax.dynamic_index_in_dim(bias_in, part, 1, keepdims=False).astype(WIDE)
    at += size
    size = up_bias.size
    bias_up = small_all[:, at : at + size].reshape((16,) + up_bias.shape)
    bias_up = jnp.moveaxis(bias_up, 0, 1).reshape(4, units)
    bias_up = lax.dynamic_index_in_dim(bias_up, part, 0, keepdims=True).astype(WIDE)
    at += size
    widths = small_all[:, at:].reshape(16, 2, micro, tok_dev)
    widths = lax.dynamic_index_in_dim(widths, batch, 2, keepdims=False).astype(jnp.int32)
    widths = widths.reshape(2, 2, 2, 2, 2, 2, half)
    widths = jnp.transpose(widths, (4, 1, 5, 3, 0, 2, 6)).reshape(2, length)
    heads_row, units_row = widths[0], widths[1]

    index = jnp.arange(length, dtype=jnp.int32).reshape(2, 2, 2, 2, 2, half)
    positions = jnp.transpose(index, (1, 4, 3, 0, 2, 5)).reshape(length)
    doc = doc_index(lax.dynamic_index_in_dim(doc_lengths, batch, 0, keepdims=False), positions)
    cosine, sine = rotary_tables(positions)
    allowed = (positions[None, :] <= positions[:, None]) & (doc[None, :] == doc[:, None])

    def to_batch(value):
        mine = lax.dynamic_slice_in_dim(value, y * half, half, 1)
        got = lax.all_to_all(mine, PARTS, 0, 0, tiled=True)
        return to_own_order(got.reshape(own, width), zh, x)

    tokens_own = to_batch(tokens)
    tokens_all = lax.all_gather(tokens_own, GROUP, axis=0, tiled=True)
    cotangent_own = to_batch(cotangent)
    cotangent_all = lax.all_gather(cotangent_own, GROUP, axis=0, tiled=True)

    def exchange(value):
        return lax.all_to_all(value, ("zl", "c"), 0, 0, tiled=True)

    w_in = in_weight.reshape(block, 3, 4, heads, head_dim)
    w_in = exchange(jnp.moveaxis(w_in, 2, 0)).reshape(4 * block, 3 * inner)
    w_in = gather_parts(w_in, 0)
    w_out = exchange(out_weight.reshape(4, inner, block))
    w_out = gather_parts(jnp.moveaxis(w_out, 0, 1).reshape(inner, 4 * block), 1)
    w_up = exchange(jnp.moveaxis(up_weight.reshape(block, 4, units), 1, 0))
    w_up = gather_parts(w_up.reshape(4 * block, units), 0)
    w_down = exchange(down_weight.reshape(4, units, block))
    w_down = gather_parts(jnp.moveaxis(w_down, 0, 1).reshape(units, 4 * block), 1)

    normed, _, _ = norm_forward(tokens_all.astype(WIDE), gain_one, shift_one)
    normed_low = normed.astype(LOW)
    logits = dot_to(normed_low, router, ((1,), (1,)))
    options = jnp.arange(GROUPS, dtype=jnp.int32)
    attn_prob = jax.nn.softmax(logits[:, :GROUPS], axis=-1)
    ffn_prob = jax.nn.softmax(logits[:, GROUPS:], axis=-1)
    attn_pick = (options[None, :] == heads_row[:, None] - 1).astype(WIDE)
    ffn_pick = (options[None, :] == units_row[:, None] - 1).astype(WIDE)
    attn_gate = GROUPS * jnp.sum(attn_prob * attn_pick, axis=-1, keepdims=True)
    ffn_gate = GROUPS * jnp.sum(ffn_prob * ffn_pick, axis=-1, keepdims=True)

    def mine(value):
        return lax.dynamic_slice_in_dim(value, place * own, own, 0)

    rows = tokens_own.astype(WIDE)
    _, scaled_one, inverse_one = norm_forward(rows, gain_one, shift_one)

    projected = dot_to(normed_low, w_in, ((1,), (0,)))
    projected = projected.reshape(length, 3, heads, head_dim) + bias_in
    queries = rotate(projected[:, 0], cosine, sine).astype(LOW)
    keys = rotate(projected[:, 1], cosine, sine).astype(LOW)
    values = projected[:, 2].astype(LOW)
    head_ids = (y * 4 + part) * heads + jnp.arange(heads, dtype=jnp.int32)
    head_active = (head_ids[None, :] // (HEADS // GROUPS) < heads_row[:, None]).astype(WIDE)
    unit_ids = (y * 4 + part) * units + jnp.arange(units, dtype=jnp.int32)
    unit_active = unit_ids[None, :] // (FF // GROUPS) < units_row[:, None]
    raw = jnp.einsum("qhd,khd->hqk", queries, keys, preferred_element_type=WIDE)
    scores = jnp.where(allowed[None], raw * scale, -jnp.inf)
    row_max = jnp.max(scores, axis=-1, keepdims=True)
    weights = jnp.exp(scores - row_max)
    row_total = jnp.sum(weights, axis=-1, keepdims=True)
    probs = weights / row_total
    probs_low = probs.astype(LOW)
    attended = jnp.einsum("hqk,khd->qhd", probs_low, values, preferred_element_type=WIDE)
    mixed = (attended * head_active[:, :, None]).astype(LOW).reshape(length, inner)
    attn_part = dot_to(mixed, w_out, ((1,), (0,)))

    def group_sum(value):
        return lax.psum_scatter(
            value.astype(LOW), GROUP, scatter_dimension=0, tiled=True
        ).astype(WIDE)

    attn_branch = group_sum(attn_part) + bias_out
    attn_gate_own = mine(attn_gate)
    ffn_gate_own = mine(ffn_gate)
    resid = rows + attn_gate_own * attn_branch
    normed_two, scaled_two, inverse_two = norm_forward(resid, gain_two, shift_two)
    normed_two_low = lax.all_gather(normed_two.astype(LOW), GROUP, axis=0, tiled=True)

    up_pre = dot_to(normed_two_low, w_up, ((1,), (0,))) + bias_up
    relu_part = jnp.where(unit_active, jnp.maximum(up_pre, 0.0), 0.0)
    hidden = jnp.square(relu_part).astype(LOW)
    down_grad = (ffn_gate * cotangent_all.astype(WIDE)).astype(LOW)
    hidden_grad = dot_to(down_grad, w_down, ((1,), (1,)))
    up_grad = (hidden_grad * 2.0 * relu_part).astype(LOW)
    normed_two_grad = group_sum(dot_to(up_grad, w_up, ((1,), (1,))))
    ffn_branch = group_sum(dot_to(hidden, w_down, ((1,), (0,)))) + bias_down
    grad_up = dot_to(normed_two_low, up_grad, ((0,), (0,)))
    grad_down = dot_to(hidden, down_grad, ((0,), (0,)))
    grad_up_bias = jnp.sum(up_grad.astype(WIDE), axis=0)

    upstream = cotangent_own.astype(WIDE)
    block_out = (resid + ffn_gate_own * ffn_branch).astype(LOW)
    ffn_gate_grad = jnp.sum(upstream * ffn_branch, axis=-1)
    grad_down_bias = jnp.sum(ffn_gate_own * upstream, axis=0)
    grad_gain_two = jnp.sum(normed_two_grad * scaled_two, axis=0)
    grad_shift_two = jnp.sum(normed_two_grad, axis=0)
    resid_grad = upstream + norm_backward(normed_two_grad, scaled_two, inverse_two, gain_two)
    attn_gate_grad = jnp.sum(resid_grad * attn_branch, axis=-1)
    gated_attn = attn_gate_own * resid_grad
    grad_out_bias = jnp.sum(gated_attn, axis=0)
    attn_out_grad = lax.all_gather(gated_attn.astype(LOW), GROUP, axis=0, tiled=True)

    mixed_grad = dot_to(attn_out_grad, w_out, ((1,), (1,)))
    attended_grad = (
        mixed_grad.reshape(length, heads, head_dim) * head_active[:, :, None]
    ).astype(LOW)
    grad_out = dot_to(mixed, attn_out_grad, ((0,), (0,)))
    prob_grad = jnp.einsum("qhd,khd->hqk", attended_grad, values, preferred_element_type=WIDE)
    row_dot = jnp.sum(probs * prob_grad, axis=-1, keepdims=True)
    score_grad = (probs * (prob_grad - row_dot) * scale).astype(LOW)
    query_grad = jnp.einsum("hqk,khd->qhd", score_grad, keys, preferred_element_type=WIDE)
    key_grad = jnp.einsum("hqk,qhd->khd", score_grad, queries, preferred_element_type=WIDE)
    value_grad = jnp.einsum("hqk,qhd->khd", probs_low, attended_grad, preferred_element_type=WIDE)
    query_grad = rotate_back(query_grad, cosine, sine)
    key_grad = rotate_back(key_grad, cosine, sine)
    proj_grad = jnp.stack([query_grad, key_grad, value_grad], axis=1).astype(LOW)
    grad_in_bias = jnp.sum(proj_grad.astype(WIDE), axis=0)
    proj_flat = proj_grad.reshape(length, 3 * inner)
    normed_part = group_sum(dot_to(proj_flat, w_in, ((1,), (1,))))
    grad_in = dot_to(normed_low, proj_flat, ((0,), (0,)))

    logit_grad = jnp.concatenate(
        [
            gate_logit_grad(mine(attn_prob), mine(attn_pick), attn_gate_grad),
            gate_logit_grad(mine(ffn_prob), mine(ffn_pick), ffn_gate_grad),
        ],
        axis=-1,
    )
    normed_own = mine(normed_low)
    grad_router = jnp.dot(logit_grad.T, normed_own.astype(WIDE), precision=HIGHEST)
    router_part = jnp.dot(logit_grad, vectors_f[6:], precision=HIGHEST)
    normed_grad = normed_part + router_part
    grad_gain_one = jnp.sum(normed_grad * scaled_one, axis=0)
    grad_shift_one = jnp.sum(normed_grad, axis=0)
    tokens_grad = resid_grad + norm_backward(normed_grad, scaled_one, inverse_one, gain_one)

    def from_batch(value):
        value = from_own_order(value, zh, x).astype(LOW).reshape(4, half, width)
        value = lax.all_to_all(value, PARTS, 0, 0, tiled=True)
        other = swap(value, "y")
        return jnp.where(
            y == 0,
            jnp.concatenate([value, other], axis=1),
            jnp.concatenate([other, value], axis=1),
        )

    def share_rows(grad):
        total = scatter_parts(jnp.swapaxes(grad.reshape(2, 2, 4 * block, -1), 0, 1))
        total = exchange(total.astype(LOW).reshape(4, block, -1))
        return total

    def share_columns(grad):
        grad = grad.reshape(grad.shape[0], 2, 2, 4 * block)
        total = scatter_parts(jnp.transpose(grad, (2, 1, 0, 3)))
        total = total.astype(LOW).reshape(-1, 4, block)
        return exchange(jnp.swapaxes(total, 0, 1))

    grad_up = jnp.swapaxes(share_rows(grad_up), 0, 1).reshape(block, tp_units)
    grad_down = share_columns(grad_down).reshape(tp_units, block)
    grad_out = share_columns(grad_out).reshape(tp_heads, head_dim, block)
    grad_in = share_rows(grad_in).reshape(4, block, 3, heads, head_dim)
    grad_in = jnp.transpose(grad_in, (1, 2, 0, 3, 4)).reshape(block, 3, tp_heads, head_dim)

    sums = jnp.stack(
        [grad_gain_one, grad_shift_one, grad_out_bias, grad_gain_two, grad_shift_two, grad_down_bias]
    )
    sums = from_own_order(jnp.concatenate([sums, grad_router], axis=0), zh, x)
    sums = jnp.swapaxes(sums.reshape(n_vec, 16, block), 0, 1).reshape(16, n_vec * block)
    chosen = (jnp.arange(4) == part).astype(WIDE)
    spread_in = (grad_in_bias[:, None] * chosen[None, :, None, None]).reshape(
        3, tp_heads, 16, head_dim // 16
    )
    spread_in = jnp.moveaxis(spread_in, 2, 0).reshape(16, -1)
    spread_up = (grad_up_bias[None, :] * chosen[:, None]).reshape(up_bias.shape[0], 16, block)
    spread_up = jnp.moveaxis(spread_up, 1, 0).reshape(16, -1)
    total = lax.psum_scatter(
        jnp.concatenate([sums, spread_in, spread_up], axis=1),
        ROWS,
        scatter_dimension=0,
        tiled=True,
    )[0]
    shared = lax.psum(total[: n_vec * block], "y").reshape(n_vec, block)
    at = n_vec * block
    return (
        from_batch(block_out),
        from_batch(tokens_grad).astype(WIDE),
        shared[0],
        shared[1],
        shared[6:],
        grad_in.astype(WIDE),
        total[at : at + in_bias.size].reshape(in_bias.shape),
        grad_out.astype(WIDE),
        shared[2],
        shared[3],
        shared[4],
        grad_up.astype(WIDE),
        total[at + in_bias.size :].reshape(up_bias.shape),
        grad_down.astype(WIDE),
        shared[5],
    )


def solution(mesh):
    body, seq, tp = local, "seq", "tp"
    if mesh.shape["seq"] == 16 and mesh.shape["tp"] == 2:
        mesh = Mesh(mesh.devices.reshape(2, 2, 2, 2, 2), ROWS + ("y",))
        body, seq, tp = grouped, ROWS, "y"
    return jax.shard_map(
        body,
        mesh=mesh,
        in_specs=(
            P(None, seq, None),
            P(None, seq, None),
            P(None, seq),
            P(None, seq),
            P(),
            P(seq),
            P(seq),
            P(None, seq),
            P(seq, None, tp, None),
            P(None, tp, seq),
            P(tp, None, seq),
            P(seq),
            P(seq),
            P(seq),
            P(seq, tp),
            P(tp, seq),
            P(tp, seq),
            P(seq),
        ),
        out_specs=(
            P(None, seq, None),
            P(None, seq, None),
            P(seq),
            P(seq),
            P(None, seq),
            P(seq, None, tp, None),
            P(None, tp, seq),
            P(tp, None, seq),
            P(seq),
            P(seq),
            P(seq),
            P(seq, tp),
            P(tp, seq),
            P(tp, seq),
            P(seq),
        ),
        check_vma=False,
    )
```

```python
import functools
import math

import jax
import jax.numpy as jnp
from jax import lax
from jax.experimental import pallas as pl
from jax.experimental.pallas import tpu as pltpu
from jax.sharding import Mesh
from jax.sharding import PartitionSpec as P

HEADS = 16
HEAD_DIM = 128
FF = 8192
GROUPS = 4


EPSILON = 1e-05
HIGHEST = lax.Precision.HIGHEST


def norm_forward(rows, gain, shift):
    center = rows - jnp.mean(rows, axis=-1, keepdims=True)
    inverse = lax.rsqrt(jnp.mean(center * center, axis=-1, keepdims=True) + EPSILON)
    scaled = center * inverse
    return (scaled * gain + shift, scaled, inverse)


def norm_backward(upstream, scaled, inverse, gain):
    through = upstream * gain
    return inverse * (
        through
        - jnp.mean(through, axis=-1, keepdims=True)
        - scaled * jnp.mean(through * scaled, axis=-1, keepdims=True)
    )


def rotary_tables(positions):
    half_dim = HEAD_DIM // 2
    steps_up = jnp.arange(half_dim, dtype=jnp.float32) * (2.0 / HEAD_DIM)
    inverse = jnp.exp(-math.log(10000.0) * steps_up)
    angles = positions.astype(jnp.float32)[:, None] * inverse[None, :]
    angles = jnp.concatenate([angles, angles], axis=1)
    return (jnp.cos(angles), jnp.sin(angles))


def rotate(vectors, cosine, sine):
    half_dim = vectors.shape[-1] // 2
    turned = jnp.concatenate([-vectors[..., half_dim:], vectors[..., :half_dim]], axis=-1)
    return vectors * cosine[:, None, :] + turned * sine[:, None, :]


def rotate_back(grads, cosine, sine):
    half_dim = grads.shape[-1] // 2
    moved = grads * sine[:, None, :]
    turned = jnp.concatenate([moved[..., half_dim:], -moved[..., :half_dim]], axis=-1)
    return grads * cosine[:, None, :] + turned


def doc_index(lengths, positions):
    ends = jnp.cumsum(lengths)
    return jnp.sum((positions[:, None] >= ends[None, :]).astype(jnp.int32), axis=1)


def gate_logit_grad(prob, pick, gate_grad):
    chosen = jnp.sum(prob * pick, axis=-1, keepdims=True)
    return GROUPS * chosen * (pick - prob) * gate_grad[:, None]


def local(
    tokens,
    cotangent,
    head_groups,
    ffn_widths,
    doc_lengths,
    first_gain,
    first_shift,
    router_weight,
    in_weight,
    in_bias,
    out_weight,
    out_bias,
    second_gain,
    second_shift,
    up_weight,
    up_bias,
    down_weight,
    down_bias,
):
    seq_count = lax.axis_size("seq")
    seq_index = lax.axis_index("seq")
    tp_index = lax.axis_index("tp")
    gathered = (
        lax.all_gather(first_gain, "seq", axis=0, tiled=True),
        lax.all_gather(first_shift, "seq", axis=0, tiled=True),
        lax.all_gather(router_weight, "seq", axis=1, tiled=True),
        lax.all_gather(in_weight, "seq", axis=0, tiled=True),
        lax.all_gather(in_bias, "seq", axis=2, tiled=True),
        lax.all_gather(out_weight, "seq", axis=2, tiled=True),
        lax.all_gather(out_bias, "seq", axis=0, tiled=True),
        lax.all_gather(second_gain, "seq", axis=0, tiled=True),
        lax.all_gather(second_shift, "seq", axis=0, tiled=True),
        lax.all_gather(up_weight, "seq", axis=0, tiled=True),
        lax.all_gather(up_bias, "seq", axis=1, tiled=True),
        lax.all_gather(down_weight, "seq", axis=1, tiled=True),
        lax.all_gather(down_bias, "seq", axis=0, tiled=True),
    )
    (
        gain_one,
        shift_one,
        router_full,
        in_full,
        in_bias_full,
        out_full,
        out_bias_full,
        gain_two,
        shift_two,
        up_full,
        up_bias_full,
        down_full,
        down_bias_full,
    ) = gathered
    micro, tok_dev, width = tokens.shape
    local_heads = in_full.shape[2]
    head_dim = in_full.shape[3]
    inner = local_heads * head_dim
    local_units = up_full.shape[1]
    length = tok_dev * seq_count
    scale = HEAD_DIM ** (-0.5)
    gain_one_f = gain_one.astype(jnp.float32)
    shift_one_f = shift_one.astype(jnp.float32)
    gain_two_f = gain_two.astype(jnp.float32)
    shift_two_f = shift_two.astype(jnp.float32)
    out_bias_f = out_bias_full.astype(jnp.float32)
    down_bias_f = down_bias_full.astype(jnp.float32)
    router_wide = router_full.astype(jnp.float32)
    bias_in = in_bias_full.astype(jnp.float32)
    up_bias_vec = up_bias_full.reshape(local_units).astype(jnp.float32)
    in_matrix = in_full.reshape(width, 3 * inner)
    out_matrix = out_full.reshape(inner, width)
    positions_all = jnp.arange(length, dtype=jnp.int32)
    positions_local = seq_index * tok_dev + jnp.arange(tok_dev, dtype=jnp.int32)
    cosine, sine = rotary_tables(positions_local)
    head_ids = tp_index * local_heads + jnp.arange(local_heads, dtype=jnp.int32)
    unit_ids = tp_index * local_units + jnp.arange(local_units, dtype=jnp.int32)
    options = jnp.arange(GROUPS, dtype=jnp.int32)
    grad_gain_one = jnp.zeros((width,), jnp.float32)
    grad_shift_one = jnp.zeros((width,), jnp.float32)
    grad_router = jnp.zeros(router_full.shape, jnp.float32)
    grad_in = jnp.zeros((width, 3 * inner), jnp.float32)
    grad_in_bias = jnp.zeros(in_bias_full.shape, jnp.float32)
    grad_out = jnp.zeros((inner, width), jnp.float32)
    grad_out_bias = jnp.zeros((width,), jnp.float32)
    grad_gain_two = jnp.zeros((width,), jnp.float32)
    grad_shift_two = jnp.zeros((width,), jnp.float32)
    grad_up = jnp.zeros(up_full.shape, jnp.float32)
    grad_up_bias = jnp.zeros((local_units,), jnp.float32)
    grad_down = jnp.zeros(down_full.shape, jnp.float32)
    grad_down_bias = jnp.zeros((width,), jnp.float32)
    outputs = []
    input_grads = []
    for batch in range(micro):
        rows = tokens[batch].astype(jnp.float32)
        doc_all = doc_index(doc_lengths[batch], positions_all)
        doc_local = lax.dynamic_slice_in_dim(doc_all, seq_index * tok_dev, tok_dev, 0)
        allowed = (positions_all[None, :] <= positions_local[:, None]) & (
            doc_all[None, :] == doc_local[:, None]
        )
        head_active = (head_ids[None, :] // (HEADS // GROUPS) < head_groups[batch][:, None]).astype(
            jnp.float32
        )
        unit_active = (unit_ids[None, :] // (FF // GROUPS) < ffn_widths[batch][:, None]).astype(
            jnp.float32
        )
        normed, scaled_one, inverse_one = norm_forward(rows, gain_one_f, shift_one_f)
        normed_low = normed.astype(jnp.bfloat16)
        logits = jnp.dot(normed_low, router_full.T, preferred_element_type=jnp.float32)
        attn_prob = jax.nn.softmax(logits[:, :GROUPS], axis=-1)
        ffn_prob = jax.nn.softmax(logits[:, GROUPS:], axis=-1)
        attn_pick = (options[None, :] == head_groups[batch][:, None] - 1).astype(jnp.float32)
        ffn_pick = (options[None, :] == ffn_widths[batch][:, None] - 1).astype(jnp.float32)
        attn_gate = GROUPS * jnp.sum(attn_prob * attn_pick, axis=-1)
        ffn_gate = GROUPS * jnp.sum(ffn_prob * ffn_pick, axis=-1)
        projected = jnp.dot(normed_low, in_matrix, preferred_element_type=jnp.float32)
        projected = projected.reshape(tok_dev, 3, local_heads, head_dim) + bias_in
        queries = rotate(projected[:, 0], cosine, sine).astype(jnp.bfloat16)
        keys_low = rotate(projected[:, 1], cosine, sine).astype(jnp.bfloat16)
        values_low = projected[:, 2].astype(jnp.bfloat16)
        keys_all, values_all = (
            lax.all_gather(keys_low, "seq", axis=0, tiled=True),
            lax.all_gather(values_low, "seq", axis=0, tiled=True),
        )
        raw_scores = jnp.einsum(
            "qhd,khd->hqk", queries, keys_all, preferred_element_type=jnp.float32
        )
        scores = jnp.where(allowed[None], raw_scores * scale, -jnp.inf)
        row_max = jnp.max(scores, axis=-1, keepdims=True)
        weights = jnp.exp(scores - row_max)
        row_total = jnp.sum(weights, axis=-1, keepdims=True)
        log_total = row_max + jnp.log(row_total)
        probs = weights / row_total
        attended = jnp.einsum(
            "hqk,khd->qhd",
            probs.astype(jnp.bfloat16),
            values_all,
            preferred_element_type=jnp.float32,
        )
        mixed_heads = (attended * head_active[:, :, None]).astype(jnp.bfloat16)
        mixed_flat = mixed_heads.reshape(tok_dev, inner)
        attn_part = jnp.dot(mixed_flat, out_matrix, preferred_element_type=jnp.float32)
        attn_sum = lax.psum(attn_part, "tp")
        attn_branch = attn_sum + out_bias_f
        resid = rows + attn_gate[:, None] * attn_branch
        normed_two, scaled_two, inverse_two = norm_forward(resid, gain_two_f, shift_two_f)
        normed_two_low = normed_two.astype(jnp.bfloat16)
        up_pre = jnp.dot(normed_two_low, up_full, preferred_element_type=jnp.float32) + up_bias_vec
        relu_part = jnp.maximum(up_pre, 0.0)
        hidden = (unit_active * jnp.square(relu_part)).astype(jnp.bfloat16)
        down_part = jnp.dot(hidden, down_full, preferred_element_type=jnp.float32)
        down_sum = lax.psum(down_part.astype(jnp.bfloat16), "tp").astype(jnp.float32)
        ffn_branch = down_sum + down_bias_f
        outputs.append((resid + ffn_gate[:, None] * ffn_branch).astype(jnp.bfloat16))
        upstream = cotangent[batch].astype(jnp.float32)
        ffn_gate_grad = jnp.sum(upstream * ffn_branch, axis=-1)
        gated_up = ffn_gate[:, None] * upstream
        grad_down_bias = grad_down_bias + jnp.sum(gated_up, axis=0)
        down_grad = gated_up.astype(jnp.bfloat16)
        grad_down = grad_down + jnp.einsum(
            "tf,td->fd", hidden, down_grad, preferred_element_type=jnp.float32
        )
        hidden_grad = jnp.einsum(
            "td,fd->tf", down_grad, down_full, preferred_element_type=jnp.float32
        )
        up_grad = (hidden_grad * unit_active * 2.0 * relu_part).astype(jnp.bfloat16)
        grad_up_bias = grad_up_bias + jnp.sum(up_grad.astype(jnp.float32), axis=0)
        grad_up = grad_up + jnp.einsum(
            "td,tf->df", normed_two_low, up_grad, preferred_element_type=jnp.float32
        )
        normed_two_part = jnp.einsum(
            "tf,df->td", up_grad, up_full, preferred_element_type=jnp.float32
        )
        normed_two_grad = lax.psum(normed_two_part, "tp")
        grad_gain_two = grad_gain_two + jnp.sum(normed_two_grad * scaled_two, axis=0)
        grad_shift_two = grad_shift_two + jnp.sum(normed_two_grad, axis=0)
        resid_grad = upstream + norm_backward(normed_two_grad, scaled_two, inverse_two, gain_two_f)
        attn_gate_grad = jnp.sum(resid_grad * attn_branch, axis=-1)
        gated_attn = attn_gate[:, None] * resid_grad
        grad_out_bias = grad_out_bias + jnp.sum(gated_attn, axis=0)
        attn_out_grad = gated_attn.astype(jnp.bfloat16)
        grad_out = grad_out + jnp.einsum(
            "ti,td->id", mixed_flat, attn_out_grad, preferred_element_type=jnp.float32
        )
        mixed_grad = jnp.einsum(
            "td,id->ti", attn_out_grad, out_matrix, preferred_element_type=jnp.float32
        )
        attended_grad = (
            mixed_grad.reshape(tok_dev, local_heads, head_dim) * head_active[:, :, None]
        ).astype(jnp.bfloat16)
        again_raw = jnp.einsum(
            "qhd,khd->hqk", queries, keys_all, preferred_element_type=jnp.float32
        )
        again_scores = jnp.where(allowed[None], again_raw * scale, -jnp.inf)
        probs_again = jnp.exp(again_scores - log_total)
        prob_grad = jnp.einsum(
            "qhd,khd->hqk", attended_grad, values_all, preferred_element_type=jnp.float32
        )
        row_dot = jnp.sum(probs_again * prob_grad, axis=-1, keepdims=True)
        score_grad = (probs_again * (prob_grad - row_dot) * scale).astype(jnp.bfloat16)
        query_rot_grad = jnp.einsum(
            "hqk,khd->qhd", score_grad, keys_all, preferred_element_type=jnp.float32
        )
        probs_low = probs_again.astype(jnp.bfloat16)
        key_part = jnp.einsum(
            "hqk,qhd->khd", score_grad, queries, preferred_element_type=jnp.float32
        )
        value_part = jnp.einsum(
            "hqk,qhd->khd", probs_low, attended_grad, preferred_element_type=jnp.float32
        )
        combined = lax.psum_scatter(
            jnp.concatenate([key_part, value_part], axis=1).reshape(
                lax.axis_size("seq") * tok_dev, 2 * inner
            ),
            "seq",
            scatter_dimension=0,
            tiled=True,
        )
        combined = combined.reshape(tok_dev, 2 * local_heads, head_dim)
        key_rot_grad = combined[:, :local_heads]
        value_grad = combined[:, local_heads:]
        query_grad = rotate_back(query_rot_grad, cosine, sine)
        key_grad = rotate_back(key_rot_grad, cosine, sine)
        proj_grad = jnp.stack([query_grad, key_grad, value_grad], axis=1).astype(jnp.bfloat16)
        grad_in_bias = grad_in_bias + jnp.sum(proj_grad.astype(jnp.float32), axis=0)
        proj_flat = proj_grad.reshape(tok_dev, 3 * inner)
        grad_in = grad_in + jnp.einsum(
            "tw,tc->wc", normed_low, proj_flat, preferred_element_type=jnp.float32
        )
        normed_part = jnp.einsum(
            "tc,wc->tw", proj_flat, in_matrix, preferred_element_type=jnp.float32
        )
        logit_grad = jnp.concatenate(
            [
                gate_logit_grad(attn_prob, attn_pick, attn_gate_grad),
                gate_logit_grad(ffn_prob, ffn_pick, ffn_gate_grad),
            ],
            axis=-1,
        )
        grad_router = grad_router + jnp.dot(
            logit_grad.T, normed_low.astype(jnp.float32), precision=HIGHEST
        )
        router_part = jnp.dot(logit_grad, router_wide, precision=HIGHEST)
        normed_grad = lax.psum(normed_part, "tp") + router_part
        grad_gain_one = grad_gain_one + jnp.sum(normed_grad * scaled_one, axis=0)
        grad_shift_one = grad_shift_one + jnp.sum(normed_grad, axis=0)
        input_grads.append(
            resid_grad + norm_backward(normed_grad, scaled_one, inverse_one, gain_one_f)
        )
    reduced = (
        lax.psum_scatter(grad_gain_one, "seq", scatter_dimension=0, tiled=True),
        lax.psum_scatter(grad_shift_one, "seq", scatter_dimension=0, tiled=True),
        lax.psum_scatter(grad_router, "seq", scatter_dimension=1, tiled=True),
        lax.psum_scatter(
            grad_in.reshape(width, 3, local_heads, head_dim), "seq", scatter_dimension=0, tiled=True
        ),
        lax.psum_scatter(grad_in_bias, "seq", scatter_dimension=2, tiled=True),
        lax.psum_scatter(
            grad_out.reshape(local_heads, head_dim, width), "seq", scatter_dimension=2, tiled=True
        ),
        lax.psum_scatter(grad_out_bias, "seq", scatter_dimension=0, tiled=True),
        lax.psum_scatter(grad_gain_two, "seq", scatter_dimension=0, tiled=True),
        lax.psum_scatter(grad_shift_two, "seq", scatter_dimension=0, tiled=True),
        lax.psum_scatter(grad_up, "seq", scatter_dimension=0, tiled=True),
        lax.psum_scatter(
            grad_up_bias.reshape(up_bias_full.shape), "seq", scatter_dimension=1, tiled=True
        ),
        lax.psum_scatter(grad_down, "seq", scatter_dimension=1, tiled=True),
        lax.psum_scatter(grad_down_bias, "seq", scatter_dimension=0, tiled=True),
    )
    return (
        jnp.stack(outputs),
        jnp.stack(input_grads),
        reduced[0],
        reduced[1],
        reduced[2],
        reduced[3],
        reduced[4],
        reduced[5],
        reduced[6],
        reduced[7],
        reduced[8],
        reduced[9],
        reduced[10],
        reduced[11],
        reduced[12],
    )


ROWS = ("zh", "zl", "x", "c")
GROUP = ("c", "zl", "y")
PARTS = ("zh", "x")
LOW = jnp.bfloat16
WIDE = jnp.float32


def swap(value, axis):
    return lax.ppermute(value, axis, [(0, 1), (1, 0)])


def flip_where(bit, value, axis):
    return jnp.where(bit == 1, jnp.flip(value, axis), value)


def to_own_order(value, zh, x):
    lead, width = value.shape[:-1], value.shape[-1]
    value = value.reshape(lead + (2, 2, 2, 2, width // 16))
    value = jnp.swapaxes(value, -4, -3)
    value = flip_where(zh, value, -5)
    value = flip_where(x, value, -4)
    return value.reshape(lead + (width,))


def from_own_order(value, zh, x):
    lead, width = value.shape[:-1], value.shape[-1]
    value = value.reshape(lead + (2, 2, 2, 2, width // 16))
    value = flip_where(zh, value, -5)
    value = flip_where(x, value, -4)
    value = jnp.swapaxes(value, -4, -3)
    return value.reshape(lead + (width,))


def tie(*values):
    return lax.optimization_barrier(values)


def dot_to(left, right, dims):
    return lax.dot_general(left, right, (dims, ((), ())), preferred_element_type=WIDE)


def gather_over(value, axes, bits):
    for axis, bit in zip(axes, bits):
        other = swap(value, axis)
        value = jnp.where(
            bit == 0,
            jnp.concatenate([value, other], axis=0),
            jnp.concatenate([other, value], axis=0),
        )
    return value


def reduce_rows(value, zh, zl, x, c):
    value = value.reshape(2, 2, 2, 2, -1)
    for axis, at, bit in (("zh", 0, zh), ("zl", 0, zl), ("x", 0, x), ("c", 0, c)):
        keep = lax.dynamic_index_in_dim(value, bit, at, keepdims=False)
        send = lax.dynamic_index_in_dim(value, 1 - bit, at, keepdims=False)
        value = keep + swap(send, axis)
    return value


BLOCK_Q = 256
NEVER = -1e30


def chunks(bits_ref, width):
    run = width // 8
    for at in range(8):
        zh, x, zl = at // 4, at // 2 % 2, at % 2
        theirs = ((zh ^ bits_ref[0]) * 2 + zl) * 2 + (x ^ bits_ref[1])
        yield at * run, pl.multiple_of(theirs * run, run)


def norm_kernel(bits_ref, x_ref, gain_ref, shift_ref, router_ref, out_ref, logits_ref):
    width = x_ref.shape[1]
    rows = x_ref[...].astype(WIDE)
    mean = jnp.mean(rows, axis=-1, keepdims=True)
    center = rows - mean
    inverse = lax.rsqrt(jnp.mean(center * center, axis=-1, keepdims=True) + EPSILON)
    logits = None
    for mine, theirs in chunks(bits_ref, width):
        at = slice(mine, mine + width // 8)
        part = (x_ref[:, pl.ds(theirs, width // 8)].astype(WIDE) - mean) * inverse
        low = (part * gain_ref[:, at] + shift_ref[:, at]).astype(LOW)
        out_ref[:, at] = low
        got = dot_to(low, router_ref[:, at], ((1,), (1,)))
        logits = got if logits is None else logits + got
    logits_ref[...] = logits


def norm_rows(bits, rows, gain, shift, router):
    length, width = rows.shape
    n = router.shape[0]
    return pl.pallas_call(
        norm_kernel,
        grid_spec=pltpu.PrefetchScalarGridSpec(
            num_scalar_prefetch=1,
            grid=(length // BLOCK_Q,),
            in_specs=[
                pl.BlockSpec((BLOCK_Q, width), lambda i, bits: (i, 0)),
                pl.BlockSpec((1, width), lambda i, bits: (0, 0)),
                pl.BlockSpec((1, width), lambda i, bits: (0, 0)),
                pl.BlockSpec((n, width), lambda i, bits: (0, 0)),
            ],
            out_specs=[
                pl.BlockSpec((BLOCK_Q, width), lambda i, bits: (i, 0)),
                pl.BlockSpec((BLOCK_Q, n), lambda i, bits: (i, 0)),
            ],
        ),
        out_shape=[
            jax.ShapeDtypeStruct((length, width), LOW),
            jax.ShapeDtypeStruct((length, n), WIDE),
        ],
        name="norm_rows",
    )(bits, rows, gain, shift, router)


def gate_kernel(bits_ref, x_ref, gate_ref, out_ref):
    width = x_ref.shape[1]
    gate = gate_ref[...]
    for mine, theirs in chunks(bits_ref, width):
        part = x_ref[:, pl.ds(theirs, width // 8)].astype(WIDE) * gate
        out_ref[:, mine : mine + width // 8] = part.astype(LOW)


def gate_rows(bits, rows, gate):
    length, width = rows.shape
    return pl.pallas_call(
        gate_kernel,
        grid_spec=pltpu.PrefetchScalarGridSpec(
            num_scalar_prefetch=1,
            grid=(length // BLOCK_Q,),
            in_specs=[
                pl.BlockSpec((BLOCK_Q, width), lambda i, bits: (i, 0)),
                pl.BlockSpec((BLOCK_Q, 1), lambda i, bits: (i, 0)),
            ],
            out_specs=pl.BlockSpec((BLOCK_Q, width), lambda i, bits: (i, 0)),
        ),
        out_shape=jax.ShapeDtypeStruct((length, width), LOW),
        name="gate_rows",
    )(bits, rows, gate)


def add_dots(left_ref, pieces, start=None):
    at, total = 0, start
    for piece in pieces:
        n = piece.shape[0]
        part = dot_to(left_ref[:, at : at + n], piece[...], ((1,), (0,)))
        total = part if total is None else total + part
        at += n
    return total


def by_half(step, away_ref, here_ref, write):
    half = pl.num_programs(0) // 2

    @pl.when(step < half)
    def _():
        write(away_ref)

    @pl.when(step >= half)
    def _():
        write(here_ref)


def half_specs(steps, rows, width, dtype):
    half = steps // 2
    shape = jax.ShapeDtypeStruct((rows * half, width), dtype)
    return (
        [
            pl.BlockSpec((rows, width), lambda i, bit: (jnp.minimum(i, half - 1), 0)),
            pl.BlockSpec((rows, width), lambda i, bit: (jnp.maximum(i - half, 0), 0)),
        ],
        [shape, shape],
    )


def row_spec(steps, rows, width):
    half = steps // 2
    return pl.BlockSpec(
        (rows, width), lambda i, bit: (jnp.where(i < half, i + (1 - bit[0]) * half, i - half + bit[0] * half), 0)
    )


def fixed(value):
    return pl.BlockSpec(value.shape, lambda *_: (0, 0))


def grad_kernel(dz_ref, *refs):
    pieces, out_ref = refs[:-1], refs[-1]
    total, at = None, 0
    for piece in pieces:
        n = piece.shape[1]
        part = dot_to(dz_ref[:, at : at + n], piece[...], ((1,), (1,)))
        total = part if total is None else total + part
        at += n
    out_ref[...] = total


def hidden_grad_rows(down_grad, downs):
    length, width = down_grad.shape
    units = downs[0].shape[0]
    return pl.pallas_call(
        grad_kernel,
        grid=(length // BLOCK_Q,),
        in_specs=[pl.BlockSpec((BLOCK_Q, width), lambda i: (i, 0))] + [fixed(p) for p in downs],
        out_specs=pl.BlockSpec((BLOCK_Q, units), lambda i: (i, 0)),
        out_shape=jax.ShapeDtypeStruct((length, units), WIDE),
        name="hidden_grad_rows",
    )(down_grad, *downs)


def wide_kernel(bit_ref, left_ref, *refs):
    pieces, (away_ref, here_ref) = refs[:-2], refs[-2:]

    def write(out_ref):
        at = 0
        for piece in pieces:
            n = piece.shape[1]
            out_ref[:, at : at + n] = dot_to(left_ref[...], piece[...], ((1,), (0,))).astype(LOW)
            at += n

    by_half(pl.program_id(0), away_ref, here_ref, write)


def wide_rows(bit, left, pieces):
    length, depth = left.shape
    rows = BLOCK_Q
    steps = length // rows
    width = sum(p.shape[1] for p in pieces)
    out_specs, out_shape = half_specs(steps, rows, width, LOW)
    return pl.pallas_call(
        wide_kernel,
        grid_spec=pltpu.PrefetchScalarGridSpec(
            num_scalar_prefetch=1,
            grid=(steps,),
            in_specs=[row_spec(steps, rows, depth)] + [fixed(p) for p in pieces],
            out_specs=out_specs,
        ),
        out_shape=out_shape,
        name="wide_rows",
    )(bit, left, *pieces)


def qkv_kernel(h_ref, *refs):
    pieces, (bias_ref, cos_ref, sin_ref, out_ref) = refs[:-4], refs[-4:]
    total = add_dots(h_ref, pieces, bias_ref[...])
    turned = out_ref.shape[1] // HEAD_DIM * 2 // 3
    cosine, sine = cos_ref[...], sin_ref[...]
    for j in range(out_ref.shape[1] // HEAD_DIM):
        at = slice(j * HEAD_DIM, (j + 1) * HEAD_DIM)
        part = total[:, at]
        if j < turned:
            part = part * cosine + pltpu.roll(part, HEAD_DIM // 2, 1) * sine
        out_ref[:, at] = part.astype(LOW)


def qkv_rows(normed, pieces, bias, cosine, sine):
    length, width = normed.shape
    out = bias.shape[1]
    rows = BLOCK_Q
    return pl.pallas_call(
        qkv_kernel,
        grid=(length // rows,),
        in_specs=[pl.BlockSpec((rows, width), lambda i: (i, 0))]
        + [fixed(p) for p in pieces]
        + [
            fixed(bias),
            pl.BlockSpec((rows, HEAD_DIM), lambda i: (i, 0)),
            pl.BlockSpec((rows, HEAD_DIM), lambda i: (i, 0)),
        ],
        out_specs=pl.BlockSpec((rows, out), lambda i: (i, 0)),
        out_shape=jax.ShapeDtypeStruct((length, out), LOW),
        name="qkv_rows",
    )(normed, *pieces, bias, cosine, sine)


def attend_kernel(q_ref, k_ref, v_ref, key_ref, span_ref, active_ref, out_ref, lse_ref):
    scores = dot_to(k_ref[...], q_ref[...], ((1,), (1,))) * (HEAD_DIM**-0.5)
    key = key_ref[...]
    allowed = (key >= span_ref[0:1, :]) & (key <= span_ref[1:2, :])
    scores = jnp.where(allowed, scores, NEVER)
    top = jnp.max(scores, axis=0, keepdims=True)
    weights = jnp.exp(scores - top)
    total = jnp.sum(weights, axis=0, keepdims=True)
    probs = (weights * (1.0 / total)).astype(LOW)
    mixed = dot_to(probs, v_ref[...], ((0,), (0,)))
    out_ref[...] = (mixed * active_ref[0]).astype(LOW)
    lse_ref[0] = top + jnp.log(total)


def turn_back(grad, cosine, sine):
    lane = lax.broadcasted_iota(jnp.int32, grad.shape, 1)
    moved = pltpu.roll(grad * sine, HEAD_DIM // 2, 1)
    return grad * cosine + jnp.where(lane < HEAD_DIM // 2, moved, -moved)


def attend_back_kernel(
    q_ref, k_ref, v_ref, da_ref, w_ref, active_ref, lse_ref,
    key_ref, span_ref, cos_ref, sin_ref, out_ref, dk_sum, dv_sum,
):
    head, step = pl.program_id(0), pl.program_id(1)
    inner = out_ref.shape[1] // 3

    @pl.when(step == 0)
    def _():
        dk_sum[...] = jnp.zeros_like(dk_sum)
        dv_sum[...] = jnp.zeros_like(dv_sum)

    scale = HEAD_DIM**-0.5
    query, key = q_ref[...], k_ref[...]
    grad = dot_to(da_ref[...], w_ref[...], ((1,), (1,)))
    grad = (grad * active_ref[0]).astype(LOW)
    scores = dot_to(key, query, ((1,), (1,))) * scale
    place = key_ref[...]
    allowed = (place >= span_ref[0:1, :]) & (place <= span_ref[1:2, :])
    probs = jnp.exp(jnp.where(allowed, scores, NEVER) - lse_ref[0])
    prob_grad = dot_to(v_ref[...], grad, ((1,), (1,)))
    delta = jnp.sum(probs * prob_grad, axis=0, keepdims=True)
    score_grad = (probs * (prob_grad - delta) * scale).astype(LOW)
    dv_sum[...] += dot_to(probs.astype(LOW), grad, ((1,), (0,)))
    dk_sum[...] += dot_to(score_grad, query, ((1,), (0,)))
    dq = dot_to(score_grad, key, ((0,), (0,)))
    at = pl.ds(pl.multiple_of(step * BLOCK_Q, BLOCK_Q), BLOCK_Q)
    col = pl.multiple_of(head * HEAD_DIM, HEAD_DIM)
    dq = turn_back(dq, cos_ref[at, :], sin_ref[at, :])
    out_ref[at, pl.ds(col, HEAD_DIM)] = dq.astype(LOW)

    @pl.when(step == pl.num_programs(1) - 1)
    def _():
        dk = turn_back(dk_sum[...], cos_ref[...], sin_ref[...])
        out_ref[:, pl.ds(inner + col, HEAD_DIM)] = dk.astype(LOW)
        out_ref[:, pl.ds(2 * inner + col, HEAD_DIM)] = dv_sum[...].astype(LOW)


def attend(qkv, key_place, span, active, heads):
    length = qkv.shape[0]
    d = HEAD_DIM
    n = heads
    return pl.pallas_call(
        attend_kernel,
        grid=(heads, length // BLOCK_Q),
        in_specs=[
            pl.BlockSpec((BLOCK_Q, d), lambda h, i: (i, h)),
            pl.BlockSpec((length, d), lambda h, i: (0, n + h)),
            pl.BlockSpec((length, d), lambda h, i: (0, 2 * n + h)),
            pl.BlockSpec((length, 1), lambda h, i: (0, 0)),
            pl.BlockSpec((2, BLOCK_Q), lambda h, i: (0, i)),
            pl.BlockSpec((1, BLOCK_Q, 1), lambda h, i: (h, i, 0)),
        ],
        out_specs=[
            pl.BlockSpec((BLOCK_Q, d), lambda h, i: (i, h)),
            pl.BlockSpec((1, 1, BLOCK_Q), lambda h, i: (h, 0, i)),
        ],
        out_shape=[
            jax.ShapeDtypeStruct((length, heads * d), LOW),
            jax.ShapeDtypeStruct((heads, 1, length), WIDE),
        ],
        name="attend",
    )(qkv, qkv, qkv, key_place, span, active)


def attend_back(qkv, out_grad, w_out, active, lse, key_place, span, cosine, sine, heads):
    length, width = out_grad.shape
    d = HEAD_DIM
    n = heads
    return pl.pallas_call(
        attend_back_kernel,
        grid=(heads, length // BLOCK_Q),
        in_specs=[
            pl.BlockSpec((BLOCK_Q, d), lambda h, i: (i, h)),
            pl.BlockSpec((length, d), lambda h, i: (0, n + h)),
            pl.BlockSpec((length, d), lambda h, i: (0, 2 * n + h)),
            pl.BlockSpec((BLOCK_Q, width), lambda h, i: (i, 0)),
            pl.BlockSpec((d, width), lambda h, i: (h, 0)),
            pl.BlockSpec((1, BLOCK_Q, 1), lambda h, i: (h, i, 0)),
            pl.BlockSpec((1, 1, BLOCK_Q), lambda h, i: (h, 0, i)),
            pl.BlockSpec((length, 1), lambda h, i: (0, 0)),
            pl.BlockSpec((2, BLOCK_Q), lambda h, i: (0, i)),
            pl.BlockSpec((length, d), lambda h, i: (0, 0)),
            pl.BlockSpec((length, d), lambda h, i: (0, 0)),
        ],
        out_specs=pl.BlockSpec((length, 3 * heads * d), lambda h, i: (0, 0)),
        out_shape=jax.ShapeDtypeStruct((length, 3 * heads * d), LOW),
        scratch_shapes=[pltpu.VMEM((length, d), WIDE), pltpu.VMEM((length, d), WIDE)],
        name="attend_back",
    )(qkv, qkv, qkv, out_grad, w_out, active, lse, key_place, span, cosine, sine)


def grouped(
    tokens,
    cotangent,
    head_groups,
    ffn_widths,
    doc_lengths,
    first_gain,
    first_shift,
    router_weight,
    in_weight,
    in_bias,
    out_weight,
    out_bias,
    second_gain,
    second_shift,
    up_weight,
    up_bias,
    down_weight,
    down_bias,
):
    zh, zl, x, c, y = (lax.axis_index(a) for a in ("zh", "zl", "x", "c", "y"))
    micro, tok_dev, width = tokens.shape
    half = tok_dev // 2
    own = 4 * half
    length = 16 * tok_dev
    block = width // 16
    tp_heads, head_dim = in_weight.shape[2:]
    heads = tp_heads // 4
    inner = heads * head_dim
    tp_units = up_weight.shape[1]
    units = tp_units // 4
    batch = zh * 2 + x
    part = zl * 2 + c
    place = (c * 2 + zl) * 2 + y

    def exchange(value):
        return lax.all_to_all(value, ("zl", "c"), 0, 0, tiled=True)

    def keep_and_send(value, bit, at):
        return (
            lax.dynamic_index_in_dim(value, bit, at, keepdims=False),
            lax.dynamic_index_in_dim(value, 1 - bit, at, keepdims=False),
        )

    def across(pieces):
        return (
            pieces[0],
            swap(pieces[1], "x"),
            swap(pieces[2], "zh"),
            lax.ppermute(pieces[3], PARTS, [(i, i ^ 3) for i in range(4)]),
        )

    def to_batch(value):
        value = lax.dynamic_slice_in_dim(value, y * half, half, 1)
        return across(
            [lax.dynamic_index_in_dim(value, batch ^ k, 0, keepdims=False) for k in range(4)]
        )

    bits = jnp.stack([zh, x]).astype(jnp.int32)
    core = c.reshape(1).astype(jnp.int32)
    small = jnp.concatenate(
        [
            first_gain,
            first_shift,
            second_gain,
            second_shift,
            out_bias,
            down_bias,
            router_weight.reshape(-1),
            in_bias.reshape(-1),
            up_bias.reshape(-1),
            head_groups.astype(LOW).reshape(-1),
            ffn_widths.astype(LOW).reshape(-1),
        ]
    )
    count = small.shape[0]
    small = jnp.pad(small, (0, 24 * 128 - count)).reshape(1, 24, 128)
    token_pieces = to_batch(tokens)
    small = gather_over(small, ("zh", "x"), (zh, x))
    *token_pieces, small, in_weight = tie(*token_pieces, small, in_weight)
    tokens_own = jnp.concatenate(token_pieces, axis=0)
    tokens_all = lax.all_gather(tokens_own, GROUP, axis=0, tiled=True)
    e_in = exchange(jnp.moveaxis(in_weight.reshape(block, 3, 4, heads, head_dim), 2, 0))
    e_in = e_in.reshape(4 * block, 3 * inner)

    index = jnp.arange(length, dtype=jnp.int32).reshape(2, 2, 2, 2, 2, half)

    def by_place(value):
        lead = tuple(range(value.ndim - 6))
        at = value.ndim - 6
        value = jnp.transpose(value, lead + tuple(at + i for i in (3, 1, 4, 0, 2, 5)))
        return value.reshape(value.shape[: value.ndim - 6] + (length,))

    e_in, small, cotangent, out_weight, up_weight = tie(
        e_in, small, cotangent, out_weight, up_weight
    )

    cut = e_in.shape[0] // 2
    in_z1 = swap(e_in[:cut], "zh")
    in_z2 = swap(e_in[cut:], "zh")
    in_x = swap(e_in, "x")
    in_zx1 = swap(in_z1, "x")
    cotangent_own = jnp.concatenate(to_batch(cotangent), axis=0)
    small = gather_over(small, ("c", "zl"), (c, zl)).reshape(2, 2, 2, 2, -1)
    small_all = jnp.transpose(small, (3, 0, 2, 1, 4)).reshape(16, 24 * 128)
    e_out = exchange(out_weight.reshape(4, inner, block))
    e_out = jnp.moveaxis(e_out, 0, 1).reshape(inner, 4 * block)
    positions = by_place(index) ^ (zh * (8 * tok_dev) + x * (2 * tok_dev))
    ends = jnp.cumsum(lax.dynamic_index_in_dim(doc_lengths, batch, 0, keepdims=False))
    first = jnp.max(jnp.where(ends[:, None] <= positions[None, :], ends[:, None], 0), axis=0)
    span = jnp.stack([first, positions])
    key_place = positions[:, None]
    cosine, sine = rotary_tables(positions)
    lane = jnp.arange(HEAD_DIM)[None, :]
    signed = jnp.where(lane < HEAD_DIM // 2, -sine, sine)
    n_vec = 6 + 2 * GROUPS
    rows_of = jnp.arange(16) ^ (zh * 8 + x * 2)
    pick = (rows_of[:, None] == jnp.arange(16)[None, :]).astype(LOW)
    small_own = dot_to(pick, small_all, ((1,), (0,)))
    vectors_f = small_own[:, : n_vec * block].reshape(2, 2, 2, 2, n_vec, block)
    vectors_f = jnp.transpose(vectors_f, (4, 0, 2, 1, 3, 5)).reshape(n_vec, width)
    router = vectors_f[6:].astype(LOW)
    at = n_vec * block
    size = in_bias.size
    bias_in = small_all[:, at : at + size].reshape((16,) + in_bias.shape)
    bias_in = jnp.moveaxis(bias_in, 0, 2).reshape(3, 4, heads, head_dim)
    bias_in = lax.dynamic_index_in_dim(bias_in, part, 1, keepdims=False).astype(WIDE)
    bias_in = bias_in.reshape(1, 3 * inner)
    at += size
    size = up_bias.size
    bias_up = small_all[:, at : at + size].reshape((16,) + up_bias.shape)
    bias_up = jnp.moveaxis(bias_up, 0, 1).reshape(4, units)
    bias_up = lax.dynamic_index_in_dim(bias_up, part, 0, keepdims=True).astype(WIDE)
    at += size
    widths = small_own[:, at:count].reshape(16, 2, micro, tok_dev)
    widths = lax.dynamic_index_in_dim(widths, batch, 2, keepdims=False).astype(jnp.int32)
    widths = jnp.swapaxes(widths, 0, 1).reshape(2, 2, 2, 2, 2, 2, half)
    heads_row, units_row = by_place(widths)
    head_ids = (y * 4 + part) * heads + jnp.arange(heads, dtype=jnp.int32)
    head_active = (head_ids[:, None] // (HEADS // GROUPS) < heads_row[None, :]).astype(WIDE)
    head_active = head_active[:, :, None]
    unit_group = (y * 4 + part) * units // (FF // GROUPS)
    unit_active = (unit_group < units_row).astype(WIDE)[:, None]
    (
        tokens_all, in_x, in_z1, in_z2, in_zx1, e_out, cotangent_own, up_weight, down_weight,
        vectors_f, router, bias_in, bias_up, head_active, unit_active,
        cosine, sine, signed, span, key_place,
    ) = tie(
        tokens_all, in_x, in_z1, in_z2, in_zx1, e_out, cotangent_own, up_weight, down_weight,
        vectors_f, router, bias_in, bias_up, head_active, unit_active,
        cosine, sine, signed, span, key_place,
    )
    gain_one, shift_one, gain_two, shift_two, bias_out, bias_down = (
        vectors_f[i : i + 1] for i in range(6)
    )

    in_zx2 = swap(in_z2, "x")
    out_z = swap(e_out, "zh")
    out_x = swap(e_out, "x")
    e_up = exchange(jnp.moveaxis(up_weight.reshape(block, 4, units), 1, 0))
    e_up = e_up.reshape(4 * block, units)
    cotangent_all = lax.all_gather(cotangent_own, GROUP, axis=0, tiled=True)
    normed_low, logits = norm_rows(bits, tokens_all, gain_one, shift_one, router)
    normed_low, in_zx2, out_z, out_x, e_up, down_weight, logits = tie(
        normed_low, in_zx2, out_z, out_x, e_up, down_weight, logits
    )

    def mine(value):
        return lax.dynamic_slice_in_dim(value, place * own, own, 0)

    up_cut = e_up.shape[0] // 2
    out_zx = swap(out_z, "x")
    up_x1 = swap(e_up[:up_cut], "x")
    up_z1 = swap(e_up[:up_cut], "zh")
    e_down = exchange(down_weight.reshape(4, units, block))
    e_down = jnp.moveaxis(e_down, 0, 1).reshape(units, 4 * block)
    w_in = (e_in, in_x, in_z1, in_z2, in_zx1, in_zx2)
    qkv = qkv_rows(normed_low, w_in, bias_in, cosine, signed)
    mixed, lse = attend(qkv, key_place, span, head_active, heads)
    w_out = jnp.concatenate([e_out, out_x, out_z, out_zx], axis=1)
    mixed, w_out, e_up, e_down, up_x1, up_z1, cotangent_own, tokens_own, logits, w_in = tie(
        mixed, w_out, e_up, e_down, up_x1, up_z1, cotangent_own, tokens_own, logits, w_in
    )

    part_own = own // 2

    def halves(value):
        return (
            lax.dynamic_slice_in_dim(value, c * (length // 2), length // 2, 0),
            lax.dynamic_slice_in_dim(value, (1 - c) * (length // 2), length // 2, 0),
        )

    def group_second(total):
        total = total.reshape(2, 2, own, width)
        a_keep, a_send = keep_and_send(total[:, :, :part_own], zl, 0)
        b_keep, b_send = keep_and_send(total[:, :, part_own:], y, 1)
        a_got = swap(a_send.astype(LOW), "zl")
        b_got = swap(b_send.astype(LOW), "y")
        return a_keep, b_keep, a_got, b_got

    def group_third(a_keep, b_keep, a_got, b_got):
        a_keep, a_send = keep_and_send(a_keep + a_got.astype(WIDE), y, 0)
        b_keep, b_send = keep_and_send(b_keep + b_got.astype(WIDE), zl, 0)
        a_got = swap(a_send.astype(LOW), "y")
        b_got = swap(b_send.astype(LOW), "zl")
        return jnp.concatenate([a_keep + a_got.astype(WIDE), b_keep + b_got.astype(WIDE)], axis=0)

    attn_here, attn_away = halves(mixed)
    attn_away = dot_to(attn_away, w_out, ((1,), (0,))).astype(LOW)
    attn_away, attn_here, tokens_own, cotangent_own, logits = tie(
        attn_away, attn_here, tokens_own, cotangent_own, logits
    )
    attn_got = swap(attn_away, "c")
    up_x2 = swap(e_up[up_cut:], "x")
    up_z2 = swap(e_up[up_cut:], "zh")
    up_zx1 = swap(up_z1, "x")
    options = jnp.arange(GROUPS, dtype=jnp.int32)
    attn_prob = jax.nn.softmax(logits[:, :GROUPS], axis=-1)
    ffn_prob = jax.nn.softmax(logits[:, GROUPS:], axis=-1)
    attn_pick = (options[None, :] == heads_row[:, None] - 1).astype(WIDE)
    ffn_pick = (options[None, :] == units_row[:, None] - 1).astype(WIDE)
    attn_gate = GROUPS * jnp.sum(attn_prob * attn_pick, axis=-1, keepdims=True)
    ffn_gate = GROUPS * jnp.sum(ffn_prob * ffn_pick, axis=-1, keepdims=True)
    attn_total = dot_to(attn_here, w_out, ((1,), (0,))) + attn_got.astype(WIDE)
    attn_total, attn_gate, ffn_gate, tokens_own, cotangent_own = tie(
        attn_total, attn_gate, ffn_gate, tokens_own, cotangent_own
    )
    attn_parts = group_second(attn_total)
    rows = to_own_order(tokens_own, zh, x).astype(WIDE)
    upstream = to_own_order(cotangent_own, zh, x).astype(WIDE)
    *attn_parts, rows, upstream, up_x2 = tie(*attn_parts, rows, upstream, up_x2)
    attn_sum = group_third(*attn_parts)
    down_cut = e_down.shape[1] // 2
    down_x1 = swap(e_down[:, :down_cut], "x")
    attn_sum, cotangent_all, up_z2, up_zx1, down_x1, e_down = tie(
        attn_sum, cotangent_all, up_z2, up_zx1, down_x1, e_down
    )

    attn_branch = attn_sum + bias_out
    attn_gate_own = mine(attn_gate)
    ffn_gate_own = mine(ffn_gate)
    resid = rows + attn_gate_own * attn_branch
    normed_two, scaled_two, inverse_two = norm_forward(resid, gain_two, shift_two)
    normed_two_low = normed_two.astype(LOW)
    normed_two_low, e_down, cotangent_all, w_in, up_z2 = tie(
        normed_two_low, e_down, cotangent_all, w_in, up_z2
    )
    normed_two_low = lax.all_gather(normed_two_low, GROUP, axis=0, tiled=True)
    down_z1 = swap(e_down[:, :down_cut], "zh")
    up_zx2 = swap(up_z2, "x")
    down_x2 = swap(e_down[:, down_cut:], "x")
    down_grad = gate_rows(bits, cotangent_all, ffn_gate)
    w_in = jnp.concatenate(w_in, axis=0)
    down_grad, down_z1, up_zx2, down_x2, w_in, e_down = tie(
        down_grad, down_z1, up_zx2, down_x2, w_in, e_down
    )
    down_z2 = swap(e_down[:, down_cut:], "zh")
    down_zx1 = swap(down_z1, "x")
    hidden_grad = hidden_grad_rows(down_grad, (e_down, down_x1, down_x2, down_z1))
    w_up = jnp.concatenate([e_up, up_x1, up_x2, up_z1, up_z2, up_zx1, up_zx2], axis=0)
    normed_two_low, hidden_grad, w_up, down_z2, down_zx1 = tie(
        normed_two_low, hidden_grad, w_up, down_z2, down_zx1
    )

    def columns(value, k):
        return value[:, k * 4 * block : (k + 1) * 4 * block]

    down_zx2 = swap(down_z2, "x")
    up_pre = dot_to(normed_two_low, w_up, ((1,), (0,))) + bias_up
    relu_part = jnp.maximum(up_pre, 0.0) * unit_active
    relu_part, down_zx2, hidden_grad, w_up = tie(relu_part, down_zx2, hidden_grad, w_up)
    late = jnp.concatenate([down_z2, down_zx1, down_zx2], axis=1)
    late_at = width - late.shape[1]
    hidden_grad = hidden_grad + dot_to(down_grad[:, late_at:], late, ((1,), (1,)))
    up_grad = (hidden_grad * 2.0 * relu_part).astype(LOW)
    w_down = (e_down, down_x1, down_x2, down_z1, down_z2, down_zx1, down_zx2)
    two_here, two_away = halves(up_grad)
    two_away = dot_to(two_away, w_up, ((1,), (1,))).astype(LOW)
    two_away, two_here, relu_part, down_grad, up_grad = tie(
        two_away, two_here, relu_part, down_grad, up_grad
    )
    two_got = swap(two_away, "c")
    hidden = jnp.square(relu_part).astype(LOW)

    def down_piece(k):
        return dot_to(hidden, columns(down_grad, k), ((0,), (0,)))

    def up_piece(k):
        return dot_to(columns(normed_two_low, k), up_grad, ((0,), (0,)))

    down_send3 = down_piece(3).astype(LOW)
    down_got3 = swap(down_send3, "x")
    two_total = dot_to(two_here, w_up, ((1,), (1,))) + two_got.astype(WIDE)
    two_total, hidden, up_grad, down_send3 = tie(two_total, hidden, up_grad, down_send3)
    two_parts = group_second(two_total)
    up_send3 = up_piece(3).astype(LOW)
    down_send1 = down_piece(1).astype(LOW)
    *two_parts, down_got3, down_send1, up_send3, up_grad = tie(
        *two_parts, down_got3, down_send1, up_send3, up_grad
    )
    normed_two_grad = group_third(*two_parts)
    up_got3 = swap(up_send3, "x")
    down_send2 = (down_piece(2) + down_got3.astype(WIDE)).astype(LOW)
    normed_two_grad, down_send2, hidden, down_grad, up_grad = tie(
        normed_two_grad, down_send2, hidden, down_grad, up_grad
    )

    resid_grad = upstream + norm_backward(normed_two_grad, scaled_two, inverse_two, gain_two)
    gated_attn = attn_gate_own * resid_grad
    gated_low = gated_attn.astype(LOW)
    gated_low, hidden, down_grad, up_grad, normed_two_grad, resid_grad, down_send2 = tie(
        gated_low, hidden, down_grad, up_grad, normed_two_grad, resid_grad, down_send2
    )
    attn_out_grad = lax.all_gather(gated_low, GROUP, axis=0, tiled=True)
    down_far = swap(down_send2, "zh")
    down_got1 = swap(down_send1, "x")
    ffn_away, ffn_here = wide_rows(core, hidden, w_down)
    ffn_got = swap(ffn_away, "c")
    ffn_total = ffn_here.astype(WIDE) + ffn_got.astype(WIDE)
    grad_gain_two = jnp.sum(normed_two_grad * scaled_two, axis=0)
    grad_shift_two = jnp.sum(normed_two_grad, axis=0)
    attn_gate_grad = jnp.sum(resid_grad * attn_branch, axis=-1)
    grad_out_bias = jnp.sum(attn_gate_own * resid_grad, axis=0)
    up_send1 = up_piece(1).astype(LOW)
    up_send2 = (up_piece(2) + up_got3.astype(WIDE)).astype(LOW)
    attn_out_grad, ffn_total, up_send1, up_send2, grad_out_bias, grad_gain_two, down_far = tie(
        attn_out_grad, ffn_total, up_send1, up_send2, grad_out_bias, grad_gain_two, down_far
    )

    up_rows = up_send2.shape[0] // 2
    up_far1 = swap(up_send2[:up_rows], "zh")
    ffn_parts = group_second(ffn_total)
    proj_grad = attend_back(
        qkv, attn_out_grad, w_out, head_active, lse, key_place, span, cosine, sine, heads
    )
    proj_grad, *ffn_parts, attn_out_grad, down_got1, up_far1, hidden, up_send1, up_send2 = tie(
        proj_grad, *ffn_parts, attn_out_grad, down_got1, up_far1, hidden, up_send1, up_send2
    )

    def in_piece(k):
        return dot_to(columns(normed_low, k), proj_grad, ((0,), (0,)))

    def out_piece(k):
        return dot_to(mixed, columns(attn_out_grad, k), ((0,), (0,)))

    one_here, one_away = halves(proj_grad)
    one_away = dot_to(one_away, w_in, ((1,), (1,))).astype(LOW)
    one_away, one_here, proj_grad, attn_out_grad, *ffn_parts, hidden = tie(
        one_away, one_here, proj_grad, attn_out_grad, *ffn_parts, hidden
    )
    one_got = swap(one_away, "c")
    up_far2 = swap(up_send2[up_rows:], "zh")
    in_send3 = in_piece(3).astype(LOW)
    in_got3 = swap(in_send3, "x")
    ffn_sum = group_third(*ffn_parts)
    one_total = dot_to(one_here, w_in, ((1,), (1,))) + one_got.astype(WIDE)
    one_total, proj_grad, attn_out_grad, ffn_sum, in_send3 = tie(
        one_total, proj_grad, attn_out_grad, ffn_sum, in_send3
    )
    one_parts = group_second(one_total)
    in_send1 = in_piece(1).astype(LOW)
    out_send = jnp.stack([out_piece(1), out_piece(3)]).astype(LOW)
    ffn_branch = ffn_sum + bias_down
    block_out = (resid + ffn_gate_own * ffn_branch).astype(LOW)
    ffn_gate_grad = jnp.sum(upstream * ffn_branch, axis=-1)
    grad_down_bias = jnp.sum(ffn_gate_own * upstream, axis=0)
    grad_up_bias = jnp.sum(up_grad.astype(WIDE), axis=0)
    grad_in_bias = jnp.sum(proj_grad.astype(WIDE), axis=0).reshape(3, heads, head_dim)
    logit_grad = jnp.concatenate(
        [
            gate_logit_grad(mine(attn_prob), mine(attn_pick), attn_gate_grad),
            gate_logit_grad(mine(ffn_prob), mine(ffn_pick), ffn_gate_grad),
        ],
        axis=-1,
    )
    normed_own = mine(normed_low)
    grad_router = jnp.dot(logit_grad.T, normed_own.astype(WIDE), precision=HIGHEST)
    router_part = jnp.dot(logit_grad, vectors_f[6:], precision=HIGHEST)

    def both_halves(value, other):
        def batches(v):
            v = v.reshape(2, 2, half, width)
            return flip_where(x, flip_where(zh, v, 0), 1).reshape(4, half, width)

        value, other = batches(value), batches(other)
        return jnp.where(
            y == 0,
            jnp.concatenate([value, other], axis=1),
            jnp.concatenate([other, value], axis=1),
        )

    def spread(rows, cut):
        rows = from_own_order(rows, zh, x)
        return jnp.swapaxes(rows.reshape(cut, 16, block), 0, 1).reshape(16, cut * block)

    sums = jnp.stack([grad_out_bias, grad_gain_two, grad_shift_two, grad_down_bias])
    sums = spread(jnp.concatenate([sums, grad_router], axis=0), n_vec - 2)
    chosen = (jnp.arange(4) == part).astype(WIDE)
    spread_in = (grad_in_bias[:, None] * chosen[None, :, None, None]).reshape(
        3, tp_heads, 16, head_dim // 16
    )
    spread_in = jnp.moveaxis(spread_in, 2, 0).reshape(16, -1)
    spread_up = (grad_up_bias[None, :] * chosen[:, None]).reshape(up_bias.shape[0], 16, block)
    spread_up = jnp.moveaxis(spread_up, 1, 0).reshape(16, -1)
    early = jnp.concatenate([sums, spread_in, spread_up], axis=1)
    _, scaled_one, inverse_one = norm_forward(rows, gain_one, shift_one)
    block_low = from_own_order(block_out, zh, x).reshape(4, half, width)
    (
        *one_parts, in_send1, out_send, block_low, early, router_part, scaled_one, inverse_one,
        in_got3,
    ) = tie(
        *one_parts, in_send1, out_send, block_low, early, router_part, scaled_one, inverse_one,
        in_got3,
    )
    normed_sum = group_third(*one_parts)
    in_got1 = swap(in_send1, "x")
    up_got1 = swap(up_send1, "x")
    in_send2 = (in_piece(2) + in_got3.astype(WIDE)).astype(LOW)
    down_home = (down_piece(0) + down_got1.astype(WIDE) + down_far.astype(WIDE)).astype(LOW)
    normed_sum, in_send2, block_low, early, out_send, up_grad, up_far2, in_got1, down_home = tie(
        normed_sum, in_send2, block_low, early, out_send, up_grad, up_far2, in_got1, down_home
    )

    in_far = swap(in_send2, "zh")
    down_home = exchange(jnp.moveaxis(down_home.reshape(units, 4, block), 1, 0))
    normed_grad = normed_sum + router_part
    tokens_grad = resid_grad + norm_backward(normed_grad, scaled_one, inverse_one, gain_one)
    tokens_low = from_own_order(tokens_grad.astype(LOW), zh, x).reshape(4, half, width)
    tokens_low, normed_grad, block_low, out_send, up_grad, early = tie(
        tokens_low, normed_grad, block_low, out_send, up_grad, early
    )
    tokens_pieces = across([tokens_low[k] for k in range(4)])
    grad_gain_one = jnp.sum(normed_grad * scaled_one, axis=0)
    grad_shift_one = jnp.sum(normed_grad, axis=0)
    last = spread(jnp.stack([grad_gain_one, grad_shift_one]), 2)
    up_far = jnp.concatenate([up_far1, up_far2], axis=0)
    up_home = (up_piece(0) + up_got1.astype(WIDE) + up_far.astype(WIDE)).astype(LOW)
    out_got = swap(out_send, "x")
    *tokens_pieces, last, early, block_low, out_got, in_far, up_home, down_home = tie(
        *tokens_pieces, last, early, block_low, out_got, in_far, up_home, down_home
    )
    tokens_grad = jnp.stack(tokens_pieces)
    tokens_other = swap(tokens_grad, "y")
    in_home = (in_piece(0) + in_got1.astype(WIDE) + in_far.astype(WIDE)).astype(LOW)
    out_far = swap((out_piece(2) + out_got[1].astype(WIDE)).astype(LOW), "zh")
    block_out = jnp.stack(across([block_low[k] for k in range(4)]))
    total = reduce_rows(jnp.concatenate([last, early], axis=1), zh, zl, x, c)
    up_home = exchange(up_home.reshape(4, block, units))
    tokens_other, block_out, out_far, in_home, up_home, total = tie(
        tokens_other, block_out, out_far, in_home, up_home, total
    )
    block_other = swap(block_out, "y")
    in_home = exchange(in_home.reshape(4, block, 3 * inner)).reshape(4, block, 3, heads, head_dim)
    out_home = (out_piece(0) + out_got[0].astype(WIDE) + out_far.astype(WIDE)).astype(LOW)
    out_home = exchange(jnp.moveaxis(out_home.reshape(inner, 4, block), 1, 0))
    at = n_vec * block
    shared = total[:at]
    shared = (shared + swap(shared, "y")).reshape(n_vec, block)
    early = total[at:]
    return (
        both_halves(block_out, block_other),
        both_halves(tokens_grad, tokens_other).astype(WIDE),
        shared[0],
        shared[1],
        shared[6:],
        jnp.transpose(in_home, (1, 2, 0, 3, 4)).reshape(in_weight.shape).astype(WIDE),
        early[: in_bias.size].reshape(in_bias.shape),
        out_home.reshape(out_weight.shape).astype(WIDE),
        shared[2],
        shared[3],
        shared[4],
        jnp.swapaxes(up_home, 0, 1).reshape(up_weight.shape).astype(WIDE),
        early[in_bias.size :].reshape(up_bias.shape),
        down_home.reshape(down_weight.shape).astype(WIDE),
        shared[5],
    )


def solution(mesh):
    body, seq, tp = local, "seq", "tp"
    if mesh.shape["seq"] == 16 and mesh.shape["tp"] == 2:
        mesh = Mesh(mesh.devices.reshape(2, 2, 2, 2, 2), ROWS + ("y",))
        body, seq, tp = grouped, ROWS, "y"
    return jax.shard_map(
        body,
        mesh=mesh,
        in_specs=(
            P(None, seq, None),
            P(None, seq, None),
            P(None, seq),
            P(None, seq),
            P(),
            P(seq),
            P(seq),
            P(None, seq),
            P(seq, None, tp, None),
            P(None, tp, seq),
            P(tp, None, seq),
            P(seq),
            P(seq),
            P(seq),
            P(seq, tp),
            P(tp, seq),
            P(tp, seq),
            P(seq),
        ),
        out_specs=(
            P(None, seq, None),
            P(None, seq, None),
            P(seq),
            P(seq),
            P(None, seq),
            P(seq, None, tp, None),
            P(None, tp, seq),
            P(tp, None, seq),
            P(seq),
            P(seq),
            P(seq),
            P(seq, tp),
            P(tp, seq),
            P(tp, seq),
            P(seq),
        ),
        check_vma=False,
    )
```

```python
import functools
import math

import jax
import jax.numpy as jnp
from jax import lax
from jax.experimental import pallas as pl
from jax.experimental.pallas import tpu as pltpu
from jax.sharding import Mesh
from jax.sharding import PartitionSpec as P

HEADS = 16
HEAD_DIM = 128
FF = 8192
GROUPS = 4


EPSILON = 1e-05
HIGHEST = lax.Precision.HIGHEST


def norm_forward(rows, gain, shift):
    center = rows - jnp.mean(rows, axis=-1, keepdims=True)
    inverse = lax.rsqrt(jnp.mean(center * center, axis=-1, keepdims=True) + EPSILON)
    scaled = center * inverse
    return (scaled * gain + shift, scaled, inverse)


def norm_backward(upstream, scaled, inverse, gain):
    through = upstream * gain
    return inverse * (
        through
        - jnp.mean(through, axis=-1, keepdims=True)
        - scaled * jnp.mean(through * scaled, axis=-1, keepdims=True)
    )


def rotary_tables(positions):
    half_dim = HEAD_DIM // 2
    steps_up = jnp.arange(half_dim, dtype=jnp.float32) * (2.0 / HEAD_DIM)
    inverse = jnp.exp(-math.log(10000.0) * steps_up)
    angles = positions.astype(jnp.float32)[:, None] * inverse[None, :]
    angles = jnp.concatenate([angles, angles], axis=1)
    return (jnp.cos(angles), jnp.sin(angles))


def rotate(vectors, cosine, sine):
    half_dim = vectors.shape[-1] // 2
    turned = jnp.concatenate([-vectors[..., half_dim:], vectors[..., :half_dim]], axis=-1)
    return vectors * cosine[:, None, :] + turned * sine[:, None, :]


def rotate_back(grads, cosine, sine):
    half_dim = grads.shape[-1] // 2
    moved = grads * sine[:, None, :]
    turned = jnp.concatenate([moved[..., half_dim:], -moved[..., :half_dim]], axis=-1)
    return grads * cosine[:, None, :] + turned


def doc_index(lengths, positions):
    ends = jnp.cumsum(lengths)
    return jnp.sum((positions[:, None] >= ends[None, :]).astype(jnp.int32), axis=1)


def gate_logit_grad(prob, pick, gate_grad):
    chosen = jnp.sum(prob * pick, axis=-1, keepdims=True)
    return GROUPS * chosen * (pick - prob) * gate_grad[:, None]


def local(
    tokens,
    cotangent,
    head_groups,
    ffn_widths,
    doc_lengths,
    first_gain,
    first_shift,
    router_weight,
    in_weight,
    in_bias,
    out_weight,
    out_bias,
    second_gain,
    second_shift,
    up_weight,
    up_bias,
    down_weight,
    down_bias,
):
    seq_count = lax.axis_size("seq")
    seq_index = lax.axis_index("seq")
    tp_index = lax.axis_index("tp")
    gathered = (
        lax.all_gather(first_gain, "seq", axis=0, tiled=True),
        lax.all_gather(first_shift, "seq", axis=0, tiled=True),
        lax.all_gather(router_weight, "seq", axis=1, tiled=True),
        lax.all_gather(in_weight, "seq", axis=0, tiled=True),
        lax.all_gather(in_bias, "seq", axis=2, tiled=True),
        lax.all_gather(out_weight, "seq", axis=2, tiled=True),
        lax.all_gather(out_bias, "seq", axis=0, tiled=True),
        lax.all_gather(second_gain, "seq", axis=0, tiled=True),
        lax.all_gather(second_shift, "seq", axis=0, tiled=True),
        lax.all_gather(up_weight, "seq", axis=0, tiled=True),
        lax.all_gather(up_bias, "seq", axis=1, tiled=True),
        lax.all_gather(down_weight, "seq", axis=1, tiled=True),
        lax.all_gather(down_bias, "seq", axis=0, tiled=True),
    )
    (
        gain_one,
        shift_one,
        router_full,
        in_full,
        in_bias_full,
        out_full,
        out_bias_full,
        gain_two,
        shift_two,
        up_full,
        up_bias_full,
        down_full,
        down_bias_full,
    ) = gathered
    micro, tok_dev, width = tokens.shape
    local_heads = in_full.shape[2]
    head_dim = in_full.shape[3]
    inner = local_heads * head_dim
    local_units = up_full.shape[1]
    length = tok_dev * seq_count
    scale = HEAD_DIM ** (-0.5)
    gain_one_f = gain_one.astype(jnp.float32)
    shift_one_f = shift_one.astype(jnp.float32)
    gain_two_f = gain_two.astype(jnp.float32)
    shift_two_f = shift_two.astype(jnp.float32)
    out_bias_f = out_bias_full.astype(jnp.float32)
    down_bias_f = down_bias_full.astype(jnp.float32)
    router_wide = router_full.astype(jnp.float32)
    bias_in = in_bias_full.astype(jnp.float32)
    up_bias_vec = up_bias_full.reshape(local_units).astype(jnp.float32)
    in_matrix = in_full.reshape(width, 3 * inner)
    out_matrix = out_full.reshape(inner, width)
    positions_all = jnp.arange(length, dtype=jnp.int32)
    positions_local = seq_index * tok_dev + jnp.arange(tok_dev, dtype=jnp.int32)
    cosine, sine = rotary_tables(positions_local)
    head_ids = tp_index * local_heads + jnp.arange(local_heads, dtype=jnp.int32)
    unit_ids = tp_index * local_units + jnp.arange(local_units, dtype=jnp.int32)
    options = jnp.arange(GROUPS, dtype=jnp.int32)
    grad_gain_one = jnp.zeros((width,), jnp.float32)
    grad_shift_one = jnp.zeros((width,), jnp.float32)
    grad_router = jnp.zeros(router_full.shape, jnp.float32)
    grad_in = jnp.zeros((width, 3 * inner), jnp.float32)
    grad_in_bias = jnp.zeros(in_bias_full.shape, jnp.float32)
    grad_out = jnp.zeros((inner, width), jnp.float32)
    grad_out_bias = jnp.zeros((width,), jnp.float32)
    grad_gain_two = jnp.zeros((width,), jnp.float32)
    grad_shift_two = jnp.zeros((width,), jnp.float32)
    grad_up = jnp.zeros(up_full.shape, jnp.float32)
    grad_up_bias = jnp.zeros((local_units,), jnp.float32)
    grad_down = jnp.zeros(down_full.shape, jnp.float32)
    grad_down_bias = jnp.zeros((width,), jnp.float32)
    outputs = []
    input_grads = []
    for batch in range(micro):
        rows = tokens[batch].astype(jnp.float32)
        doc_all = doc_index(doc_lengths[batch], positions_all)
        doc_local = lax.dynamic_slice_in_dim(doc_all, seq_index * tok_dev, tok_dev, 0)
        allowed = (positions_all[None, :] <= positions_local[:, None]) & (
            doc_all[None, :] == doc_local[:, None]
        )
        head_active = (head_ids[None, :] // (HEADS // GROUPS) < head_groups[batch][:, None]).astype(
            jnp.float32
        )
        unit_active = (unit_ids[None, :] // (FF // GROUPS) < ffn_widths[batch][:, None]).astype(
            jnp.float32
        )
        normed, scaled_one, inverse_one = norm_forward(rows, gain_one_f, shift_one_f)
        normed_low = normed.astype(jnp.bfloat16)
        logits = jnp.dot(normed_low, router_full.T, preferred_element_type=jnp.float32)
        attn_prob = jax.nn.softmax(logits[:, :GROUPS], axis=-1)
        ffn_prob = jax.nn.softmax(logits[:, GROUPS:], axis=-1)
        attn_pick = (options[None, :] == head_groups[batch][:, None] - 1).astype(jnp.float32)
        ffn_pick = (options[None, :] == ffn_widths[batch][:, None] - 1).astype(jnp.float32)
        attn_gate = GROUPS * jnp.sum(attn_prob * attn_pick, axis=-1)
        ffn_gate = GROUPS * jnp.sum(ffn_prob * ffn_pick, axis=-1)
        projected = jnp.dot(normed_low, in_matrix, preferred_element_type=jnp.float32)
        projected = projected.reshape(tok_dev, 3, local_heads, head_dim) + bias_in
        queries = rotate(projected[:, 0], cosine, sine).astype(jnp.bfloat16)
        keys_low = rotate(projected[:, 1], cosine, sine).astype(jnp.bfloat16)
        values_low = projected[:, 2].astype(jnp.bfloat16)
        keys_all, values_all = (
            lax.all_gather(keys_low, "seq", axis=0, tiled=True),
            lax.all_gather(values_low, "seq", axis=0, tiled=True),
        )
        raw_scores = jnp.einsum(
            "qhd,khd->hqk", queries, keys_all, preferred_element_type=jnp.float32
        )
        scores = jnp.where(allowed[None], raw_scores * scale, -jnp.inf)
        row_max = jnp.max(scores, axis=-1, keepdims=True)
        weights = jnp.exp(scores - row_max)
        row_total = jnp.sum(weights, axis=-1, keepdims=True)
        log_total = row_max + jnp.log(row_total)
        probs = weights / row_total
        attended = jnp.einsum(
            "hqk,khd->qhd",
            probs.astype(jnp.bfloat16),
            values_all,
            preferred_element_type=jnp.float32,
        )
        mixed_heads = (attended * head_active[:, :, None]).astype(jnp.bfloat16)
        mixed_flat = mixed_heads.reshape(tok_dev, inner)
        attn_part = jnp.dot(mixed_flat, out_matrix, preferred_element_type=jnp.float32)
        attn_sum = lax.psum(attn_part, "tp")
        attn_branch = attn_sum + out_bias_f
        resid = rows + attn_gate[:, None] * attn_branch
        normed_two, scaled_two, inverse_two = norm_forward(resid, gain_two_f, shift_two_f)
        normed_two_low = normed_two.astype(jnp.bfloat16)
        up_pre = jnp.dot(normed_two_low, up_full, preferred_element_type=jnp.float32) + up_bias_vec
        relu_part = jnp.maximum(up_pre, 0.0)
        hidden = (unit_active * jnp.square(relu_part)).astype(jnp.bfloat16)
        down_part = jnp.dot(hidden, down_full, preferred_element_type=jnp.float32)
        down_sum = lax.psum(down_part.astype(jnp.bfloat16), "tp").astype(jnp.float32)
        ffn_branch = down_sum + down_bias_f
        outputs.append((resid + ffn_gate[:, None] * ffn_branch).astype(jnp.bfloat16))
        upstream = cotangent[batch].astype(jnp.float32)
        ffn_gate_grad = jnp.sum(upstream * ffn_branch, axis=-1)
        gated_up = ffn_gate[:, None] * upstream
        grad_down_bias = grad_down_bias + jnp.sum(gated_up, axis=0)
        down_grad = gated_up.astype(jnp.bfloat16)
        grad_down = grad_down + jnp.einsum(
            "tf,td->fd", hidden, down_grad, preferred_element_type=jnp.float32
        )
        hidden_grad = jnp.einsum(
            "td,fd->tf", down_grad, down_full, preferred_element_type=jnp.float32
        )
        up_grad = (hidden_grad * unit_active * 2.0 * relu_part).astype(jnp.bfloat16)
        grad_up_bias = grad_up_bias + jnp.sum(up_grad.astype(jnp.float32), axis=0)
        grad_up = grad_up + jnp.einsum(
            "td,tf->df", normed_two_low, up_grad, preferred_element_type=jnp.float32
        )
        normed_two_part = jnp.einsum(
            "tf,df->td", up_grad, up_full, preferred_element_type=jnp.float32
        )
        normed_two_grad = lax.psum(normed_two_part, "tp")
        grad_gain_two = grad_gain_two + jnp.sum(normed_two_grad * scaled_two, axis=0)
        grad_shift_two = grad_shift_two + jnp.sum(normed_two_grad, axis=0)
        resid_grad = upstream + norm_backward(normed_two_grad, scaled_two, inverse_two, gain_two_f)
        attn_gate_grad = jnp.sum(resid_grad * attn_branch, axis=-1)
        gated_attn = attn_gate[:, None] * resid_grad
        grad_out_bias = grad_out_bias + jnp.sum(gated_attn, axis=0)
        attn_out_grad = gated_attn.astype(jnp.bfloat16)
        grad_out = grad_out + jnp.einsum(
            "ti,td->id", mixed_flat, attn_out_grad, preferred_element_type=jnp.float32
        )
        mixed_grad = jnp.einsum(
            "td,id->ti", attn_out_grad, out_matrix, preferred_element_type=jnp.float32
        )
        attended_grad = (
            mixed_grad.reshape(tok_dev, local_heads, head_dim) * head_active[:, :, None]
        ).astype(jnp.bfloat16)
        again_raw = jnp.einsum(
            "qhd,khd->hqk", queries, keys_all, preferred_element_type=jnp.float32
        )
        again_scores = jnp.where(allowed[None], again_raw * scale, -jnp.inf)
        probs_again = jnp.exp(again_scores - log_total)
        prob_grad = jnp.einsum(
            "qhd,khd->hqk", attended_grad, values_all, preferred_element_type=jnp.float32
        )
        row_dot = jnp.sum(probs_again * prob_grad, axis=-1, keepdims=True)
        score_grad = (probs_again * (prob_grad - row_dot) * scale).astype(jnp.bfloat16)
        query_rot_grad = jnp.einsum(
            "hqk,khd->qhd", score_grad, keys_all, preferred_element_type=jnp.float32
        )
        probs_low = probs_again.astype(jnp.bfloat16)
        key_part = jnp.einsum(
            "hqk,qhd->khd", score_grad, queries, preferred_element_type=jnp.float32
        )
        value_part = jnp.einsum(
            "hqk,qhd->khd", probs_low, attended_grad, preferred_element_type=jnp.float32
        )
        combined = lax.psum_scatter(
            jnp.concatenate([key_part, value_part], axis=1).reshape(
                lax.axis_size("seq") * tok_dev, 2 * inner
            ),
            "seq",
            scatter_dimension=0,
            tiled=True,
        )
        combined = combined.reshape(tok_dev, 2 * local_heads, head_dim)
        key_rot_grad = combined[:, :local_heads]
        value_grad = combined[:, local_heads:]
        query_grad = rotate_back(query_rot_grad, cosine, sine)
        key_grad = rotate_back(key_rot_grad, cosine, sine)
        proj_grad = jnp.stack([query_grad, key_grad, value_grad], axis=1).astype(jnp.bfloat16)
        grad_in_bias = grad_in_bias + jnp.sum(proj_grad.astype(jnp.float32), axis=0)
        proj_flat = proj_grad.reshape(tok_dev, 3 * inner)
        grad_in = grad_in + jnp.einsum(
            "tw,tc->wc", normed_low, proj_flat, preferred_element_type=jnp.float32
        )
        normed_part = jnp.einsum(
            "tc,wc->tw", proj_flat, in_matrix, preferred_element_type=jnp.float32
        )
        logit_grad = jnp.concatenate(
            [
                gate_logit_grad(attn_prob, attn_pick, attn_gate_grad),
                gate_logit_grad(ffn_prob, ffn_pick, ffn_gate_grad),
            ],
            axis=-1,
        )
        grad_router = grad_router + jnp.dot(
            logit_grad.T, normed_low.astype(jnp.float32), precision=HIGHEST
        )
        router_part = jnp.dot(logit_grad, router_wide, precision=HIGHEST)
        normed_grad = lax.psum(normed_part, "tp") + router_part
        grad_gain_one = grad_gain_one + jnp.sum(normed_grad * scaled_one, axis=0)
        grad_shift_one = grad_shift_one + jnp.sum(normed_grad, axis=0)
        input_grads.append(
            resid_grad + norm_backward(normed_grad, scaled_one, inverse_one, gain_one_f)
        )
    reduced = (
        lax.psum_scatter(grad_gain_one, "seq", scatter_dimension=0, tiled=True),
        lax.psum_scatter(grad_shift_one, "seq", scatter_dimension=0, tiled=True),
        lax.psum_scatter(grad_router, "seq", scatter_dimension=1, tiled=True),
        lax.psum_scatter(
            grad_in.reshape(width, 3, local_heads, head_dim), "seq", scatter_dimension=0, tiled=True
        ),
        lax.psum_scatter(grad_in_bias, "seq", scatter_dimension=2, tiled=True),
        lax.psum_scatter(
            grad_out.reshape(local_heads, head_dim, width), "seq", scatter_dimension=2, tiled=True
        ),
        lax.psum_scatter(grad_out_bias, "seq", scatter_dimension=0, tiled=True),
        lax.psum_scatter(grad_gain_two, "seq", scatter_dimension=0, tiled=True),
        lax.psum_scatter(grad_shift_two, "seq", scatter_dimension=0, tiled=True),
        lax.psum_scatter(grad_up, "seq", scatter_dimension=0, tiled=True),
        lax.psum_scatter(
            grad_up_bias.reshape(up_bias_full.shape), "seq", scatter_dimension=1, tiled=True
        ),
        lax.psum_scatter(grad_down, "seq", scatter_dimension=1, tiled=True),
        lax.psum_scatter(grad_down_bias, "seq", scatter_dimension=0, tiled=True),
    )
    return (
        jnp.stack(outputs),
        jnp.stack(input_grads),
        reduced[0],
        reduced[1],
        reduced[2],
        reduced[3],
        reduced[4],
        reduced[5],
        reduced[6],
        reduced[7],
        reduced[8],
        reduced[9],
        reduced[10],
        reduced[11],
        reduced[12],
    )


ROWS = ("zh", "zl", "x", "c")
GROUP = ("c", "zl", "y")
PARTS = ("zh", "x")
LOW = jnp.bfloat16
WIDE = jnp.float32


def swap(value, axis):
    return lax.ppermute(value, axis, [(0, 1), (1, 0)])


def flip_where(bit, value, axis):
    return jnp.where(bit == 1, jnp.flip(value, axis), value)


def to_own_order(value, zh, x):
    lead, width = value.shape[:-1], value.shape[-1]
    value = value.reshape(lead + (2, 2, 2, 2, width // 16))
    value = jnp.swapaxes(value, -4, -3)
    value = flip_where(zh, value, -5)
    value = flip_where(x, value, -4)
    return value.reshape(lead + (width,))


def from_own_order(value, zh, x):
    lead, width = value.shape[:-1], value.shape[-1]
    value = value.reshape(lead + (2, 2, 2, 2, width // 16))
    value = flip_where(zh, value, -5)
    value = flip_where(x, value, -4)
    value = jnp.swapaxes(value, -4, -3)
    return value.reshape(lead + (width,))


def tie(*values):
    return lax.optimization_barrier(values)


def dot_to(left, right, dims):
    return lax.dot_general(left, right, (dims, ((), ())), preferred_element_type=WIDE)


def gather_over(value, axes, bits):
    for axis, bit in zip(axes, bits):
        other = swap(value, axis)
        value = jnp.where(
            bit == 0,
            jnp.concatenate([value, other], axis=0),
            jnp.concatenate([other, value], axis=0),
        )
    return value


def reduce_rows(value, zh, zl, x, c):
    value = value.reshape(2, 2, 2, 2, -1)
    for axis, at, bit in (("zh", 0, zh), ("zl", 0, zl), ("x", 0, x), ("c", 0, c)):
        keep = lax.dynamic_index_in_dim(value, bit, at, keepdims=False)
        send = lax.dynamic_index_in_dim(value, 1 - bit, at, keepdims=False)
        value = keep + swap(send, axis)
    return value


BLOCK_Q = 256
NEVER = -1e30


def chunks(bits_ref, width):
    run = width // 8
    for at in range(8):
        zh, x, zl = at // 4, at // 2 % 2, at % 2
        theirs = ((zh ^ bits_ref[0]) * 2 + zl) * 2 + (x ^ bits_ref[1])
        yield at * run, pl.multiple_of(theirs * run, run)


def norm_kernel(bits_ref, x_ref, gain_ref, shift_ref, router_ref, out_ref, logits_ref):
    width = x_ref.shape[1]
    rows = x_ref[...].astype(WIDE)
    mean = jnp.mean(rows, axis=-1, keepdims=True)
    center = rows - mean
    inverse = lax.rsqrt(jnp.mean(center * center, axis=-1, keepdims=True) + EPSILON)
    logits = None
    for mine, theirs in chunks(bits_ref, width):
        at = slice(mine, mine + width // 8)
        part = (x_ref[:, pl.ds(theirs, width // 8)].astype(WIDE) - mean) * inverse
        low = (part * gain_ref[:, at] + shift_ref[:, at]).astype(LOW)
        out_ref[:, at] = low
        got = dot_to(low, router_ref[:, at], ((1,), (1,)))
        logits = got if logits is None else logits + got
    logits_ref[...] = logits


def norm_rows(bits, rows, gain, shift, router):
    length, width = rows.shape
    n = router.shape[0]
    return pl.pallas_call(
        norm_kernel,
        grid_spec=pltpu.PrefetchScalarGridSpec(
            num_scalar_prefetch=1,
            grid=(length // BLOCK_Q,),
            in_specs=[
                pl.BlockSpec((BLOCK_Q, width), lambda i, bits: (i, 0)),
                pl.BlockSpec((1, width), lambda i, bits: (0, 0)),
                pl.BlockSpec((1, width), lambda i, bits: (0, 0)),
                pl.BlockSpec((n, width), lambda i, bits: (0, 0)),
            ],
            out_specs=[
                pl.BlockSpec((BLOCK_Q, width), lambda i, bits: (i, 0)),
                pl.BlockSpec((BLOCK_Q, n), lambda i, bits: (i, 0)),
            ],
        ),
        out_shape=[
            jax.ShapeDtypeStruct((length, width), LOW),
            jax.ShapeDtypeStruct((length, n), WIDE),
        ],
        name="norm_rows",
    )(bits, rows, gain, shift, router)


def gate_kernel(bits_ref, x_ref, gate_ref, out_ref):
    width = x_ref.shape[1]
    gate = gate_ref[...]
    for mine, theirs in chunks(bits_ref, width):
        part = x_ref[:, pl.ds(theirs, width // 8)].astype(WIDE) * gate
        out_ref[:, mine : mine + width // 8] = part.astype(LOW)


def gate_rows(bits, rows, gate):
    length, width = rows.shape
    return pl.pallas_call(
        gate_kernel,
        grid_spec=pltpu.PrefetchScalarGridSpec(
            num_scalar_prefetch=1,
            grid=(length // BLOCK_Q,),
            in_specs=[
                pl.BlockSpec((BLOCK_Q, width), lambda i, bits: (i, 0)),
                pl.BlockSpec((BLOCK_Q, 1), lambda i, bits: (i, 0)),
            ],
            out_specs=pl.BlockSpec((BLOCK_Q, width), lambda i, bits: (i, 0)),
        ),
        out_shape=jax.ShapeDtypeStruct((length, width), LOW),
        name="gate_rows",
    )(bits, rows, gate)


def add_dots(left_ref, pieces, start=None):
    at, total = 0, start
    for piece in pieces:
        n = piece.shape[0]
        part = dot_to(left_ref[:, at : at + n], piece[...], ((1,), (0,)))
        total = part if total is None else total + part
        at += n
    return total


def row_spec(steps, rows, width):
    half = steps // 2
    return pl.BlockSpec((rows, width), lambda i, bit: ((i + (1 - bit[0]) * half) % steps, 0))


def fixed(value):
    return pl.BlockSpec(value.shape, lambda *_: (0, 0))


def hidden_kernel(cuts, h_ref, active_ref, bias_ref, *refs):
    pieces, (relu_ref, hidden_ref) = refs[:-2], refs[-2:]
    at, used = 0, 0
    for n in cuts:
        group = pieces[used : used + n]
        used += n
        width = group[0].shape[1]
        total = add_dots(h_ref, group, bias_ref[:, at : at + width])
        relu = jnp.maximum(total, 0.0) * active_ref[...]
        relu_ref[:, at : at + width] = relu
        hidden_ref[:, at : at + width] = (relu * relu).astype(LOW)
        at += width


def hidden_rows(normed, active, bias, groups):
    length, width = normed.shape
    units = bias.shape[1]
    rows = BLOCK_Q
    pieces = [p for group in groups for p in group]
    return pl.pallas_call(
        functools.partial(hidden_kernel, tuple(len(g) for g in groups)),
        grid=(length // rows,),
        in_specs=[
            pl.BlockSpec((rows, width), lambda i: (i, 0)),
            pl.BlockSpec((rows, 1), lambda i: (i, 0)),
            fixed(bias),
        ]
        + [fixed(p) for p in pieces],
        out_specs=[pl.BlockSpec((rows, units), lambda i: (i, 0))] * 2,
        out_shape=[
            jax.ShapeDtypeStruct((length, units), WIDE),
            jax.ShapeDtypeStruct((length, units), LOW),
        ],
        name="hidden_rows",
    )(normed, active, bias, *pieces)


def ffn_kernel(cuts_down, cuts_up, bit_ref, dz_ref, relu_ref, *refs):
    du_ref, dh_ref = refs[-2:]
    n_down = sum(cuts_down)
    downs, ups = refs[:n_down], refs[n_down:-2]
    at, used = 0, 0
    parts = []
    for n in cuts_down:
        group = downs[used : used + n]
        used += n
        grad, col = None, 0
        for piece in group:
            k = piece.shape[1]
            part = dot_to(dz_ref[:, col : col + k], piece[...], ((1,), (1,)))
            grad = part if grad is None else grad + part
            col += k
        m = grad.shape[1]
        du = (grad * 2.0 * relu_ref[:, at : at + m]).astype(LOW)
        du_ref[:, at : at + m] = du
        parts.append((at, m, du))
        at += m
    for j in range(cuts_up[0]):
        total, used = None, 0
        for g, n in enumerate(cuts_up):
            piece = ups[used + j]
            used += n
            part = dot_to(parts[g][2], piece[...], ((1,), (1,)))
            total = part if total is None else total + part
        k = total.shape[1]
        dh_ref[:, j * k : (j + 1) * k] = total.astype(LOW)


def ffn_rows(bit, down_grad, relu, down_groups, up_groups):
    length, width = down_grad.shape
    units = relu.shape[1]
    rows = BLOCK_Q
    steps = length // rows
    downs = [p for group in down_groups for p in group]
    ups = [p for group in up_groups for p in group]
    return pl.pallas_call(
        functools.partial(
            ffn_kernel, tuple(len(g) for g in down_groups), tuple(len(g) for g in up_groups)
        ),
        grid_spec=pltpu.PrefetchScalarGridSpec(
            num_scalar_prefetch=1,
            grid=(steps,),
            in_specs=[row_spec(steps, rows, width), row_spec(steps, rows, units)]
            + [fixed(p) for p in downs]
            + [fixed(p) for p in ups],
            out_specs=[
                row_spec(steps, rows, units),
                pl.BlockSpec((rows, width), lambda i, bit: (i, 0)),
            ],
        ),
        out_shape=[
            jax.ShapeDtypeStruct((length, units), LOW),
            jax.ShapeDtypeStruct((length, width), LOW),
        ],
        name="ffn_rows",
    )(bit, down_grad, relu, *downs, *ups)


def wide_kernel(cuts, left_ref, *refs):
    pieces, out_ref = refs[:-1], refs[-1]
    for j in range(cuts[0]):
        total, used, at = None, 0, 0
        for n in cuts:
            piece = pieces[used + j]
            used += n
            k = piece.shape[0]
            part = dot_to(left_ref[:, at : at + k], piece[...], ((1,), (0,)))
            total = part if total is None else total + part
            at += k
        m = total.shape[1]
        out_ref[:, j * m : (j + 1) * m] = total.astype(LOW)


def wide_rows(left, groups):
    length, depth = left.shape
    rows = BLOCK_Q
    pieces = [p for group in groups for p in group]
    width = sum(p.shape[1] for p in groups[0])
    return pl.pallas_call(
        functools.partial(wide_kernel, tuple(len(g) for g in groups)),
        grid=(length // rows,),
        in_specs=[pl.BlockSpec((rows, depth), lambda i: (i, 0))] + [fixed(p) for p in pieces],
        out_specs=pl.BlockSpec((rows, width), lambda i: (i, 0)),
        out_shape=jax.ShapeDtypeStruct((length, width), LOW),
        name="wide_rows",
    )(left, *pieces)


def own_kernel(bits_ref, a_ref, b_ref, a_out, b_out):
    width = a_ref.shape[1]
    for mine, theirs in chunks(bits_ref, width):
        at = slice(mine, mine + width // 8)
        a_out[:, at] = a_ref[:, pl.ds(theirs, width // 8)].astype(WIDE)
        b_out[:, at] = b_ref[:, pl.ds(theirs, width // 8)].astype(WIDE)


def own_rows(bits, a, b):
    shape = jax.ShapeDtypeStruct(a.shape, WIDE)
    whole = pl.BlockSpec(a.shape, lambda i, bits: (0, 0))
    return pl.pallas_call(
        own_kernel,
        grid_spec=pltpu.PrefetchScalarGridSpec(
            num_scalar_prefetch=1, grid=(1,), in_specs=[whole, whole], out_specs=[whole, whole]
        ),
        out_shape=[shape, shape],
        name="own_rows",
    )(bits, a, b)


def home_kernel(bits_ref, a_ref, out_ref):
    width = a_ref.shape[1]
    for mine, theirs in chunks(bits_ref, width):
        part = a_ref[:, mine : mine + width // 8]
        out_ref[:, pl.ds(theirs, width // 8)] = part.astype(LOW)


def home_rows(bits, a):
    whole = pl.BlockSpec(a.shape, lambda i, bits: (0, 0))
    return pl.pallas_call(
        home_kernel,
        grid_spec=pltpu.PrefetchScalarGridSpec(
            num_scalar_prefetch=1, grid=(1,), in_specs=[whole], out_specs=whole
        ),
        out_shape=jax.ShapeDtypeStruct(a.shape, LOW),
        name="home_rows",
    )(bits, a)


def first_kernel(
    bits_ref, sum_ref, router_ref, rows_ref, resid_ref, gain_ref, out_ref, sums_ref
):
    grad = sum_ref[...] + router_ref[...]
    rows = rows_ref[...]
    gain = gain_ref[...]
    _, scaled, inverse = norm_forward(rows, gain, 0.0)
    sums_ref[0:1, :] = jnp.sum(grad * scaled, axis=0, keepdims=True)
    sums_ref[1:2, :] = jnp.sum(grad, axis=0, keepdims=True)
    out = (resid_ref[...] + norm_backward(grad, scaled, inverse, gain)).astype(LOW)
    width = out.shape[1]
    for mine, theirs in chunks(bits_ref, width):
        out_ref[:, pl.ds(theirs, width // 8)] = out[:, mine : mine + width // 8]


def first_back(bits, normed_sum, router_part, rows, resid_grad, gain):
    whole = pl.BlockSpec(rows.shape, lambda i, bits: (0, 0))
    width = rows.shape[1]
    return pl.pallas_call(
        first_kernel,
        grid_spec=pltpu.PrefetchScalarGridSpec(
            num_scalar_prefetch=1,
            grid=(1,),
            in_specs=[whole] * 4 + [pl.BlockSpec((1, width), lambda i, bits: (0, 0))],
            out_specs=[whole, pl.BlockSpec((2, width), lambda i, bits: (0, 0))],
        ),
        out_shape=[
            jax.ShapeDtypeStruct(rows.shape, LOW),
            jax.ShapeDtypeStruct((2, width), WIDE),
        ],
        name="first_back",
    )(bits, normed_sum, router_part, rows, resid_grad, gain)


def qkv_kernel(h_ref, *refs):
    pieces, (bias_ref, cos_ref, sin_ref, out_ref) = refs[:-4], refs[-4:]
    total = add_dots(h_ref, pieces, bias_ref[...])
    turned = out_ref.shape[1] // HEAD_DIM * 2 // 3
    cosine, sine = cos_ref[...], sin_ref[...]
    for j in range(out_ref.shape[1] // HEAD_DIM):
        at = slice(j * HEAD_DIM, (j + 1) * HEAD_DIM)
        part = total[:, at]
        if j < turned:
            part = part * cosine + pltpu.roll(part, HEAD_DIM // 2, 1) * sine
        out_ref[:, at] = part.astype(LOW)


def qkv_rows(normed, pieces, bias, cosine, sine):
    length, width = normed.shape
    out = bias.shape[1]
    rows = BLOCK_Q
    return pl.pallas_call(
        qkv_kernel,
        grid=(length // rows,),
        in_specs=[pl.BlockSpec((rows, width), lambda i: (i, 0))]
        + [fixed(p) for p in pieces]
        + [
            fixed(bias),
            pl.BlockSpec((rows, HEAD_DIM), lambda i: (i, 0)),
            pl.BlockSpec((rows, HEAD_DIM), lambda i: (i, 0)),
        ],
        out_specs=pl.BlockSpec((rows, out), lambda i: (i, 0)),
        out_shape=jax.ShapeDtypeStruct((length, out), LOW),
        name="qkv_rows",
    )(normed, *pieces, bias, cosine, sine)


def attend_kernel(q_ref, k_ref, v_ref, key_ref, span_ref, active_ref, out_ref, lse_ref):
    scores = dot_to(k_ref[...], q_ref[...], ((1,), (1,))) * (HEAD_DIM**-0.5)
    key = key_ref[...]
    allowed = (key >= span_ref[0:1, :]) & (key <= span_ref[1:2, :])
    scores = jnp.where(allowed, scores, NEVER)
    top = jnp.max(scores, axis=0, keepdims=True)
    weights = jnp.exp(scores - top)
    total = jnp.sum(weights, axis=0, keepdims=True)
    probs = (weights * (1.0 / total)).astype(LOW)
    mixed = dot_to(probs, v_ref[...], ((0,), (0,)))
    out_ref[...] = (mixed * active_ref[0]).astype(LOW)
    lse_ref[0] = top + jnp.log(total)


def turn_back(grad, cosine, sine):
    lane = lax.broadcasted_iota(jnp.int32, grad.shape, 1)
    moved = pltpu.roll(grad * sine, HEAD_DIM // 2, 1)
    return grad * cosine + jnp.where(lane < HEAD_DIM // 2, moved, -moved)


def attend_back_kernel(
    q_ref, k_ref, v_ref, da_ref, w_ref, active_ref, lse_ref,
    key_ref, span_ref, cos_ref, sin_ref, out_ref, dk_sum, dv_sum,
):
    head, step = pl.program_id(0), pl.program_id(1)
    inner = out_ref.shape[1] // 3

    @pl.when(step == 0)
    def _():
        dk_sum[...] = jnp.zeros_like(dk_sum)
        dv_sum[...] = jnp.zeros_like(dv_sum)

    scale = HEAD_DIM**-0.5
    query, key = q_ref[...], k_ref[...]
    grad = dot_to(da_ref[...], w_ref[...], ((1,), (1,)))
    grad = (grad * active_ref[0]).astype(LOW)
    scores = dot_to(key, query, ((1,), (1,))) * scale
    place = key_ref[...]
    allowed = (place >= span_ref[0:1, :]) & (place <= span_ref[1:2, :])
    probs = jnp.exp(jnp.where(allowed, scores, NEVER) - lse_ref[0])
    prob_grad = dot_to(v_ref[...], grad, ((1,), (1,)))
    delta = jnp.sum(probs * prob_grad, axis=0, keepdims=True)
    score_grad = (probs * (prob_grad - delta) * scale).astype(LOW)
    dv_sum[...] += dot_to(probs.astype(LOW), grad, ((1,), (0,)))
    dk_sum[...] += dot_to(score_grad, query, ((1,), (0,)))
    dq = dot_to(score_grad, key, ((0,), (0,)))
    at = pl.ds(pl.multiple_of(step * BLOCK_Q, BLOCK_Q), BLOCK_Q)
    col = pl.multiple_of(head * HEAD_DIM, HEAD_DIM)
    dq = turn_back(dq, cos_ref[at, :], sin_ref[at, :])
    out_ref[at, pl.ds(col, HEAD_DIM)] = dq.astype(LOW)

    @pl.when(step == pl.num_programs(1) - 1)
    def _():
        dk = turn_back(dk_sum[...], cos_ref[...], sin_ref[...])
        out_ref[:, pl.ds(inner + col, HEAD_DIM)] = dk.astype(LOW)
        out_ref[:, pl.ds(2 * inner + col, HEAD_DIM)] = dv_sum[...].astype(LOW)


def attend(qkv, key_place, span, active, heads):
    length = qkv.shape[0]
    d = HEAD_DIM
    n = heads
    return pl.pallas_call(
        attend_kernel,
        grid=(heads, length // BLOCK_Q),
        in_specs=[
            pl.BlockSpec((BLOCK_Q, d), lambda h, i: (i, h)),
            pl.BlockSpec((length, d), lambda h, i: (0, n + h)),
            pl.BlockSpec((length, d), lambda h, i: (0, 2 * n + h)),
            pl.BlockSpec((length, 1), lambda h, i: (0, 0)),
            pl.BlockSpec((2, BLOCK_Q), lambda h, i: (0, i)),
            pl.BlockSpec((1, BLOCK_Q, 1), lambda h, i: (h, i, 0)),
        ],
        out_specs=[
            pl.BlockSpec((BLOCK_Q, d), lambda h, i: (i, h)),
            pl.BlockSpec((1, 1, BLOCK_Q), lambda h, i: (h, 0, i)),
        ],
        out_shape=[
            jax.ShapeDtypeStruct((length, heads * d), LOW),
            jax.ShapeDtypeStruct((heads, 1, length), WIDE),
        ],
        name="attend",
    )(qkv, qkv, qkv, key_place, span, active)


def attend_back(qkv, out_grad, w_out, active, lse, key_place, span, cosine, sine, heads):
    length, width = out_grad.shape
    d = HEAD_DIM
    n = heads
    return pl.pallas_call(
        attend_back_kernel,
        grid=(heads, length // BLOCK_Q),
        in_specs=[
            pl.BlockSpec((BLOCK_Q, d), lambda h, i: (i, h)),
            pl.BlockSpec((length, d), lambda h, i: (0, n + h)),
            pl.BlockSpec((length, d), lambda h, i: (0, 2 * n + h)),
            pl.BlockSpec((BLOCK_Q, width), lambda h, i: (i, 0)),
            pl.BlockSpec((d, width), lambda h, i: (h, 0)),
            pl.BlockSpec((1, BLOCK_Q, 1), lambda h, i: (h, i, 0)),
            pl.BlockSpec((1, 1, BLOCK_Q), lambda h, i: (h, 0, i)),
            pl.BlockSpec((length, 1), lambda h, i: (0, 0)),
            pl.BlockSpec((2, BLOCK_Q), lambda h, i: (0, i)),
            pl.BlockSpec((length, d), lambda h, i: (0, 0)),
            pl.BlockSpec((length, d), lambda h, i: (0, 0)),
        ],
        out_specs=pl.BlockSpec((length, 3 * heads * d), lambda h, i: (0, 0)),
        out_shape=jax.ShapeDtypeStruct((length, 3 * heads * d), LOW),
        scratch_shapes=[pltpu.VMEM((length, d), WIDE), pltpu.VMEM((length, d), WIDE)],
        name="attend_back",
    )(qkv, qkv, qkv, out_grad, w_out, active, lse, key_place, span, cosine, sine)


def grouped(
    tokens,
    cotangent,
    head_groups,
    ffn_widths,
    doc_lengths,
    first_gain,
    first_shift,
    router_weight,
    in_weight,
    in_bias,
    out_weight,
    out_bias,
    second_gain,
    second_shift,
    up_weight,
    up_bias,
    down_weight,
    down_bias,
):
    zh, zl, x, c, y = (lax.axis_index(a) for a in ("zh", "zl", "x", "c", "y"))
    micro, tok_dev, width = tokens.shape
    half = tok_dev // 2
    own = 4 * half
    length = 16 * tok_dev
    block = width // 16
    tp_heads, head_dim = in_weight.shape[2:]
    heads = tp_heads // 4
    inner = heads * head_dim
    tp_units = up_weight.shape[1]
    units = tp_units // 4
    batch = zh * 2 + x
    part = zl * 2 + c
    place = (c * 2 + zl) * 2 + y

    def exchange(value):
        return lax.all_to_all(value, ("zl", "c"), 0, 0, tiled=True)

    def keep_and_send(value, bit, at):
        return (
            lax.dynamic_index_in_dim(value, bit, at, keepdims=False),
            lax.dynamic_index_in_dim(value, 1 - bit, at, keepdims=False),
        )

    def across(pieces):
        return (
            pieces[0],
            swap(pieces[1], "x"),
            swap(pieces[2], "zh"),
            lax.ppermute(pieces[3], PARTS, [(i, i ^ 3) for i in range(4)]),
        )

    def to_batch(value):
        value = lax.dynamic_slice_in_dim(value, y * half, half, 1)
        return across(
            [lax.dynamic_index_in_dim(value, batch ^ k, 0, keepdims=False) for k in range(4)]
        )

    bits = jnp.stack([zh, x]).astype(jnp.int32)
    core = c.reshape(1).astype(jnp.int32)
    e_in = exchange(jnp.moveaxis(in_weight.reshape(block, 3, 4, heads, head_dim), 2, 0))
    e_in = e_in.reshape(4 * block, 3 * inner)
    token_pieces = to_batch(tokens)

    def rows_of_block(value):
        value = value.astype(WIDE).reshape(-1)
        return jnp.pad(value, (0, -value.shape[0] % block)).reshape(-1, block)

    small = jnp.concatenate(
        [
            rows_of_block(v)
            for v in (
                first_gain,
                first_shift,
                second_gain,
                second_shift,
                out_bias,
                down_bias,
                router_weight,
                up_bias,
                head_groups,
                ffn_widths,
                in_bias,
            )
        ],
        axis=0,
    )
    n_small = small.shape[0]
    small = small[None]
    small = gather_over(small, ("zh", "x"), (zh, x))
    *token_pieces, small, e_in = tie(*token_pieces, small, e_in)
    tokens_own = jnp.concatenate(token_pieces, axis=0)
    tokens_all = lax.all_gather(tokens_own, GROUP, axis=0, tiled=True)

    index = jnp.arange(length, dtype=jnp.int32).reshape(2, 2, 2, 2, 2, half)

    def by_place(value):
        lead = tuple(range(value.ndim - 6))
        at = value.ndim - 6
        value = jnp.transpose(value, lead + tuple(at + i for i in (3, 1, 4, 0, 2, 5)))
        return value.reshape(value.shape[: value.ndim - 6] + (length,))

    cut = e_in.shape[0] // 2
    in_z1 = swap(e_in[:cut], "zh")
    in_z2 = swap(e_in[cut:], "zh")
    in_x = swap(e_in, "x")
    in_zx1 = swap(in_z1, "x")
    small = gather_over(small, ("c", "zl"), (c, zl)).reshape(2, 2, 2, 2, -1)
    small_all = jnp.transpose(small, (3, 0, 2, 1, 4)).reshape(16, n_small * block)
    e_out = exchange(out_weight.reshape(4, inner, block))
    e_out = jnp.moveaxis(e_out, 0, 1).reshape(inner, 4 * block)
    positions = by_place(index) ^ (zh * (8 * tok_dev) + x * (2 * tok_dev))
    ends = jnp.cumsum(lax.dynamic_index_in_dim(doc_lengths, batch, 0, keepdims=False))
    first = jnp.max(jnp.where(ends[:, None] <= positions[None, :], ends[:, None], 0), axis=0)
    span = jnp.stack([first, positions])
    key_place = positions[:, None]
    cosine, sine = rotary_tables(positions)
    lane = jnp.arange(HEAD_DIM)[None, :]
    signed = jnp.where(lane < HEAD_DIM // 2, -sine, sine)
    n_vec = 6 + 2 * GROUPS
    rows_of = jnp.arange(16) ^ (zh * 8 + x * 2)
    pick = (rows_of[:, None] == jnp.arange(16)[None, :]).astype(WIDE)
    small_own = jnp.dot(pick, small_all, precision=HIGHEST)
    vectors_f = small_own[:, : n_vec * block].reshape(2, 2, 2, 2, n_vec, block)
    vectors_f = jnp.transpose(vectors_f, (4, 0, 2, 1, 3, 5)).reshape(n_vec, width)
    router = vectors_f[6:].astype(LOW)
    at = n_vec * block
    size = up_bias.size
    bias_up = small_all[:, at : at + size].reshape((16,) + up_bias.shape)
    bias_up = jnp.moveaxis(bias_up, 0, 1).reshape(4, units)
    bias_up = lax.dynamic_index_in_dim(bias_up, part, 0, keepdims=True)
    at += size
    size = 2 * micro * tok_dev
    widths = small_own[:, at : at + size].reshape(16, 2, micro, tok_dev)
    widths = lax.dynamic_index_in_dim(widths, batch, 2, keepdims=False).astype(jnp.int32)
    widths = jnp.swapaxes(widths, 0, 1).reshape(2, 2, 2, 2, 2, 2, half)
    at += size
    bias_in = small_all[:, at : at + in_bias.size].reshape((16,) + in_bias.shape)
    bias_in = jnp.moveaxis(bias_in, 0, 2).reshape(3, 4, heads, head_dim)
    bias_in = lax.dynamic_index_in_dim(bias_in, part, 1, keepdims=False)
    bias_in = bias_in.reshape(1, 3 * inner)
    heads_row, units_row = by_place(widths)
    head_ids = (y * 4 + part) * heads + jnp.arange(heads, dtype=jnp.int32)
    head_active = (head_ids[:, None] // (HEADS // GROUPS) < heads_row[None, :]).astype(WIDE)
    head_active = head_active[:, :, None]
    unit_group = (y * 4 + part) * units // (FF // GROUPS)
    unit_active = (unit_group < units_row).astype(WIDE)[:, None]
    (
        tokens_all, in_x, in_z1, in_z2, in_zx1, e_out, cotangent, up_weight, down_weight,
        vectors_f, router, bias_in, bias_up, head_active, unit_active,
        cosine, sine, signed, span, key_place,
    ) = tie(
        tokens_all, in_x, in_z1, in_z2, in_zx1, e_out, cotangent, up_weight, down_weight,
        vectors_f, router, bias_in, bias_up, head_active, unit_active,
        cosine, sine, signed, span, key_place,
    )
    gain_one, shift_one, gain_two, shift_two, bias_out, bias_down = (
        vectors_f[i : i + 1] for i in range(6)
    )

    in_zx2 = swap(in_z2, "x")
    out_z = swap(e_out, "zh")
    out_x = swap(e_out, "x")
    e_up = exchange(jnp.moveaxis(up_weight.reshape(block, 4, units), 1, 0))
    e_up = e_up.reshape(4 * block, units)
    cotangent_pieces = to_batch(cotangent)
    normed_low, logits = norm_rows(bits, tokens_all, gain_one, shift_one, router)
    normed_low, in_zx2, out_z, out_x, e_up, down_weight, logits, *cotangent_pieces = tie(
        normed_low, in_zx2, out_z, out_x, e_up, down_weight, logits, *cotangent_pieces
    )
    cotangent_own = jnp.concatenate(cotangent_pieces, axis=0)

    def mine(value):
        return lax.dynamic_slice_in_dim(value, place * own, own, 0)

    cut_units = units // 2
    out_zx = swap(out_z, "x")
    up_x1 = swap(e_up[:, :cut_units], "x")
    up_z1 = swap(e_up[:, :cut_units], "zh")
    e_down = exchange(down_weight.reshape(4, units, block))
    e_down = jnp.moveaxis(e_down, 0, 1).reshape(units, 4 * block)
    w_in = (e_in, in_x, in_z1, in_z2, in_zx1, in_zx2)
    qkv = qkv_rows(normed_low, w_in, bias_in, cosine, signed)
    mixed, lse = attend(qkv, key_place, span, head_active, heads)
    w_out = jnp.concatenate([e_out, out_x, out_z, out_zx], axis=1)
    mixed, w_out, e_up, e_down, up_x1, up_z1, cotangent_own, tokens_own, logits = tie(
        mixed, w_out, e_up, e_down, up_x1, up_z1, cotangent_own, tokens_own, logits
    )

    part_own = own // 2

    def halves(value):
        return (
            lax.dynamic_slice_in_dim(value, c * (length // 2), length // 2, 0),
            lax.dynamic_slice_in_dim(value, (1 - c) * (length // 2), length // 2, 0),
        )

    def group_second(total):
        total = total.reshape(2, 2, own, width)
        a_keep, a_send = keep_and_send(total[:, :, :part_own], zl, 0)
        b_keep, b_send = keep_and_send(total[:, :, part_own:], y, 1)
        a_got = swap(a_send.astype(LOW), "zl")
        b_got = swap(b_send.astype(LOW), "y")
        return a_keep, b_keep, a_got, b_got

    def group_third(a_keep, b_keep, a_got, b_got):
        a_keep, a_send = keep_and_send(a_keep + a_got.astype(WIDE), y, 0)
        b_keep, b_send = keep_and_send(b_keep + b_got.astype(WIDE), zl, 0)
        a_got = swap(a_send.astype(LOW), "y")
        b_got = swap(b_send.astype(LOW), "zl")
        return jnp.concatenate([a_keep + a_got.astype(WIDE), b_keep + b_got.astype(WIDE)], axis=0)

    attn_here, attn_away = halves(mixed)
    attn_away = dot_to(attn_away, w_out, ((1,), (0,))).astype(LOW)
    cotangent_all = lax.all_gather(cotangent_own, GROUP, axis=0, tiled=True)
    attn_away, attn_here, tokens_own, cotangent_own, logits = tie(
        attn_away, attn_here, tokens_own, cotangent_own, logits
    )
    attn_got = swap(attn_away, "c")
    up_x2 = swap(e_up[:, cut_units:], "x")
    up_z2 = swap(e_up[:, cut_units:], "zh")
    up_zx1 = swap(up_z1, "x")
    options = jnp.arange(GROUPS, dtype=jnp.int32)
    attn_prob = jax.nn.softmax(logits[:, :GROUPS], axis=-1)
    ffn_prob = jax.nn.softmax(logits[:, GROUPS:], axis=-1)
    attn_pick = (options[None, :] == heads_row[:, None] - 1).astype(WIDE)
    ffn_pick = (options[None, :] == units_row[:, None] - 1).astype(WIDE)
    attn_gate = GROUPS * jnp.sum(attn_prob * attn_pick, axis=-1, keepdims=True)
    ffn_gate = GROUPS * jnp.sum(ffn_prob * ffn_pick, axis=-1, keepdims=True)
    attn_total = dot_to(attn_here, w_out, ((1,), (0,))) + attn_got.astype(WIDE)
    attn_total, attn_gate, ffn_gate, tokens_own, cotangent_own = tie(
        attn_total, attn_gate, ffn_gate, tokens_own, cotangent_own
    )
    attn_parts = group_second(attn_total)
    rows, upstream = own_rows(bits, tokens_own, cotangent_own)
    *attn_parts, rows, upstream, up_x2 = tie(*attn_parts, rows, upstream, up_x2)
    attn_sum = group_third(*attn_parts)
    down_x1 = swap(e_down[:cut_units], "x")
    attn_sum, cotangent_all, up_z2, up_zx1, down_x1, e_down = tie(
        attn_sum, cotangent_all, up_z2, up_zx1, down_x1, e_down
    )

    attn_branch = attn_sum + bias_out
    attn_gate_own = mine(attn_gate)
    ffn_gate_own = mine(ffn_gate)
    resid = rows + attn_gate_own * attn_branch
    normed_two, scaled_two, inverse_two = norm_forward(resid, gain_two, shift_two)
    normed_two_low = normed_two.astype(LOW)
    normed_two_low, e_down, cotangent_all, up_z2 = tie(
        normed_two_low, e_down, cotangent_all, up_z2
    )
    normed_two_low = lax.all_gather(normed_two_low, GROUP, axis=0, tiled=True)
    down_z1 = swap(e_down[:cut_units], "zh")
    up_zx2 = swap(up_z2, "x")
    down_x2 = swap(e_down[cut_units:], "x")
    down_grad = gate_rows(bits, cotangent_all, ffn_gate)
    down_grad, down_z1, up_zx2, down_x2, e_down = tie(
        down_grad, down_z1, up_zx2, down_x2, e_down
    )
    down_z2 = swap(e_down[cut_units:], "zh")
    down_zx1 = swap(down_z1, "x")
    normed_two_low, down_z2, down_zx1 = tie(normed_two_low, down_z2, down_zx1)

    def columns(value, k):
        return value[:, k * 4 * block : (k + 1) * 4 * block]

    down_zx2 = swap(down_z2, "x")
    w_up = (
        (e_up[:, :cut_units], up_x1, up_z1, up_zx1),
        (e_up[:, cut_units:], up_x2, up_z2, up_zx2),
    )
    relu_part, hidden = hidden_rows(normed_two_low, unit_active, bias_up, w_up)
    relu_part, hidden, down_zx2 = tie(relu_part, hidden, down_zx2)
    w_down = (
        (e_down[:cut_units], down_x1, down_z1, down_zx1),
        (e_down[cut_units:], down_x2, down_z2, down_zx2),
    )
    up_grad, two_part = ffn_rows(core, down_grad, relu_part, w_down, w_up)
    two_away, two_here = two_part[: length // 2], two_part[length // 2 :]
    two_got = swap(two_away, "c")

    def down_piece(k):
        return dot_to(hidden, columns(down_grad, k), ((0,), (0,)))

    def up_piece(k):
        return dot_to(columns(normed_two_low, k), up_grad, ((0,), (0,)))

    down_send3 = down_piece(3).astype(LOW)
    down_got3 = swap(down_send3, "x")
    two_total = two_here.astype(WIDE) + two_got.astype(WIDE)
    two_total, hidden, up_grad, down_send3 = tie(two_total, hidden, up_grad, down_send3)
    two_parts = group_second(two_total)
    up_send3 = up_piece(3).astype(LOW)
    down_send1 = down_piece(1).astype(LOW)
    *two_parts, down_got3, down_send1, up_send3, up_grad = tie(
        *two_parts, down_got3, down_send1, up_send3, up_grad
    )
    normed_two_grad = group_third(*two_parts)
    up_got3 = swap(up_send3, "x")
    down_send2 = (down_piece(2) + down_got3.astype(WIDE)).astype(LOW)
    normed_two_grad, down_send2, hidden, down_grad, up_grad = tie(
        normed_two_grad, down_send2, hidden, down_grad, up_grad
    )

    resid_grad = upstream + norm_backward(normed_two_grad, scaled_two, inverse_two, gain_two)
    gated_attn = attn_gate_own * resid_grad
    gated_low = gated_attn.astype(LOW)
    gated_low, hidden, down_grad, up_grad, normed_two_grad, resid_grad, down_send2 = tie(
        gated_low, hidden, down_grad, up_grad, normed_two_grad, resid_grad, down_send2
    )
    attn_out_grad = lax.all_gather(gated_low, GROUP, axis=0, tiled=True)
    down_far1 = swap(down_send2[:cut_units], "zh")
    down_got1 = swap(down_send1, "x")
    w_in = jnp.concatenate(w_in, axis=0)
    ffn_part = wide_rows(hidden, w_down)
    grad_gain_two = jnp.sum(normed_two_grad * scaled_two, axis=0)
    grad_shift_two = jnp.sum(normed_two_grad, axis=0)
    attn_gate_grad = jnp.sum(resid_grad * attn_branch, axis=-1)
    grad_out_bias = jnp.sum(attn_gate_own * resid_grad, axis=0)
    up_send1 = up_piece(1).astype(LOW)
    up_send2 = (up_piece(2) + up_got3.astype(WIDE)).astype(LOW)
    (
        attn_out_grad, ffn_part, up_send1, up_send2, grad_out_bias, grad_gain_two, w_in,
        down_far1, down_send2,
    ) = tie(
        attn_out_grad, ffn_part, up_send1, up_send2, grad_out_bias, grad_gain_two, w_in,
        down_far1, down_send2,
    )
    down_far2 = swap(down_send2[cut_units:], "zh")

    def out_piece(k):
        return dot_to(mixed, columns(attn_out_grad, k), ((0,), (0,)))

    ffn_sum = lax.psum_scatter(ffn_part, GROUP, scatter_dimension=0, tiled=True)
    out_got = swap(jnp.stack([out_piece(1), out_piece(3)]).astype(LOW), "x")
    proj_grad = attend_back(
        qkv, attn_out_grad, w_out, head_active, lse, key_place, span, cosine, sine, heads
    )
    proj_grad, attn_out_grad, down_got1, down_far2, hidden, up_send1, up_send2, out_got = tie(
        proj_grad, attn_out_grad, down_got1, down_far2, hidden, up_send1, up_send2, out_got
    )

    def in_piece(k):
        return dot_to(columns(normed_low, k), proj_grad, ((0,), (0,)))

    one_here, one_away = halves(proj_grad)
    one_away = dot_to(one_away, w_in, ((1,), (1,))).astype(LOW)
    one_away, one_here, proj_grad, hidden, out_got, up_send2 = tie(
        one_away, one_here, proj_grad, hidden, out_got, up_send2
    )
    one_got = swap(one_away, "c")
    up_far = swap(up_send2, "zh")
    in_send3 = in_piece(3).astype(LOW)
    in_got3 = swap(in_send3, "x")
    one_total = dot_to(one_here, w_in, ((1,), (1,))) + one_got.astype(WIDE)
    one_total, proj_grad, in_send3, out_got, up_send1, hidden = tie(
        one_total, proj_grad, in_send3, out_got, up_send1, hidden
    )
    one_parts = group_second(one_total)
    in_send1 = in_piece(1).astype(LOW)
    out_send2 = (out_piece(2) + out_got[1].astype(WIDE)).astype(LOW)
    *one_parts, in_send1, out_send2, in_got3, ffn_sum, up_send1, hidden = tie(
        *one_parts, in_send1, out_send2, in_got3, ffn_sum, up_send1, hidden
    )
    normed_sum = group_third(*one_parts)
    in_got1 = swap(in_send1, "x")
    up_got1 = swap(up_send1, "x")
    out_far = swap(out_send2, "zh")
    in_send2 = (in_piece(2) + in_got3.astype(WIDE)).astype(LOW)
    ffn_branch = ffn_sum.astype(WIDE) + bias_down
    ffn_gate_grad = jnp.sum(upstream * ffn_branch, axis=-1)
    logit_grad = jnp.concatenate(
        [
            gate_logit_grad(mine(attn_prob), mine(attn_pick), attn_gate_grad),
            gate_logit_grad(mine(ffn_prob), mine(ffn_pick), ffn_gate_grad),
        ],
        axis=-1,
    )
    router_part = jnp.dot(logit_grad, vectors_f[6:], precision=HIGHEST)

    def both_halves(value, other):
        def batches(v):
            v = v.reshape(2, 2, half, width)
            return flip_where(x, flip_where(zh, v, 0), 1).reshape(4, half, width)

        value, other = batches(value), batches(other)
        return jnp.where(
            y == 0,
            jnp.concatenate([value, other], axis=1),
            jnp.concatenate([other, value], axis=1),
        )

    def spread(rows, cut):
        rows = from_own_order(rows, zh, x)
        return jnp.swapaxes(rows.reshape(cut, 16, block), 0, 1).reshape(16, cut * block)

    normed_sum, in_send2, router_part, ffn_branch, logit_grad, up_far, hidden = tie(
        normed_sum, in_send2, router_part, ffn_branch, logit_grad, up_far, hidden
    )

    in_far = swap(in_send2, "zh")
    tokens_low, last = first_back(bits, normed_sum, router_part, rows, resid_grad, gain_one)
    tokens_low = tokens_low.reshape(4, half, width)
    tokens_low, last, ffn_branch, logit_grad, up_grad, out_far, up_far, hidden = tie(
        tokens_low, last, ffn_branch, logit_grad, up_grad, out_far, up_far, hidden
    )
    tokens_pieces = across([tokens_low[k] for k in range(4)])
    block_low = home_rows(bits, resid + ffn_gate_own * ffn_branch).reshape(4, half, width)
    normed_own = mine(normed_low)
    grad_router = jnp.dot(logit_grad.T, normed_own.astype(WIDE), precision=HIGHEST)
    grad_down_bias = jnp.sum(ffn_gate_own * upstream, axis=0)
    grad_up_bias = jnp.sum(up_grad.astype(WIDE), axis=0)
    grad_in_bias = jnp.sum(proj_grad.astype(WIDE), axis=0).reshape(3, heads, head_dim)
    sums = jnp.stack([grad_out_bias, grad_gain_two, grad_shift_two, grad_down_bias])
    sums = spread(jnp.concatenate([last, sums, grad_router], axis=0), n_vec)
    chosen = (jnp.arange(4) == part).astype(WIDE)
    spread_in = (grad_in_bias[:, None] * chosen[None, :, None, None]).reshape(
        3, tp_heads, 16, head_dim // 16
    )
    spread_in = jnp.moveaxis(spread_in, 2, 0).reshape(16, -1)
    spread_up = (grad_up_bias[None, :] * chosen[:, None]).reshape(up_bias.shape[0], 16, block)
    spread_up = jnp.moveaxis(spread_up, 1, 0).reshape(16, -1)
    total = jnp.concatenate([sums, spread_in, spread_up], axis=1)
    down_far = jnp.concatenate([down_far1, down_far2], axis=0)
    down_home = (down_piece(0) + down_got1.astype(WIDE) + down_far.astype(WIDE)).astype(LOW)
    down_home = exchange(jnp.moveaxis(down_home.reshape(units, 4, block), 1, 0))
    up_home = (up_piece(0) + up_got1.astype(WIDE) + up_far.astype(WIDE)).astype(LOW)
    up_home = exchange(up_home.reshape(4, block, units))
    out_home = (out_piece(0) + out_got[0].astype(WIDE) + out_far.astype(WIDE)).astype(LOW)
    *tokens_pieces, total, block_low, up_home, out_home, in_got1, down_home, in_far = tie(
        *tokens_pieces, total, block_low, up_home, out_home, in_got1, down_home, in_far
    )
    total = reduce_rows(total, zh, zl, x, c)
    tokens_grad = jnp.stack(tokens_pieces)
    tokens_other = swap(tokens_grad, "y")
    block_out = jnp.stack(across([block_low[k] for k in range(4)]))
    out_home = exchange(jnp.moveaxis(out_home.reshape(inner, 4, block), 1, 0))
    in_home = (in_piece(0) + in_got1.astype(WIDE) + in_far.astype(WIDE)).astype(LOW)
    tokens_other, block_out, in_home, out_home, total = tie(
        tokens_other, block_out, in_home, out_home, total
    )
    block_other = swap(block_out, "y")
    in_home = exchange(in_home.reshape(4, block, 3 * inner)).reshape(4, block, 3, heads, head_dim)
    at = n_vec * block
    shared = total[:at]
    shared = (shared + swap(shared, "y")).reshape(n_vec, block)
    early = total[at:]
    return (
        both_halves(block_out, block_other),
        both_halves(tokens_grad, tokens_other).astype(WIDE),
        shared[0],
        shared[1],
        shared[6:],
        jnp.transpose(in_home, (1, 2, 0, 3, 4)).reshape(in_weight.shape).astype(WIDE),
        early[: in_bias.size].reshape(in_bias.shape),
        out_home.reshape(out_weight.shape).astype(WIDE),
        shared[2],
        shared[3],
        shared[4],
        jnp.swapaxes(up_home, 0, 1).reshape(up_weight.shape).astype(WIDE),
        early[in_bias.size :].reshape(up_bias.shape),
        down_home.reshape(down_weight.shape).astype(WIDE),
        shared[5],
    )


def solution(mesh):
    body, seq, tp = local, "seq", "tp"
    if mesh.shape["seq"] == 16 and mesh.shape["tp"] == 2:
        mesh = Mesh(mesh.devices.reshape(2, 2, 2, 2, 2), ROWS + ("y",))
        body, seq, tp = grouped, ROWS, "y"
    return jax.shard_map(
        body,
        mesh=mesh,
        in_specs=(
            P(None, seq, None),
            P(None, seq, None),
            P(None, seq),
            P(None, seq),
            P(),
            P(seq),
            P(seq),
            P(None, seq),
            P(seq, None, tp, None),
            P(None, tp, seq),
            P(tp, None, seq),
            P(seq),
            P(seq),
            P(seq),
            P(seq, tp),
            P(tp, seq),
            P(tp, seq),
            P(seq),
        ),
        out_specs=(
            P(None, seq, None),
            P(None, seq, None),
            P(seq),
            P(seq),
            P(None, seq),
            P(seq, None, tp, None),
            P(None, tp, seq),
            P(tp, None, seq),
            P(seq),
            P(seq),
            P(seq),
            P(seq, tp),
            P(tp, seq),
            P(tp, seq),
            P(seq),
        ),
        check_vma=False,
    )
```

```python
import functools
import math

import jax
import jax.numpy as jnp
from jax import lax
from jax.experimental import pallas as pl
from jax.experimental.pallas import tpu as pltpu
from jax.sharding import Mesh
from jax.sharding import PartitionSpec as P

HEADS = 16
HEAD_DIM = 128
FF = 8192
GROUPS = 4


EPSILON = 1e-05
HIGHEST = lax.Precision.HIGHEST


def norm_forward(rows, gain, shift):
    center = rows - jnp.mean(rows, axis=-1, keepdims=True)
    inverse = lax.rsqrt(jnp.mean(center * center, axis=-1, keepdims=True) + EPSILON)
    scaled = center * inverse
    return (scaled * gain + shift, scaled, inverse)


def norm_backward(upstream, scaled, inverse, gain):
    through = upstream * gain
    return inverse * (
        through
        - jnp.mean(through, axis=-1, keepdims=True)
        - scaled * jnp.mean(through * scaled, axis=-1, keepdims=True)
    )


def rotary_tables(positions):
    half_dim = HEAD_DIM // 2
    steps_up = jnp.arange(half_dim, dtype=jnp.float32) * (2.0 / HEAD_DIM)
    inverse = jnp.exp(-math.log(10000.0) * steps_up)
    angles = positions.astype(jnp.float32)[:, None] * inverse[None, :]
    angles = jnp.concatenate([angles, angles], axis=1)
    return (jnp.cos(angles), jnp.sin(angles))


def rotate(vectors, cosine, sine):
    half_dim = vectors.shape[-1] // 2
    turned = jnp.concatenate([-vectors[..., half_dim:], vectors[..., :half_dim]], axis=-1)
    return vectors * cosine[:, None, :] + turned * sine[:, None, :]


def rotate_back(grads, cosine, sine):
    half_dim = grads.shape[-1] // 2
    moved = grads * sine[:, None, :]
    turned = jnp.concatenate([moved[..., half_dim:], -moved[..., :half_dim]], axis=-1)
    return grads * cosine[:, None, :] + turned


def doc_index(lengths, positions):
    ends = jnp.cumsum(lengths)
    return jnp.sum((positions[:, None] >= ends[None, :]).astype(jnp.int32), axis=1)


def gate_logit_grad(prob, pick, gate_grad):
    chosen = jnp.sum(prob * pick, axis=-1, keepdims=True)
    return GROUPS * chosen * (pick - prob) * gate_grad[:, None]


def local(
    tokens,
    cotangent,
    head_groups,
    ffn_widths,
    doc_lengths,
    first_gain,
    first_shift,
    router_weight,
    in_weight,
    in_bias,
    out_weight,
    out_bias,
    second_gain,
    second_shift,
    up_weight,
    up_bias,
    down_weight,
    down_bias,
):
    seq_count = lax.axis_size("seq")
    seq_index = lax.axis_index("seq")
    tp_index = lax.axis_index("tp")
    gathered = (
        lax.all_gather(first_gain, "seq", axis=0, tiled=True),
        lax.all_gather(first_shift, "seq", axis=0, tiled=True),
        lax.all_gather(router_weight, "seq", axis=1, tiled=True),
        lax.all_gather(in_weight, "seq", axis=0, tiled=True),
        lax.all_gather(in_bias, "seq", axis=2, tiled=True),
        lax.all_gather(out_weight, "seq", axis=2, tiled=True),
        lax.all_gather(out_bias, "seq", axis=0, tiled=True),
        lax.all_gather(second_gain, "seq", axis=0, tiled=True),
        lax.all_gather(second_shift, "seq", axis=0, tiled=True),
        lax.all_gather(up_weight, "seq", axis=0, tiled=True),
        lax.all_gather(up_bias, "seq", axis=1, tiled=True),
        lax.all_gather(down_weight, "seq", axis=1, tiled=True),
        lax.all_gather(down_bias, "seq", axis=0, tiled=True),
    )
    (
        gain_one,
        shift_one,
        router_full,
        in_full,
        in_bias_full,
        out_full,
        out_bias_full,
        gain_two,
        shift_two,
        up_full,
        up_bias_full,
        down_full,
        down_bias_full,
    ) = gathered
    micro, tok_dev, width = tokens.shape
    local_heads = in_full.shape[2]
    head_dim = in_full.shape[3]
    inner = local_heads * head_dim
    local_units = up_full.shape[1]
    length = tok_dev * seq_count
    scale = HEAD_DIM ** (-0.5)
    gain_one_f = gain_one.astype(jnp.float32)
    shift_one_f = shift_one.astype(jnp.float32)
    gain_two_f = gain_two.astype(jnp.float32)
    shift_two_f = shift_two.astype(jnp.float32)
    out_bias_f = out_bias_full.astype(jnp.float32)
    down_bias_f = down_bias_full.astype(jnp.float32)
    router_wide = router_full.astype(jnp.float32)
    bias_in = in_bias_full.astype(jnp.float32)
    up_bias_vec = up_bias_full.reshape(local_units).astype(jnp.float32)
    in_matrix = in_full.reshape(width, 3 * inner)
    out_matrix = out_full.reshape(inner, width)
    positions_all = jnp.arange(length, dtype=jnp.int32)
    positions_local = seq_index * tok_dev + jnp.arange(tok_dev, dtype=jnp.int32)
    cosine, sine = rotary_tables(positions_local)
    head_ids = tp_index * local_heads + jnp.arange(local_heads, dtype=jnp.int32)
    unit_ids = tp_index * local_units + jnp.arange(local_units, dtype=jnp.int32)
    options = jnp.arange(GROUPS, dtype=jnp.int32)
    grad_gain_one = jnp.zeros((width,), jnp.float32)
    grad_shift_one = jnp.zeros((width,), jnp.float32)
    grad_router = jnp.zeros(router_full.shape, jnp.float32)
    grad_in = jnp.zeros((width, 3 * inner), jnp.float32)
    grad_in_bias = jnp.zeros(in_bias_full.shape, jnp.float32)
    grad_out = jnp.zeros((inner, width), jnp.float32)
    grad_out_bias = jnp.zeros((width,), jnp.float32)
    grad_gain_two = jnp.zeros((width,), jnp.float32)
    grad_shift_two = jnp.zeros((width,), jnp.float32)
    grad_up = jnp.zeros(up_full.shape, jnp.float32)
    grad_up_bias = jnp.zeros((local_units,), jnp.float32)
    grad_down = jnp.zeros(down_full.shape, jnp.float32)
    grad_down_bias = jnp.zeros((width,), jnp.float32)
    outputs = []
    input_grads = []
    for batch in range(micro):
        rows = tokens[batch].astype(jnp.float32)
        doc_all = doc_index(doc_lengths[batch], positions_all)
        doc_local = lax.dynamic_slice_in_dim(doc_all, seq_index * tok_dev, tok_dev, 0)
        allowed = (positions_all[None, :] <= positions_local[:, None]) & (
            doc_all[None, :] == doc_local[:, None]
        )
        head_active = (head_ids[None, :] // (HEADS // GROUPS) < head_groups[batch][:, None]).astype(
            jnp.float32
        )
        unit_active = (unit_ids[None, :] // (FF // GROUPS) < ffn_widths[batch][:, None]).astype(
            jnp.float32
        )
        normed, scaled_one, inverse_one = norm_forward(rows, gain_one_f, shift_one_f)
        normed_low = normed.astype(jnp.bfloat16)
        logits = jnp.dot(normed_low, router_full.T, preferred_element_type=jnp.float32)
        attn_prob = jax.nn.softmax(logits[:, :GROUPS], axis=-1)
        ffn_prob = jax.nn.softmax(logits[:, GROUPS:], axis=-1)
        attn_pick = (options[None, :] == head_groups[batch][:, None] - 1).astype(jnp.float32)
        ffn_pick = (options[None, :] == ffn_widths[batch][:, None] - 1).astype(jnp.float32)
        attn_gate = GROUPS * jnp.sum(attn_prob * attn_pick, axis=-1)
        ffn_gate = GROUPS * jnp.sum(ffn_prob * ffn_pick, axis=-1)
        projected = jnp.dot(normed_low, in_matrix, preferred_element_type=jnp.float32)
        projected = projected.reshape(tok_dev, 3, local_heads, head_dim) + bias_in
        queries = rotate(projected[:, 0], cosine, sine).astype(jnp.bfloat16)
        keys_low = rotate(projected[:, 1], cosine, sine).astype(jnp.bfloat16)
        values_low = projected[:, 2].astype(jnp.bfloat16)
        keys_all, values_all = (
            lax.all_gather(keys_low, "seq", axis=0, tiled=True),
            lax.all_gather(values_low, "seq", axis=0, tiled=True),
        )
        raw_scores = jnp.einsum(
            "qhd,khd->hqk", queries, keys_all, preferred_element_type=jnp.float32
        )
        scores = jnp.where(allowed[None], raw_scores * scale, -jnp.inf)
        row_max = jnp.max(scores, axis=-1, keepdims=True)
        weights = jnp.exp(scores - row_max)
        row_total = jnp.sum(weights, axis=-1, keepdims=True)
        log_total = row_max + jnp.log(row_total)
        probs = weights / row_total
        attended = jnp.einsum(
            "hqk,khd->qhd",
            probs.astype(jnp.bfloat16),
            values_all,
            preferred_element_type=jnp.float32,
        )
        mixed_heads = (attended * head_active[:, :, None]).astype(jnp.bfloat16)
        mixed_flat = mixed_heads.reshape(tok_dev, inner)
        attn_part = jnp.dot(mixed_flat, out_matrix, preferred_element_type=jnp.float32)
        attn_sum = lax.psum(attn_part, "tp")
        attn_branch = attn_sum + out_bias_f
        resid = rows + attn_gate[:, None] * attn_branch
        normed_two, scaled_two, inverse_two = norm_forward(resid, gain_two_f, shift_two_f)
        normed_two_low = normed_two.astype(jnp.bfloat16)
        up_pre = jnp.dot(normed_two_low, up_full, preferred_element_type=jnp.float32) + up_bias_vec
        relu_part = jnp.maximum(up_pre, 0.0)
        hidden = (unit_active * jnp.square(relu_part)).astype(jnp.bfloat16)
        down_part = jnp.dot(hidden, down_full, preferred_element_type=jnp.float32)
        down_sum = lax.psum(down_part.astype(jnp.bfloat16), "tp").astype(jnp.float32)
        ffn_branch = down_sum + down_bias_f
        outputs.append((resid + ffn_gate[:, None] * ffn_branch).astype(jnp.bfloat16))
        upstream = cotangent[batch].astype(jnp.float32)
        ffn_gate_grad = jnp.sum(upstream * ffn_branch, axis=-1)
        gated_up = ffn_gate[:, None] * upstream
        grad_down_bias = grad_down_bias + jnp.sum(gated_up, axis=0)
        down_grad = gated_up.astype(jnp.bfloat16)
        grad_down = grad_down + jnp.einsum(
            "tf,td->fd", hidden, down_grad, preferred_element_type=jnp.float32
        )
        hidden_grad = jnp.einsum(
            "td,fd->tf", down_grad, down_full, preferred_element_type=jnp.float32
        )
        up_grad = (hidden_grad * unit_active * 2.0 * relu_part).astype(jnp.bfloat16)
        grad_up_bias = grad_up_bias + jnp.sum(up_grad.astype(jnp.float32), axis=0)
        grad_up = grad_up + jnp.einsum(
            "td,tf->df", normed_two_low, up_grad, preferred_element_type=jnp.float32
        )
        normed_two_part = jnp.einsum(
            "tf,df->td", up_grad, up_full, preferred_element_type=jnp.float32
        )
        normed_two_grad = lax.psum(normed_two_part, "tp")
        grad_gain_two = grad_gain_two + jnp.sum(normed_two_grad * scaled_two, axis=0)
        grad_shift_two = grad_shift_two + jnp.sum(normed_two_grad, axis=0)
        resid_grad = upstream + norm_backward(normed_two_grad, scaled_two, inverse_two, gain_two_f)
        attn_gate_grad = jnp.sum(resid_grad * attn_branch, axis=-1)
        gated_attn = attn_gate[:, None] * resid_grad
        grad_out_bias = grad_out_bias + jnp.sum(gated_attn, axis=0)
        attn_out_grad = gated_attn.astype(jnp.bfloat16)
        grad_out = grad_out + jnp.einsum(
            "ti,td->id", mixed_flat, attn_out_grad, preferred_element_type=jnp.float32
        )
        mixed_grad = jnp.einsum(
            "td,id->ti", attn_out_grad, out_matrix, preferred_element_type=jnp.float32
        )
        attended_grad = (
            mixed_grad.reshape(tok_dev, local_heads, head_dim) * head_active[:, :, None]
        ).astype(jnp.bfloat16)
        again_raw = jnp.einsum(
            "qhd,khd->hqk", queries, keys_all, preferred_element_type=jnp.float32
        )
        again_scores = jnp.where(allowed[None], again_raw * scale, -jnp.inf)
        probs_again = jnp.exp(again_scores - log_total)
        prob_grad = jnp.einsum(
            "qhd,khd->hqk", attended_grad, values_all, preferred_element_type=jnp.float32
        )
        row_dot = jnp.sum(probs_again * prob_grad, axis=-1, keepdims=True)
        score_grad = (probs_again * (prob_grad - row_dot) * scale).astype(jnp.bfloat16)
        query_rot_grad = jnp.einsum(
            "hqk,khd->qhd", score_grad, keys_all, preferred_element_type=jnp.float32
        )
        probs_low = probs_again.astype(jnp.bfloat16)
        key_part = jnp.einsum(
            "hqk,qhd->khd", score_grad, queries, preferred_element_type=jnp.float32
        )
        value_part = jnp.einsum(
            "hqk,qhd->khd", probs_low, attended_grad, preferred_element_type=jnp.float32
        )
        combined = lax.psum_scatter(
            jnp.concatenate([key_part, value_part], axis=1).reshape(
                lax.axis_size("seq") * tok_dev, 2 * inner
            ),
            "seq",
            scatter_dimension=0,
            tiled=True,
        )
        combined = combined.reshape(tok_dev, 2 * local_heads, head_dim)
        key_rot_grad = combined[:, :local_heads]
        value_grad = combined[:, local_heads:]
        query_grad = rotate_back(query_rot_grad, cosine, sine)
        key_grad = rotate_back(key_rot_grad, cosine, sine)
        proj_grad = jnp.stack([query_grad, key_grad, value_grad], axis=1).astype(jnp.bfloat16)
        grad_in_bias = grad_in_bias + jnp.sum(proj_grad.astype(jnp.float32), axis=0)
        proj_flat = proj_grad.reshape(tok_dev, 3 * inner)
        grad_in = grad_in + jnp.einsum(
            "tw,tc->wc", normed_low, proj_flat, preferred_element_type=jnp.float32
        )
        normed_part = jnp.einsum(
            "tc,wc->tw", proj_flat, in_matrix, preferred_element_type=jnp.float32
        )
        logit_grad = jnp.concatenate(
            [
                gate_logit_grad(attn_prob, attn_pick, attn_gate_grad),
                gate_logit_grad(ffn_prob, ffn_pick, ffn_gate_grad),
            ],
            axis=-1,
        )
        grad_router = grad_router + jnp.dot(
            logit_grad.T, normed_low.astype(jnp.float32), precision=HIGHEST
        )
        router_part = jnp.dot(logit_grad, router_wide, precision=HIGHEST)
        normed_grad = lax.psum(normed_part, "tp") + router_part
        grad_gain_one = grad_gain_one + jnp.sum(normed_grad * scaled_one, axis=0)
        grad_shift_one = grad_shift_one + jnp.sum(normed_grad, axis=0)
        input_grads.append(
            resid_grad + norm_backward(normed_grad, scaled_one, inverse_one, gain_one_f)
        )
    reduced = (
        lax.psum_scatter(grad_gain_one, "seq", scatter_dimension=0, tiled=True),
        lax.psum_scatter(grad_shift_one, "seq", scatter_dimension=0, tiled=True),
        lax.psum_scatter(grad_router, "seq", scatter_dimension=1, tiled=True),
        lax.psum_scatter(
            grad_in.reshape(width, 3, local_heads, head_dim), "seq", scatter_dimension=0, tiled=True
        ),
        lax.psum_scatter(grad_in_bias, "seq", scatter_dimension=2, tiled=True),
        lax.psum_scatter(
            grad_out.reshape(local_heads, head_dim, width), "seq", scatter_dimension=2, tiled=True
        ),
        lax.psum_scatter(grad_out_bias, "seq", scatter_dimension=0, tiled=True),
        lax.psum_scatter(grad_gain_two, "seq", scatter_dimension=0, tiled=True),
        lax.psum_scatter(grad_shift_two, "seq", scatter_dimension=0, tiled=True),
        lax.psum_scatter(grad_up, "seq", scatter_dimension=0, tiled=True),
        lax.psum_scatter(
            grad_up_bias.reshape(up_bias_full.shape), "seq", scatter_dimension=1, tiled=True
        ),
        lax.psum_scatter(grad_down, "seq", scatter_dimension=1, tiled=True),
        lax.psum_scatter(grad_down_bias, "seq", scatter_dimension=0, tiled=True),
    )
    return (
        jnp.stack(outputs),
        jnp.stack(input_grads),
        reduced[0],
        reduced[1],
        reduced[2],
        reduced[3],
        reduced[4],
        reduced[5],
        reduced[6],
        reduced[7],
        reduced[8],
        reduced[9],
        reduced[10],
        reduced[11],
        reduced[12],
    )


ROWS = ("zh", "zl", "x", "c")
GROUP = ("c", "zl", "y")
PARTS = ("zh", "x")
LOW = jnp.bfloat16
WIDE = jnp.float32


def swap(value, axis):
    return lax.ppermute(value, axis, [(0, 1), (1, 0)])


def flip_where(bit, value, axis):
    return jnp.where(bit == 1, jnp.flip(value, axis), value)


def to_own_order(value, zh, x):
    lead, width = value.shape[:-1], value.shape[-1]
    value = value.reshape(lead + (2, 2, 2, 2, width // 16))
    value = jnp.swapaxes(value, -4, -3)
    value = flip_where(zh, value, -5)
    value = flip_where(x, value, -4)
    return value.reshape(lead + (width,))


def from_own_order(value, zh, x):
    lead, width = value.shape[:-1], value.shape[-1]
    value = value.reshape(lead + (2, 2, 2, 2, width // 16))
    value = flip_where(zh, value, -5)
    value = flip_where(x, value, -4)
    value = jnp.swapaxes(value, -4, -3)
    return value.reshape(lead + (width,))


def tie(*values):
    return lax.optimization_barrier(values)


def dot_to(left, right, dims):
    return lax.dot_general(left, right, (dims, ((), ())), preferred_element_type=WIDE)


def gather_over(value, axes, bits):
    for axis, bit in zip(axes, bits):
        other = swap(value, axis)
        value = jnp.where(
            bit == 0,
            jnp.concatenate([value, other], axis=0),
            jnp.concatenate([other, value], axis=0),
        )
    return value


def reduce_rows(value, zh, zl, x, c):
    value = value.reshape(2, 2, 2, 2, -1)
    for axis, at, bit in (("c", 3, c), ("zl", 1, zl), ("x", 1, x), ("zh", 0, zh)):
        keep = lax.dynamic_index_in_dim(value, bit, at, keepdims=False)
        send = lax.dynamic_index_in_dim(value, 1 - bit, at, keepdims=False)
        value = keep + swap(send, axis)
    return value


BLOCK_Q = 256
BLOCK_A = 512
NEVER = -1e30


def chunks(bits_ref, width):
    run = width // 8
    for at in range(8):
        zh, x, zl = at // 4, at // 2 % 2, at % 2
        theirs = ((zh ^ bits_ref[0]) * 2 + zl) * 2 + (x ^ bits_ref[1])
        yield at * run, pl.multiple_of(theirs * run, run)


def norm_kernel(bits_ref, x_ref, gain_ref, shift_ref, router_ref, out_ref, logits_ref):
    width = x_ref.shape[1]
    rows = x_ref[...].astype(WIDE)
    mean = jnp.mean(rows, axis=-1, keepdims=True)
    center = rows - mean
    inverse = lax.rsqrt(jnp.mean(center * center, axis=-1, keepdims=True) + EPSILON)
    logits = None
    for mine, theirs in chunks(bits_ref, width):
        at = slice(mine, mine + width // 8)
        part = (x_ref[:, pl.ds(theirs, width // 8)].astype(WIDE) - mean) * inverse
        low = (part * gain_ref[:, at] + shift_ref[:, at]).astype(LOW)
        out_ref[:, at] = low
        got = dot_to(low, router_ref[:, at], ((1,), (1,)))
        logits = got if logits is None else logits + got
    logits_ref[...] = logits


def norm_rows(bits, rows, gain, shift, router):
    length, width = rows.shape
    n = router.shape[0]
    return pl.pallas_call(
        norm_kernel,
        grid_spec=pltpu.PrefetchScalarGridSpec(
            num_scalar_prefetch=1,
            grid=(length // BLOCK_Q,),
            in_specs=[
                pl.BlockSpec((BLOCK_Q, width), lambda i, bits: (i, 0)),
                pl.BlockSpec((1, width), lambda i, bits: (0, 0)),
                pl.BlockSpec((1, width), lambda i, bits: (0, 0)),
                pl.BlockSpec((n, width), lambda i, bits: (0, 0)),
            ],
            out_specs=[
                pl.BlockSpec((BLOCK_Q, width), lambda i, bits: (i, 0)),
                pl.BlockSpec((BLOCK_Q, n), lambda i, bits: (i, 0)),
            ],
        ),
        out_shape=[
            jax.ShapeDtypeStruct((length, width), LOW),
            jax.ShapeDtypeStruct((length, n), WIDE),
        ],
        name="norm_rows",
    )(bits, rows, gain, shift, router)


def gate_kernel(bits_ref, x_ref, gate_ref, out_ref):
    width = x_ref.shape[1]
    gate = gate_ref[...]
    for mine, theirs in chunks(bits_ref, width):
        part = x_ref[:, pl.ds(theirs, width // 8)].astype(WIDE) * gate
        out_ref[:, mine : mine + width // 8] = part.astype(LOW)


def gate_rows(bits, rows, gate):
    length, width = rows.shape
    return pl.pallas_call(
        gate_kernel,
        grid_spec=pltpu.PrefetchScalarGridSpec(
            num_scalar_prefetch=1,
            grid=(length // BLOCK_Q,),
            in_specs=[
                pl.BlockSpec((BLOCK_Q, width), lambda i, bits: (i, 0)),
                pl.BlockSpec((BLOCK_Q, 1), lambda i, bits: (i, 0)),
            ],
            out_specs=pl.BlockSpec((BLOCK_Q, width), lambda i, bits: (i, 0)),
        ),
        out_shape=jax.ShapeDtypeStruct((length, width), LOW),
        name="gate_rows",
    )(bits, rows, gate)


def add_dots(left_ref, pieces, start=None):
    at, total = 0, start
    for piece in pieces:
        n = piece.shape[0]
        part = dot_to(left_ref[:, at : at + n], piece[...], ((1,), (0,)))
        total = part if total is None else total + part
        at += n
    return total


def row_spec(steps, rows, width):
    half = steps // 2
    return pl.BlockSpec((rows, width), lambda i, bit: ((i + (1 - bit[0]) * half) % steps, 0))


def fixed(value):
    return pl.BlockSpec(value.shape, lambda *_: (0, 0))


def hidden_kernel(cuts, h_ref, active_ref, bias_ref, *refs):
    pieces, (relu_ref, hidden_ref) = refs[:-2], refs[-2:]
    at, used = 0, 0
    for n in cuts:
        group = pieces[used : used + n]
        used += n
        width = group[0].shape[1]
        total = add_dots(h_ref, group, bias_ref[:, at : at + width])
        relu = jnp.maximum(total, 0.0) * active_ref[...]
        relu_ref[:, at : at + width] = relu
        hidden_ref[:, at : at + width] = (relu * relu).astype(LOW)
        at += width


def hidden_rows(normed, active, bias, groups):
    length, width = normed.shape
    units = bias.shape[1]
    rows = BLOCK_Q
    pieces = [p for group in groups for p in group]
    return pl.pallas_call(
        functools.partial(hidden_kernel, tuple(len(g) for g in groups)),
        grid=(length // rows,),
        in_specs=[
            pl.BlockSpec((rows, width), lambda i: (i, 0)),
            pl.BlockSpec((rows, 1), lambda i: (i, 0)),
            fixed(bias),
        ]
        + [fixed(p) for p in pieces],
        out_specs=[pl.BlockSpec((rows, units), lambda i: (i, 0))] * 2,
        out_shape=[
            jax.ShapeDtypeStruct((length, units), WIDE),
            jax.ShapeDtypeStruct((length, units), LOW),
        ],
        name="hidden_rows",
    )(normed, active, bias, *pieces)


def ffn_kernel(cuts_down, cuts_up, bit_ref, dz_ref, relu_ref, *refs):
    du_ref, dh_ref = refs[-2:]
    n_down = sum(cuts_down)
    downs, ups = refs[:n_down], refs[n_down:-2]
    at, used = 0, 0
    parts = []
    for n in cuts_down:
        group = downs[used : used + n]
        used += n
        grad, col = None, 0
        for piece in group:
            k = piece.shape[1]
            part = dot_to(dz_ref[:, col : col + k], piece[...], ((1,), (1,)))
            grad = part if grad is None else grad + part
            col += k
        m = grad.shape[1]
        du = (grad * 2.0 * relu_ref[:, at : at + m]).astype(LOW)
        du_ref[:, at : at + m] = du
        parts.append((at, m, du))
        at += m
    for j in range(cuts_up[0]):
        total, used = None, 0
        for g, n in enumerate(cuts_up):
            piece = ups[used + j]
            used += n
            part = dot_to(parts[g][2], piece[...], ((1,), (1,)))
            total = part if total is None else total + part
        k = total.shape[1]
        dh_ref[:, j * k : (j + 1) * k] = total.astype(LOW)


def ffn_rows(bit, down_grad, relu, down_groups, up_groups):
    length, width = down_grad.shape
    units = relu.shape[1]
    rows = BLOCK_Q
    steps = length // rows
    downs = [p for group in down_groups for p in group]
    ups = [p for group in up_groups for p in group]
    return pl.pallas_call(
        functools.partial(
            ffn_kernel, tuple(len(g) for g in down_groups), tuple(len(g) for g in up_groups)
        ),
        grid_spec=pltpu.PrefetchScalarGridSpec(
            num_scalar_prefetch=1,
            grid=(steps,),
            in_specs=[row_spec(steps, rows, width), row_spec(steps, rows, units)]
            + [fixed(p) for p in downs]
            + [fixed(p) for p in ups],
            out_specs=[
                row_spec(steps, rows, units),
                pl.BlockSpec((rows, width), lambda i, bit: (i, 0)),
            ],
        ),
        out_shape=[
            jax.ShapeDtypeStruct((length, units), LOW),
            jax.ShapeDtypeStruct((length, width), LOW),
        ],
        name="ffn_rows",
    )(bit, down_grad, relu, *downs, *ups)


def wide_kernel(cuts, left_ref, *refs):
    pieces, out_ref = refs[:-1], refs[-1]
    for j in range(cuts[0]):
        total, used, at = None, 0, 0
        for n in cuts:
            piece = pieces[used + j]
            used += n
            k = piece.shape[0]
            part = dot_to(left_ref[:, at : at + k], piece[...], ((1,), (0,)))
            total = part if total is None else total + part
            at += k
        m = total.shape[1]
        out_ref[:, j * m : (j + 1) * m] = total.astype(LOW)


def wide_rows(left, groups):
    length, depth = left.shape
    rows = BLOCK_Q
    pieces = [p for group in groups for p in group]
    width = sum(p.shape[1] for p in groups[0])
    return pl.pallas_call(
        functools.partial(wide_kernel, tuple(len(g) for g in groups)),
        grid=(length // rows,),
        in_specs=[pl.BlockSpec((rows, depth), lambda i: (i, 0))] + [fixed(p) for p in pieces],
        out_specs=pl.BlockSpec((rows, width), lambda i: (i, 0)),
        out_shape=jax.ShapeDtypeStruct((length, width), LOW),
        name="wide_rows",
    )(left, *pieces)


def own_kernel(bits_ref, a_ref, b_ref, a_out, b_out):
    width = a_ref.shape[1]
    for mine, theirs in chunks(bits_ref, width):
        at = slice(mine, mine + width // 8)
        a_out[:, at] = a_ref[:, pl.ds(theirs, width // 8)].astype(WIDE)
        b_out[:, at] = b_ref[:, pl.ds(theirs, width // 8)].astype(WIDE)


def own_rows(bits, a, b):
    shape = jax.ShapeDtypeStruct(a.shape, WIDE)
    whole = pl.BlockSpec(a.shape, lambda i, bits: (0, 0))
    return pl.pallas_call(
        own_kernel,
        grid_spec=pltpu.PrefetchScalarGridSpec(
            num_scalar_prefetch=1, grid=(1,), in_specs=[whole, whole], out_specs=[whole, whole]
        ),
        out_shape=[shape, shape],
        name="own_rows",
    )(bits, a, b)


def home_kernel(bits_ref, a_ref, out_ref):
    width = a_ref.shape[1]
    for mine, theirs in chunks(bits_ref, width):
        part = a_ref[:, mine : mine + width // 8]
        out_ref[:, pl.ds(theirs, width // 8)] = part.astype(LOW)


def home_rows(bits, a):
    whole = pl.BlockSpec(a.shape, lambda i, bits: (0, 0))
    return pl.pallas_call(
        home_kernel,
        grid_spec=pltpu.PrefetchScalarGridSpec(
            num_scalar_prefetch=1, grid=(1,), in_specs=[whole], out_specs=whole
        ),
        out_shape=jax.ShapeDtypeStruct(a.shape, LOW),
        name="home_rows",
    )(bits, a)


def first_kernel(
    bits_ref, sum_ref, router_ref, rows_ref, resid_ref, gain_ref, out_ref, sums_ref
):
    grad = sum_ref[...] + router_ref[...]
    rows = rows_ref[...]
    gain = gain_ref[...]
    _, scaled, inverse = norm_forward(rows, gain, 0.0)
    sums_ref[0:1, :] = jnp.sum(grad * scaled, axis=0, keepdims=True)
    sums_ref[1:2, :] = jnp.sum(grad, axis=0, keepdims=True)
    out = (resid_ref[...] + norm_backward(grad, scaled, inverse, gain)).astype(LOW)
    width = out.shape[1]
    for mine, theirs in chunks(bits_ref, width):
        out_ref[:, pl.ds(theirs, width // 8)] = out[:, mine : mine + width // 8]


def first_back(bits, normed_sum, router_part, rows, resid_grad, gain):
    whole = pl.BlockSpec(rows.shape, lambda i, bits: (0, 0))
    width = rows.shape[1]
    return pl.pallas_call(
        first_kernel,
        grid_spec=pltpu.PrefetchScalarGridSpec(
            num_scalar_prefetch=1,
            grid=(1,),
            in_specs=[whole] * 4 + [pl.BlockSpec((1, width), lambda i, bits: (0, 0))],
            out_specs=[whole, pl.BlockSpec((2, width), lambda i, bits: (0, 0))],
        ),
        out_shape=[
            jax.ShapeDtypeStruct(rows.shape, LOW),
            jax.ShapeDtypeStruct((2, width), WIDE),
        ],
        name="first_back",
    )(bits, normed_sum, router_part, rows, resid_grad, gain)


def qkv_kernel(h_ref, *refs):
    pieces, (bias_ref, cos_ref, sin_ref, out_ref) = refs[:-4], refs[-4:]
    total = add_dots(h_ref, pieces, bias_ref[...])
    turned = out_ref.shape[1] // HEAD_DIM * 2 // 3
    cosine, sine = cos_ref[...], sin_ref[...]
    for j in range(out_ref.shape[1] // HEAD_DIM):
        at = slice(j * HEAD_DIM, (j + 1) * HEAD_DIM)
        part = total[:, at]
        if j < turned:
            part = part * cosine + pltpu.roll(part, HEAD_DIM // 2, 1) * sine
        out_ref[:, at] = part.astype(LOW)


def qkv_rows(normed, pieces, bias, cosine, sine):
    length, width = normed.shape
    out = bias.shape[1]
    rows = BLOCK_Q
    return pl.pallas_call(
        qkv_kernel,
        grid=(length // rows,),
        in_specs=[pl.BlockSpec((rows, width), lambda i: (i, 0))]
        + [fixed(p) for p in pieces]
        + [
            fixed(bias),
            pl.BlockSpec((rows, HEAD_DIM), lambda i: (i, 0)),
            pl.BlockSpec((rows, HEAD_DIM), lambda i: (i, 0)),
        ],
        out_specs=pl.BlockSpec((rows, out), lambda i: (i, 0)),
        out_shape=jax.ShapeDtypeStruct((length, out), LOW),
        name="qkv_rows",
    )(normed, *pieces, bias, cosine, sine)


def attend_kernel(q_ref, k_ref, v_ref, key_ref, span_ref, active_ref, out_ref, lse_ref):
    scores = dot_to(k_ref[...], q_ref[...], ((1,), (1,))) * (HEAD_DIM**-0.5)
    key = key_ref[...]
    allowed = (key >= span_ref[0:1, :]) & (key <= span_ref[1:2, :])
    scores = jnp.where(allowed, scores, NEVER)
    top = jnp.max(scores, axis=0, keepdims=True)
    weights = jnp.exp(scores - top)
    total = jnp.sum(weights, axis=0, keepdims=True)
    probs = (weights * (1.0 / total)).astype(LOW)
    mixed = dot_to(probs, v_ref[...], ((0,), (0,)))
    out_ref[...] = (mixed * active_ref[0]).astype(LOW)
    lse_ref[0] = top + jnp.log(total)


def turn_back(grad, cosine, sine):
    lane = lax.broadcasted_iota(jnp.int32, grad.shape, 1)
    moved = pltpu.roll(grad * sine, HEAD_DIM // 2, 1)
    return grad * cosine + jnp.where(lane < HEAD_DIM // 2, moved, -moved)


def attend_back_kernel(
    q_ref, k_ref, v_ref, da_ref, w_ref, active_ref, lse_ref,
    key_ref, span_ref, cos_ref, sin_ref, out_ref, dk_sum, dv_sum,
):
    head, step = pl.program_id(0), pl.program_id(1)
    inner = out_ref.shape[1] // 3

    @pl.when(step == 0)
    def _():
        dk_sum[...] = jnp.zeros_like(dk_sum)
        dv_sum[...] = jnp.zeros_like(dv_sum)

    scale = HEAD_DIM**-0.5
    query, key = q_ref[...], k_ref[...]
    grad = dot_to(da_ref[...], w_ref[...], ((1,), (1,)))
    grad = (grad * active_ref[0]).astype(LOW)
    scores = dot_to(key, query, ((1,), (1,))) * scale
    place = key_ref[...]
    allowed = (place >= span_ref[0:1, :]) & (place <= span_ref[1:2, :])
    probs = jnp.exp(jnp.where(allowed, scores, NEVER) - lse_ref[0])
    prob_grad = dot_to(v_ref[...], grad, ((1,), (1,)))
    delta = jnp.sum(probs * prob_grad, axis=0, keepdims=True)
    score_grad = (probs * (prob_grad - delta) * scale).astype(LOW)
    dv_sum[...] += dot_to(probs.astype(LOW), grad, ((1,), (0,)))
    dk_sum[...] += dot_to(score_grad, query, ((1,), (0,)))
    dq = dot_to(score_grad, key, ((0,), (0,)))
    at = pl.ds(pl.multiple_of(step * BLOCK_A, BLOCK_A), BLOCK_A)
    col = pl.multiple_of(head * HEAD_DIM, HEAD_DIM)
    dq = turn_back(dq, cos_ref[at, :], sin_ref[at, :])
    out_ref[at, pl.ds(col, HEAD_DIM)] = dq.astype(LOW)

    @pl.when(step == pl.num_programs(1) - 1)
    def _():
        dk = turn_back(dk_sum[...], cos_ref[...], sin_ref[...])
        out_ref[:, pl.ds(inner + col, HEAD_DIM)] = dk.astype(LOW)
        out_ref[:, pl.ds(2 * inner + col, HEAD_DIM)] = dv_sum[...].astype(LOW)


def attend(qkv, key_place, span, active, heads):
    length = qkv.shape[0]
    d = HEAD_DIM
    n = heads
    return pl.pallas_call(
        attend_kernel,
        grid=(heads, length // BLOCK_A),
        in_specs=[
            pl.BlockSpec((BLOCK_A, d), lambda h, i: (i, h)),
            pl.BlockSpec((length, d), lambda h, i: (0, n + h)),
            pl.BlockSpec((length, d), lambda h, i: (0, 2 * n + h)),
            pl.BlockSpec((length, 1), lambda h, i: (0, 0)),
            pl.BlockSpec((2, BLOCK_A), lambda h, i: (0, i)),
            pl.BlockSpec((1, BLOCK_A, 1), lambda h, i: (h, i, 0)),
        ],
        out_specs=[
            pl.BlockSpec((BLOCK_A, d), lambda h, i: (i, h)),
            pl.BlockSpec((1, 1, BLOCK_A), lambda h, i: (h, 0, i)),
        ],
        out_shape=[
            jax.ShapeDtypeStruct((length, heads * d), LOW),
            jax.ShapeDtypeStruct((heads, 1, length), WIDE),
        ],
        name="attend",
    )(qkv, qkv, qkv, key_place, span, active)


def attend_back(qkv, out_grad, w_out, active, lse, key_place, span, cosine, sine, heads):
    length, width = out_grad.shape
    d = HEAD_DIM
    n = heads
    return pl.pallas_call(
        attend_back_kernel,
        grid=(heads, length // BLOCK_A),
        in_specs=[
            pl.BlockSpec((BLOCK_A, d), lambda h, i: (i, h)),
            pl.BlockSpec((length, d), lambda h, i: (0, n + h)),
            pl.BlockSpec((length, d), lambda h, i: (0, 2 * n + h)),
            pl.BlockSpec((BLOCK_A, width), lambda h, i: (i, 0)),
            pl.BlockSpec((d, width), lambda h, i: (h, 0)),
            pl.BlockSpec((1, BLOCK_A, 1), lambda h, i: (h, i, 0)),
            pl.BlockSpec((1, 1, BLOCK_A), lambda h, i: (h, 0, i)),
            pl.BlockSpec((length, 1), lambda h, i: (0, 0)),
            pl.BlockSpec((2, BLOCK_A), lambda h, i: (0, i)),
            pl.BlockSpec((length, d), lambda h, i: (0, 0)),
            pl.BlockSpec((length, d), lambda h, i: (0, 0)),
        ],
        out_specs=pl.BlockSpec((length, 3 * heads * d), lambda h, i: (0, 0)),
        out_shape=jax.ShapeDtypeStruct((length, 3 * heads * d), LOW),
        scratch_shapes=[pltpu.VMEM((length, d), WIDE), pltpu.VMEM((length, d), WIDE)],
        name="attend_back",
    )(qkv, qkv, qkv, out_grad, w_out, active, lse, key_place, span, cosine, sine)


def grouped(
    tokens,
    cotangent,
    head_groups,
    ffn_widths,
    doc_lengths,
    first_gain,
    first_shift,
    router_weight,
    in_weight,
    in_bias,
    out_weight,
    out_bias,
    second_gain,
    second_shift,
    up_weight,
    up_bias,
    down_weight,
    down_bias,
):
    zh, zl, x, c, y = (lax.axis_index(a) for a in ("zh", "zl", "x", "c", "y"))
    micro, tok_dev, width = tokens.shape
    half = tok_dev // 2
    own = 4 * half
    length = 16 * tok_dev
    block = width // 16
    tp_heads, head_dim = in_weight.shape[2:]
    heads = tp_heads // 4
    inner = heads * head_dim
    tp_units = up_weight.shape[1]
    units = tp_units // 4
    batch = zh * 2 + x
    part = zl * 2 + c
    place = (c * 2 + zl) * 2 + y

    def exchange(value):
        return lax.all_to_all(value, ("zl", "c"), 0, 0, tiled=True)

    def keep_and_send(value, bit, at):
        return (
            lax.dynamic_index_in_dim(value, bit, at, keepdims=False),
            lax.dynamic_index_in_dim(value, 1 - bit, at, keepdims=False),
        )

    def across(pieces):
        return (
            pieces[0],
            swap(pieces[1], "x"),
            swap(pieces[2], "zh"),
            lax.ppermute(pieces[3], PARTS, [(i, i ^ 3) for i in range(4)]),
        )

    def to_batch(value):
        value = lax.dynamic_slice_in_dim(value, y * half, half, 1)
        return across(
            [lax.dynamic_index_in_dim(value, batch ^ k, 0, keepdims=False) for k in range(4)]
        )

    bits = jnp.stack([zh, x]).astype(jnp.int32)
    core = c.reshape(1).astype(jnp.int32)
    e_in = exchange(jnp.moveaxis(in_weight.reshape(block, 3, 4, heads, head_dim), 2, 0))
    e_in = e_in.reshape(4 * block, 3 * inner)

    def rows_of_block(value):
        value = value.astype(LOW).reshape(-1)
        return jnp.pad(value, (0, -value.shape[0] % block)).reshape(-1, block)

    small = jnp.concatenate(
        [
            rows_of_block(v)
            for v in (
                first_gain,
                first_shift,
                second_gain,
                second_shift,
                out_bias,
                down_bias,
                router_weight,
                up_bias,
                head_groups,
                ffn_widths,
                in_bias,
            )
        ],
        axis=0,
    )
    n_small = small.shape[0]
    small_rows = -(-n_small * block // width)
    small = jnp.pad(small.reshape(-1), (0, small_rows * width - n_small * block))
    small = small.reshape(small_rows, width)
    mine_of = lax.dynamic_slice_in_dim(tokens, y * half, half, 1)
    token_pieces = across(
        [
            jnp.concatenate(
                [lax.dynamic_index_in_dim(mine_of, batch ^ k, 0, keepdims=False), small], axis=0
            )
            for k in range(4)
        ]
    )
    small = jnp.stack([p[half:].reshape(-1)[: n_small * block] for p in token_pieces])
    small = gather_over(small[None], ("c", "zl"), (c, zl))
    tokens_own = jnp.concatenate([p[:half] for p in token_pieces], axis=0)

    index = jnp.arange(length, dtype=jnp.int32).reshape(2, 2, 2, 2, 2, half)

    def by_place(value):
        lead = tuple(range(value.ndim - 6))
        at = value.ndim - 6
        value = jnp.transpose(value, lead + tuple(at + i for i in (3, 1, 4, 0, 2, 5)))
        return value.reshape(value.shape[: value.ndim - 6] + (length,))

    positions = by_place(index) ^ (zh * (8 * tok_dev) + x * (2 * tok_dev))
    ends = jnp.cumsum(lax.dynamic_index_in_dim(doc_lengths, batch, 0, keepdims=False))
    first = jnp.max(jnp.where(ends[:, None] <= positions[None, :], ends[:, None], 0), axis=0)
    span = jnp.stack([first, positions])
    key_place = positions[:, None]
    cosine, sine = rotary_tables(positions)
    lane = jnp.arange(HEAD_DIM)[None, :]
    signed = jnp.where(lane < HEAD_DIM // 2, -sine, sine)
    tokens_own, small, e_in, cosine, sine, signed, span, key_place = tie(
        tokens_own, small, e_in, cosine, sine, signed, span, key_place
    )

    tokens_all = lax.all_gather(tokens_own, GROUP, axis=0, tiled=True)
    in_z = swap(e_in, "zh")
    in_x = swap(e_in, "x")
    e_out = exchange(out_weight.reshape(4, inner, block))
    e_out = jnp.moveaxis(e_out, 0, 1).reshape(inner, 4 * block)
    small_own = small.reshape(2, 2, 2, 2, n_small * block).astype(WIDE)
    small_own = jnp.transpose(small_own, (2, 0, 3, 1, 4)).reshape(16, n_small * block)
    n_vec = 6 + 2 * GROUPS
    rows_of = jnp.arange(16) ^ (zh * 8 + x * 2)
    pick = (rows_of[:, None] == jnp.arange(16)[None, :]).astype(WIDE)
    small_all = jnp.dot(pick, small_own[:, n_vec * block :], precision=HIGHEST)
    vectors_f = small_own[:, : n_vec * block].reshape(2, 2, 2, 2, n_vec, block)
    vectors_f = jnp.transpose(vectors_f, (4, 0, 2, 1, 3, 5)).reshape(n_vec, width)
    router = vectors_f[6:].astype(LOW)
    size = up_bias.size
    bias_up = small_all[:, :size].reshape((16,) + up_bias.shape)
    bias_up = jnp.moveaxis(bias_up, 0, 1).reshape(4, units)
    bias_up = lax.dynamic_index_in_dim(bias_up, part, 0, keepdims=True)
    at = size
    size = 2 * micro * tok_dev
    widths = small_own[:, n_vec * block + at : n_vec * block + at + size]
    widths = widths.reshape(16, 2, micro, tok_dev)
    widths = lax.dynamic_index_in_dim(widths, batch, 2, keepdims=False).astype(jnp.int32)
    widths = jnp.swapaxes(widths, 0, 1).reshape(2, 2, 2, 2, 2, 2, half)
    at += size
    bias_in = small_all[:, at : at + in_bias.size].reshape((16,) + in_bias.shape)
    bias_in = jnp.moveaxis(bias_in, 0, 2).reshape(3, 4, heads, head_dim)
    bias_in = lax.dynamic_index_in_dim(bias_in, part, 1, keepdims=False)
    bias_in = bias_in.reshape(1, 3 * inner)
    heads_row, units_row = by_place(widths)
    head_ids = (y * 4 + part) * heads + jnp.arange(heads, dtype=jnp.int32)
    head_active = (head_ids[:, None] // (HEADS // GROUPS) < heads_row[None, :]).astype(WIDE)
    head_active = head_active[:, :, None]
    unit_group = (y * 4 + part) * units // (FF // GROUPS)
    unit_active = (unit_group < units_row).astype(WIDE)[:, None]
    (
        in_z, in_x, e_out, vectors_f, router, bias_in, bias_up, head_active, unit_active,
        cotangent, up_weight,
    ) = tie(
        in_z, in_x, e_out, vectors_f, router, bias_in, bias_up, head_active, unit_active,
        cotangent, up_weight,
    )
    gain_one, shift_one, gain_two, shift_two, bias_out, bias_down = (
        vectors_f[i : i + 1] for i in range(6)
    )

    in_zx = swap(in_z, "x")
    out_z = swap(e_out, "zh")
    cotangent_pieces = to_batch(cotangent)
    e_up = exchange(jnp.moveaxis(up_weight.reshape(block, 4, units), 1, 0))
    e_up = e_up.reshape(4 * block, units)
    normed_low, logits = norm_rows(bits, tokens_all, gain_one, shift_one, router)
    normed_low, in_zx, out_z, e_up, down_weight, logits, e_out, *cotangent_pieces = tie(
        normed_low, in_zx, out_z, e_up, down_weight, logits, e_out, *cotangent_pieces
    )
    cotangent_own = jnp.concatenate(cotangent_pieces, axis=0)
    cotangent_all = lax.all_gather(cotangent_own, GROUP, axis=0, tiled=True)
    def mine(value):
        return lax.dynamic_slice_in_dim(value, place * own, own, 0)

    cut_units = units // 2
    out_zx = swap(out_z, "x")
    out_x = swap(e_out, "x")
    up_x1 = swap(e_up[:, :cut_units], "x")
    up_z1 = swap(e_up[:, :cut_units], "zh")
    e_down = exchange(down_weight.reshape(4, units, block))
    e_down = jnp.moveaxis(e_down, 0, 1).reshape(units, 4 * block)
    w_in = (e_in, in_x, in_z, in_zx)
    qkv = qkv_rows(normed_low, w_in, bias_in, cosine, signed)
    mixed, lse = attend(qkv, key_place, span, head_active, heads)
    w_out = jnp.concatenate([e_out, out_x, out_z, out_zx], axis=1)
    mixed, w_out, e_up, up_x1, up_z1, tokens_own, logits = tie(
        mixed, w_out, e_up, up_x1, up_z1, tokens_own, logits
    )

    part_own = own // 2

    def halves(value):
        return (
            lax.dynamic_slice_in_dim(value, c * (length // 2), length // 2, 0),
            lax.dynamic_slice_in_dim(value, (1 - c) * (length // 2), length // 2, 0),
        )

    def group_second(total):
        total = total.reshape(2, 2, own, width)
        a_keep, a_send = keep_and_send(total[:, :, :part_own], zl, 0)
        b_keep, b_send = keep_and_send(total[:, :, part_own:], y, 1)
        a_got = swap(a_send.astype(LOW), "zl")
        b_got = swap(b_send.astype(LOW), "y")
        return a_keep, b_keep, a_got, b_got

    def group_third(a_keep, b_keep, a_got, b_got):
        a_keep, a_send = keep_and_send(a_keep + a_got.astype(WIDE), y, 0)
        b_keep, b_send = keep_and_send(b_keep + b_got.astype(WIDE), zl, 0)
        a_got = swap(a_send.astype(LOW), "y")
        b_got = swap(b_send.astype(LOW), "zl")
        return jnp.concatenate([a_keep + a_got.astype(WIDE), b_keep + b_got.astype(WIDE)], axis=0)

    attn_here, attn_away = halves(mixed)
    attn_away = dot_to(attn_away, w_out, ((1,), (0,))).astype(LOW)
    attn_away, attn_here, tokens_own, cotangent_own, logits = tie(
        attn_away, attn_here, tokens_own, cotangent_own, logits
    )
    attn_got = swap(attn_away, "c")
    up_x2 = swap(e_up[:, cut_units:], "x")
    up_z2 = swap(e_up[:, cut_units:], "zh")
    up_zx1 = swap(up_z1, "x")
    options = jnp.arange(GROUPS, dtype=jnp.int32)
    attn_prob = jax.nn.softmax(logits[:, :GROUPS], axis=-1)
    ffn_prob = jax.nn.softmax(logits[:, GROUPS:], axis=-1)
    attn_pick = (options[None, :] == heads_row[:, None] - 1).astype(WIDE)
    ffn_pick = (options[None, :] == units_row[:, None] - 1).astype(WIDE)
    attn_gate = GROUPS * jnp.sum(attn_prob * attn_pick, axis=-1, keepdims=True)
    ffn_gate = GROUPS * jnp.sum(ffn_prob * ffn_pick, axis=-1, keepdims=True)
    attn_total = dot_to(attn_here, w_out, ((1,), (0,))) + attn_got.astype(WIDE)
    attn_total, attn_gate, ffn_gate, tokens_own, cotangent_own, e_down = tie(
        attn_total, attn_gate, ffn_gate, tokens_own, cotangent_own, e_down
    )
    attn_total = attn_total.reshape(2, 2, own, width)
    attn_keep, attn_send = keep_and_send(attn_total, y, 1)
    attn_got = swap(attn_send.astype(LOW), "y")
    rows, upstream = own_rows(bits, tokens_own, cotangent_own)
    attn_keep, attn_got, rows, upstream, up_x2, up_z2, cotangent_all = tie(
        attn_keep, attn_got, rows, upstream, up_x2, up_z2, cotangent_all
    )
    attn_keep, attn_send = keep_and_send(attn_keep + attn_got.astype(WIDE), zl, 0)
    attn_sum = attn_keep + swap(attn_send.astype(LOW), "zl").astype(WIDE)
    down_x1 = swap(e_down[:cut_units], "x")
    attn_sum, down_x1, e_down = tie(attn_sum, down_x1, e_down)

    attn_branch = attn_sum + bias_out
    attn_gate_own = mine(attn_gate)
    ffn_gate_own = mine(ffn_gate)
    resid = rows + attn_gate_own * attn_branch
    normed_two, scaled_two, inverse_two = norm_forward(resid, gain_two, shift_two)
    normed_two_low = normed_two.astype(LOW)
    normed_two_low, e_down, cotangent_all, up_z2 = tie(
        normed_two_low, e_down, cotangent_all, up_z2
    )
    normed_two_low = lax.all_gather(normed_two_low, GROUP, axis=0, tiled=True)
    down_z1 = swap(e_down[:cut_units], "zh")
    up_zx2 = swap(up_z2, "x")
    down_x2 = swap(e_down[cut_units:], "x")
    down_grad = gate_rows(bits, cotangent_all, ffn_gate)
    down_grad, down_z1, up_zx2, down_x2, e_down = tie(
        down_grad, down_z1, up_zx2, down_x2, e_down
    )
    down_z2 = swap(e_down[cut_units:], "zh")
    down_zx1 = swap(down_z1, "x")
    normed_two_low, down_z2, down_zx1, up_zx1 = tie(normed_two_low, down_z2, down_zx1, up_zx1)

    def columns(value, k):
        return value[:, k * 4 * block : (k + 1) * 4 * block]

    down_zx2 = swap(down_z2, "x")
    w_up = (
        (e_up[:, :cut_units], up_x1, up_z1, up_zx1),
        (e_up[:, cut_units:], up_x2, up_z2, up_zx2),
    )
    relu_part, hidden = hidden_rows(normed_two_low, unit_active, bias_up, w_up)

    def down_piece(k):
        return dot_to(hidden, columns(down_grad, k), ((0,), (0,)))

    relu_part, hidden, down_zx2 = tie(relu_part, hidden, down_zx2)
    w_down = (
        (e_down[:cut_units], down_x1, down_z1, down_zx1),
        (e_down[cut_units:], down_x2, down_z2, down_zx2),
    )
    up_grad, two_part = ffn_rows(core, down_grad, relu_part, w_down, w_up)
    two_away, two_here = two_part[: length // 2], two_part[length // 2 :]
    two_got = swap(two_away, "c")

    def up_piece(k):
        return dot_to(columns(normed_two_low, k), up_grad, ((0,), (0,)))

    down_got3 = swap(down_piece(3).astype(LOW), "x")
    two_total = two_here.astype(WIDE) + two_got.astype(WIDE)
    two_total, hidden, up_grad = tie(two_total, hidden, up_grad)
    two_parts = group_second(two_total)
    up_send3 = up_piece(3).astype(LOW)
    down_send1 = down_piece(1).astype(LOW)
    *two_parts, down_send1, up_send3, up_grad = tie(*two_parts, down_send1, up_send3, up_grad)
    normed_two_grad = group_third(*two_parts)
    up_got3 = swap(up_send3, "x")
    normed_two_grad, hidden, down_grad, up_grad, down_got3 = tie(
        normed_two_grad, hidden, down_grad, up_grad, down_got3
    )
    down_send2 = (down_piece(2) + down_got3.astype(WIDE)).astype(LOW)

    resid_grad = upstream + norm_backward(normed_two_grad, scaled_two, inverse_two, gain_two)
    gated_attn = attn_gate_own * resid_grad
    gated_low = gated_attn.astype(LOW)
    gated_low, hidden, down_grad, up_grad, normed_two_grad, resid_grad, down_send2 = tie(
        gated_low, hidden, down_grad, up_grad, normed_two_grad, resid_grad, down_send2
    )
    attn_out_grad = lax.all_gather(gated_low, GROUP, axis=0, tiled=True)
    down_far1 = swap(down_send2[:cut_units], "zh")
    down_got1 = swap(down_send1, "x")
    w_in = jnp.concatenate(w_in, axis=0)
    ffn_part = wide_rows(hidden, w_down)
    grad_gain_two = jnp.sum(normed_two_grad * scaled_two, axis=0)
    grad_shift_two = jnp.sum(normed_two_grad, axis=0)
    attn_gate_grad = jnp.sum(resid_grad * attn_branch, axis=-1)
    grad_out_bias = jnp.sum(attn_gate_own * resid_grad, axis=0)
    up_send1 = up_piece(1).astype(LOW)
    up_send2 = (up_piece(2) + up_got3.astype(WIDE)).astype(LOW)
    (
        attn_out_grad, ffn_part, up_send1, up_send2, grad_out_bias, grad_gain_two, w_in,
        down_far1, down_send2,
    ) = tie(
        attn_out_grad, ffn_part, up_send1, up_send2, grad_out_bias, grad_gain_two, w_in,
        down_far1, down_send2,
    )
    down_far2 = swap(down_send2[cut_units:], "zh")

    def out_piece(k):
        return dot_to(mixed, columns(attn_out_grad, k), ((0,), (0,)))

    ffn_sum = lax.psum_scatter(ffn_part, GROUP, scatter_dimension=0, tiled=True)
    out_got = swap(jnp.stack([out_piece(1), out_piece(3)]).astype(LOW), "x")
    proj_grad = attend_back(
        qkv, attn_out_grad, w_out, head_active, lse, key_place, span, cosine, sine, heads
    )
    proj_grad, attn_out_grad, down_got1, down_far2, hidden, up_send1, up_send2, out_got = tie(
        proj_grad, attn_out_grad, down_got1, down_far2, hidden, up_send1, up_send2, out_got
    )

    def in_piece(k):
        return dot_to(columns(normed_low, k), proj_grad, ((0,), (0,)))

    one_here, one_away = halves(proj_grad)
    one_away = dot_to(one_away, w_in, ((1,), (1,))).astype(LOW)
    one_away, one_here, proj_grad, hidden, out_got, up_send2 = tie(
        one_away, one_here, proj_grad, hidden, out_got, up_send2
    )
    one_got = swap(one_away, "c")
    up_far = swap(up_send2, "zh")
    in_send3 = in_piece(3).astype(LOW)
    in_got3 = swap(in_send3, "x")
    one_total = dot_to(one_here, w_in, ((1,), (1,))) + one_got.astype(WIDE)
    one_total, proj_grad, in_send3, out_got, up_send1, hidden = tie(
        one_total, proj_grad, in_send3, out_got, up_send1, hidden
    )
    one_parts = group_second(one_total)
    in_send1 = in_piece(1).astype(LOW)
    out_send2 = (out_piece(2) + out_got[1].astype(WIDE)).astype(LOW)
    *one_parts, in_send1, out_send2, in_got3, ffn_sum, up_send1, hidden = tie(
        *one_parts, in_send1, out_send2, in_got3, ffn_sum, up_send1, hidden
    )
    normed_sum = group_third(*one_parts)
    in_got1 = swap(in_send1, "x")
    up_got1 = swap(up_send1, "x")
    out_far = swap(out_send2, "zh")
    in_send2 = (in_piece(2) + in_got3.astype(WIDE)).astype(LOW)
    ffn_branch = ffn_sum.astype(WIDE) + bias_down
    ffn_gate_grad = jnp.sum(upstream * ffn_branch, axis=-1)
    logit_grad = jnp.concatenate(
        [
            gate_logit_grad(mine(attn_prob), mine(attn_pick), attn_gate_grad),
            gate_logit_grad(mine(ffn_prob), mine(ffn_pick), ffn_gate_grad),
        ],
        axis=-1,
    )
    router_part = jnp.dot(logit_grad, vectors_f[6:], precision=HIGHEST)

    def both_halves(value, other):
        def batches(v):
            v = v.reshape(2, 2, half, width)
            return flip_where(x, flip_where(zh, v, 0), 1).reshape(4, half, width)

        value, other = batches(value), batches(other)
        return jnp.where(
            y == 0,
            jnp.concatenate([value, other], axis=1),
            jnp.concatenate([other, value], axis=1),
        )

    def spread(rows, cut):
        rows = from_own_order(rows, zh, x)
        return jnp.swapaxes(rows.reshape(cut, 16, block), 0, 1).reshape(16, cut * block)

    normed_sum, in_send2, router_part, ffn_branch, logit_grad, up_far, hidden = tie(
        normed_sum, in_send2, router_part, ffn_branch, logit_grad, up_far, hidden
    )

    in_far = swap(in_send2, "zh")
    tokens_low, last = first_back(bits, normed_sum, router_part, rows, resid_grad, gain_one)
    tokens_low = tokens_low.reshape(4, half, width)
    tokens_low, last, ffn_branch, logit_grad, up_grad, out_far, up_far, hidden = tie(
        tokens_low, last, ffn_branch, logit_grad, up_grad, out_far, up_far, hidden
    )
    tokens_pieces = across([tokens_low[k] for k in range(4)])
    block_low = home_rows(bits, resid + ffn_gate_own * ffn_branch).reshape(4, half, width)
    normed_own = mine(normed_low)
    grad_router = jnp.dot(logit_grad.T, normed_own.astype(WIDE), precision=HIGHEST)
    grad_down_bias = jnp.sum(ffn_gate_own * upstream, axis=0)
    grad_up_bias = jnp.sum(up_grad.astype(WIDE), axis=0)
    grad_in_bias = jnp.sum(proj_grad.astype(WIDE), axis=0).reshape(3, heads, head_dim)
    sums = jnp.stack([grad_out_bias, grad_gain_two, grad_shift_two, grad_down_bias])
    sums = spread(jnp.concatenate([last, sums, grad_router], axis=0), n_vec)
    chosen = (jnp.arange(4) == part).astype(WIDE)
    spread_in = (grad_in_bias[:, None] * chosen[None, :, None, None]).reshape(
        3, tp_heads, 16, head_dim // 16
    )
    spread_in = jnp.moveaxis(spread_in, 2, 0).reshape(16, -1)
    spread_up = (grad_up_bias[None, :] * chosen[:, None]).reshape(up_bias.shape[0], 16, block)
    spread_up = jnp.moveaxis(spread_up, 1, 0).reshape(16, -1)
    total = jnp.concatenate([sums, spread_in, spread_up], axis=1)
    down_far = jnp.concatenate([down_far1, down_far2], axis=0)
    down_home = (down_piece(0) + down_got1.astype(WIDE) + down_far.astype(WIDE)).astype(LOW)
    down_home = exchange(jnp.moveaxis(down_home.reshape(units, 4, block), 1, 0))
    up_home = (up_piece(0) + up_got1.astype(WIDE) + up_far.astype(WIDE)).astype(LOW)
    up_home = exchange(up_home.reshape(4, block, units))
    out_home = (out_piece(0) + out_got[0].astype(WIDE) + out_far.astype(WIDE)).astype(LOW)
    *tokens_pieces, total, block_low, up_home, out_home, in_got1, down_home, in_far = tie(
        *tokens_pieces, total, block_low, up_home, out_home, in_got1, down_home, in_far
    )
    total = reduce_rows(total, zh, zl, x, c)
    tokens_grad = jnp.stack(tokens_pieces)
    tokens_other = swap(tokens_grad, "y")
    block_out = jnp.stack(across([block_low[k] for k in range(4)]))
    out_home = exchange(jnp.moveaxis(out_home.reshape(inner, 4, block), 1, 0))
    in_home = (in_piece(0) + in_got1.astype(WIDE) + in_far.astype(WIDE)).astype(LOW)
    tokens_other, block_out, in_home, out_home, total = tie(
        tokens_other, block_out, in_home, out_home, total
    )
    block_other = swap(block_out, "y")
    in_home = exchange(in_home.reshape(4, block, 3 * inner)).reshape(4, block, 3, heads, head_dim)
    at = n_vec * block
    shared = total[:at]
    shared = (shared + swap(shared, "y")).reshape(n_vec, block)
    early = total[at:]
    return (
        both_halves(block_out, block_other),
        both_halves(tokens_grad, tokens_other).astype(WIDE),
        shared[0],
        shared[1],
        shared[6:],
        jnp.transpose(in_home, (1, 2, 0, 3, 4)).reshape(in_weight.shape).astype(WIDE),
        early[: in_bias.size].reshape(in_bias.shape),
        out_home.reshape(out_weight.shape).astype(WIDE),
        shared[2],
        shared[3],
        shared[4],
        jnp.swapaxes(up_home, 0, 1).reshape(up_weight.shape).astype(WIDE),
        early[in_bias.size :].reshape(up_bias.shape),
        down_home.reshape(down_weight.shape).astype(WIDE),
        shared[5],
    )


def solution(mesh):
    body, seq, tp = local, "seq", "tp"
    if mesh.shape["seq"] == 16 and mesh.shape["tp"] == 2:
        mesh = Mesh(mesh.devices.reshape(2, 2, 2, 2, 2), ROWS + ("y",))
        body, seq, tp = grouped, ROWS, "y"
    return jax.shard_map(
        body,
        mesh=mesh,
        in_specs=(
            P(None, seq, None),
            P(None, seq, None),
            P(None, seq),
            P(None, seq),
            P(),
            P(seq),
            P(seq),
            P(None, seq),
            P(seq, None, tp, None),
            P(None, tp, seq),
            P(tp, None, seq),
            P(seq),
            P(seq),
            P(seq),
            P(seq, tp),
            P(tp, seq),
            P(tp, seq),
            P(seq),
        ),
        out_specs=(
            P(None, seq, None),
            P(None, seq, None),
            P(seq),
            P(seq),
            P(None, seq),
            P(seq, None, tp, None),
            P(None, tp, seq),
            P(tp, None, seq),
            P(seq),
            P(seq),
            P(seq),
            P(seq, tp),
            P(tp, seq),
            P(tp, seq),
            P(seq),
        ),
        check_vma=False,
    )
```

```python
import functools
import math

import jax
import jax.numpy as jnp
from jax import lax
from jax.experimental import pallas as pl
from jax.experimental.pallas import tpu as pltpu
from jax.sharding import Mesh
from jax.sharding import PartitionSpec as P

HEADS = 16
HEAD_DIM = 128
FF = 8192
GROUPS = 4


EPSILON = 1e-05
HIGHEST = lax.Precision.HIGHEST


def norm_forward(rows, gain, shift):
    center = rows - jnp.mean(rows, axis=-1, keepdims=True)
    inverse = lax.rsqrt(jnp.mean(center * center, axis=-1, keepdims=True) + EPSILON)
    scaled = center * inverse
    return (scaled * gain + shift, scaled, inverse)


def norm_backward(upstream, scaled, inverse, gain):
    through = upstream * gain
    return inverse * (
        through
        - jnp.mean(through, axis=-1, keepdims=True)
        - scaled * jnp.mean(through * scaled, axis=-1, keepdims=True)
    )


def rotary_tables(positions):
    half_dim = HEAD_DIM // 2
    steps_up = jnp.arange(half_dim, dtype=jnp.float32) * (2.0 / HEAD_DIM)
    inverse = jnp.exp(-math.log(10000.0) * steps_up)
    angles = positions.astype(jnp.float32)[:, None] * inverse[None, :]
    angles = jnp.concatenate([angles, angles], axis=1)
    return (jnp.cos(angles), jnp.sin(angles))


def rotate(vectors, cosine, sine):
    half_dim = vectors.shape[-1] // 2
    turned = jnp.concatenate([-vectors[..., half_dim:], vectors[..., :half_dim]], axis=-1)
    return vectors * cosine[:, None, :] + turned * sine[:, None, :]


def rotate_back(grads, cosine, sine):
    half_dim = grads.shape[-1] // 2
    moved = grads * sine[:, None, :]
    turned = jnp.concatenate([moved[..., half_dim:], -moved[..., :half_dim]], axis=-1)
    return grads * cosine[:, None, :] + turned


def doc_index(lengths, positions):
    ends = jnp.cumsum(lengths)
    return jnp.sum((positions[:, None] >= ends[None, :]).astype(jnp.int32), axis=1)


def gate_logit_grad(prob, pick, gate_grad):
    chosen = jnp.sum(prob * pick, axis=-1, keepdims=True)
    return GROUPS * chosen * (pick - prob) * gate_grad[:, None]


def local(
    tokens,
    cotangent,
    head_groups,
    ffn_widths,
    doc_lengths,
    first_gain,
    first_shift,
    router_weight,
    in_weight,
    in_bias,
    out_weight,
    out_bias,
    second_gain,
    second_shift,
    up_weight,
    up_bias,
    down_weight,
    down_bias,
):
    seq_count = lax.axis_size("seq")
    seq_index = lax.axis_index("seq")
    tp_index = lax.axis_index("tp")
    gathered = (
        lax.all_gather(first_gain, "seq", axis=0, tiled=True),
        lax.all_gather(first_shift, "seq", axis=0, tiled=True),
        lax.all_gather(router_weight, "seq", axis=1, tiled=True),
        lax.all_gather(in_weight, "seq", axis=0, tiled=True),
        lax.all_gather(in_bias, "seq", axis=2, tiled=True),
        lax.all_gather(out_weight, "seq", axis=2, tiled=True),
        lax.all_gather(out_bias, "seq", axis=0, tiled=True),
        lax.all_gather(second_gain, "seq", axis=0, tiled=True),
        lax.all_gather(second_shift, "seq", axis=0, tiled=True),
        lax.all_gather(up_weight, "seq", axis=0, tiled=True),
        lax.all_gather(up_bias, "seq", axis=1, tiled=True),
        lax.all_gather(down_weight, "seq", axis=1, tiled=True),
        lax.all_gather(down_bias, "seq", axis=0, tiled=True),
    )
    (
        gain_one,
        shift_one,
        router_full,
        in_full,
        in_bias_full,
        out_full,
        out_bias_full,
        gain_two,
        shift_two,
        up_full,
        up_bias_full,
        down_full,
        down_bias_full,
    ) = gathered
    micro, tok_dev, width = tokens.shape
    local_heads = in_full.shape[2]
    head_dim = in_full.shape[3]
    inner = local_heads * head_dim
    local_units = up_full.shape[1]
    length = tok_dev * seq_count
    scale = HEAD_DIM ** (-0.5)
    gain_one_f = gain_one.astype(jnp.float32)
    shift_one_f = shift_one.astype(jnp.float32)
    gain_two_f = gain_two.astype(jnp.float32)
    shift_two_f = shift_two.astype(jnp.float32)
    out_bias_f = out_bias_full.astype(jnp.float32)
    down_bias_f = down_bias_full.astype(jnp.float32)
    router_wide = router_full.astype(jnp.float32)
    bias_in = in_bias_full.astype(jnp.float32)
    up_bias_vec = up_bias_full.reshape(local_units).astype(jnp.float32)
    in_matrix = in_full.reshape(width, 3 * inner)
    out_matrix = out_full.reshape(inner, width)
    positions_all = jnp.arange(length, dtype=jnp.int32)
    positions_local = seq_index * tok_dev + jnp.arange(tok_dev, dtype=jnp.int32)
    cosine, sine = rotary_tables(positions_local)
    head_ids = tp_index * local_heads + jnp.arange(local_heads, dtype=jnp.int32)
    unit_ids = tp_index * local_units + jnp.arange(local_units, dtype=jnp.int32)
    options = jnp.arange(GROUPS, dtype=jnp.int32)
    grad_gain_one = jnp.zeros((width,), jnp.float32)
    grad_shift_one = jnp.zeros((width,), jnp.float32)
    grad_router = jnp.zeros(router_full.shape, jnp.float32)
    grad_in = jnp.zeros((width, 3 * inner), jnp.float32)
    grad_in_bias = jnp.zeros(in_bias_full.shape, jnp.float32)
    grad_out = jnp.zeros((inner, width), jnp.float32)
    grad_out_bias = jnp.zeros((width,), jnp.float32)
    grad_gain_two = jnp.zeros((width,), jnp.float32)
    grad_shift_two = jnp.zeros((width,), jnp.float32)
    grad_up = jnp.zeros(up_full.shape, jnp.float32)
    grad_up_bias = jnp.zeros((local_units,), jnp.float32)
    grad_down = jnp.zeros(down_full.shape, jnp.float32)
    grad_down_bias = jnp.zeros((width,), jnp.float32)
    outputs = []
    input_grads = []
    for batch in range(micro):
        rows = tokens[batch].astype(jnp.float32)
        doc_all = doc_index(doc_lengths[batch], positions_all)
        doc_local = lax.dynamic_slice_in_dim(doc_all, seq_index * tok_dev, tok_dev, 0)
        allowed = (positions_all[None, :] <= positions_local[:, None]) & (
            doc_all[None, :] == doc_local[:, None]
        )
        head_active = (head_ids[None, :] // (HEADS // GROUPS) < head_groups[batch][:, None]).astype(
            jnp.float32
        )
        unit_active = (unit_ids[None, :] // (FF // GROUPS) < ffn_widths[batch][:, None]).astype(
            jnp.float32
        )
        normed, scaled_one, inverse_one = norm_forward(rows, gain_one_f, shift_one_f)
        normed_low = normed.astype(jnp.bfloat16)
        logits = jnp.dot(normed_low, router_full.T, preferred_element_type=jnp.float32)
        attn_prob = jax.nn.softmax(logits[:, :GROUPS], axis=-1)
        ffn_prob = jax.nn.softmax(logits[:, GROUPS:], axis=-1)
        attn_pick = (options[None, :] == head_groups[batch][:, None] - 1).astype(jnp.float32)
        ffn_pick = (options[None, :] == ffn_widths[batch][:, None] - 1).astype(jnp.float32)
        attn_gate = GROUPS * jnp.sum(attn_prob * attn_pick, axis=-1)
        ffn_gate = GROUPS * jnp.sum(ffn_prob * ffn_pick, axis=-1)
        projected = jnp.dot(normed_low, in_matrix, preferred_element_type=jnp.float32)
        projected = projected.reshape(tok_dev, 3, local_heads, head_dim) + bias_in
        queries = rotate(projected[:, 0], cosine, sine).astype(jnp.bfloat16)
        keys_low = rotate(projected[:, 1], cosine, sine).astype(jnp.bfloat16)
        values_low = projected[:, 2].astype(jnp.bfloat16)
        keys_all, values_all = (
            lax.all_gather(keys_low, "seq", axis=0, tiled=True),
            lax.all_gather(values_low, "seq", axis=0, tiled=True),
        )
        raw_scores = jnp.einsum(
            "qhd,khd->hqk", queries, keys_all, preferred_element_type=jnp.float32
        )
        scores = jnp.where(allowed[None], raw_scores * scale, -jnp.inf)
        row_max = jnp.max(scores, axis=-1, keepdims=True)
        weights = jnp.exp(scores - row_max)
        row_total = jnp.sum(weights, axis=-1, keepdims=True)
        log_total = row_max + jnp.log(row_total)
        probs = weights / row_total
        attended = jnp.einsum(
            "hqk,khd->qhd",
            probs.astype(jnp.bfloat16),
            values_all,
            preferred_element_type=jnp.float32,
        )
        mixed_heads = (attended * head_active[:, :, None]).astype(jnp.bfloat16)
        mixed_flat = mixed_heads.reshape(tok_dev, inner)
        attn_part = jnp.dot(mixed_flat, out_matrix, preferred_element_type=jnp.float32)
        attn_sum = lax.psum(attn_part, "tp")
        attn_branch = attn_sum + out_bias_f
        resid = rows + attn_gate[:, None] * attn_branch
        normed_two, scaled_two, inverse_two = norm_forward(resid, gain_two_f, shift_two_f)
        normed_two_low = normed_two.astype(jnp.bfloat16)
        up_pre = jnp.dot(normed_two_low, up_full, preferred_element_type=jnp.float32) + up_bias_vec
        relu_part = jnp.maximum(up_pre, 0.0)
        hidden = (unit_active * jnp.square(relu_part)).astype(jnp.bfloat16)
        down_part = jnp.dot(hidden, down_full, preferred_element_type=jnp.float32)
        down_sum = lax.psum(down_part.astype(jnp.bfloat16), "tp").astype(jnp.float32)
        ffn_branch = down_sum + down_bias_f
        outputs.append((resid + ffn_gate[:, None] * ffn_branch).astype(jnp.bfloat16))
        upstream = cotangent[batch].astype(jnp.float32)
        ffn_gate_grad = jnp.sum(upstream * ffn_branch, axis=-1)
        gated_up = ffn_gate[:, None] * upstream
        grad_down_bias = grad_down_bias + jnp.sum(gated_up, axis=0)
        down_grad = gated_up.astype(jnp.bfloat16)
        grad_down = grad_down + jnp.einsum(
            "tf,td->fd", hidden, down_grad, preferred_element_type=jnp.float32
        )
        hidden_grad = jnp.einsum(
            "td,fd->tf", down_grad, down_full, preferred_element_type=jnp.float32
        )
        up_grad = (hidden_grad * unit_active * 2.0 * relu_part).astype(jnp.bfloat16)
        grad_up_bias = grad_up_bias + jnp.sum(up_grad.astype(jnp.float32), axis=0)
        grad_up = grad_up + jnp.einsum(
            "td,tf->df", normed_two_low, up_grad, preferred_element_type=jnp.float32
        )
        normed_two_part = jnp.einsum(
            "tf,df->td", up_grad, up_full, preferred_element_type=jnp.float32
        )
        normed_two_grad = lax.psum(normed_two_part, "tp")
        grad_gain_two = grad_gain_two + jnp.sum(normed_two_grad * scaled_two, axis=0)
        grad_shift_two = grad_shift_two + jnp.sum(normed_two_grad, axis=0)
        resid_grad = upstream + norm_backward(normed_two_grad, scaled_two, inverse_two, gain_two_f)
        attn_gate_grad = jnp.sum(resid_grad * attn_branch, axis=-1)
        gated_attn = attn_gate[:, None] * resid_grad
        grad_out_bias = grad_out_bias + jnp.sum(gated_attn, axis=0)
        attn_out_grad = gated_attn.astype(jnp.bfloat16)
        grad_out = grad_out + jnp.einsum(
            "ti,td->id", mixed_flat, attn_out_grad, preferred_element_type=jnp.float32
        )
        mixed_grad = jnp.einsum(
            "td,id->ti", attn_out_grad, out_matrix, preferred_element_type=jnp.float32
        )
        attended_grad = (
            mixed_grad.reshape(tok_dev, local_heads, head_dim) * head_active[:, :, None]
        ).astype(jnp.bfloat16)
        again_raw = jnp.einsum(
            "qhd,khd->hqk", queries, keys_all, preferred_element_type=jnp.float32
        )
        again_scores = jnp.where(allowed[None], again_raw * scale, -jnp.inf)
        probs_again = jnp.exp(again_scores - log_total)
        prob_grad = jnp.einsum(
            "qhd,khd->hqk", attended_grad, values_all, preferred_element_type=jnp.float32
        )
        row_dot = jnp.sum(probs_again * prob_grad, axis=-1, keepdims=True)
        score_grad = (probs_again * (prob_grad - row_dot) * scale).astype(jnp.bfloat16)
        query_rot_grad = jnp.einsum(
            "hqk,khd->qhd", score_grad, keys_all, preferred_element_type=jnp.float32
        )
        probs_low = probs_again.astype(jnp.bfloat16)
        key_part = jnp.einsum(
            "hqk,qhd->khd", score_grad, queries, preferred_element_type=jnp.float32
        )
        value_part = jnp.einsum(
            "hqk,qhd->khd", probs_low, attended_grad, preferred_element_type=jnp.float32
        )
        combined = lax.psum_scatter(
            jnp.concatenate([key_part, value_part], axis=1).reshape(
                lax.axis_size("seq") * tok_dev, 2 * inner
            ),
            "seq",
            scatter_dimension=0,
            tiled=True,
        )
        combined = combined.reshape(tok_dev, 2 * local_heads, head_dim)
        key_rot_grad = combined[:, :local_heads]
        value_grad = combined[:, local_heads:]
        query_grad = rotate_back(query_rot_grad, cosine, sine)
        key_grad = rotate_back(key_rot_grad, cosine, sine)
        proj_grad = jnp.stack([query_grad, key_grad, value_grad], axis=1).astype(jnp.bfloat16)
        grad_in_bias = grad_in_bias + jnp.sum(proj_grad.astype(jnp.float32), axis=0)
        proj_flat = proj_grad.reshape(tok_dev, 3 * inner)
        grad_in = grad_in + jnp.einsum(
            "tw,tc->wc", normed_low, proj_flat, preferred_element_type=jnp.float32
        )
        normed_part = jnp.einsum(
            "tc,wc->tw", proj_flat, in_matrix, preferred_element_type=jnp.float32
        )
        logit_grad = jnp.concatenate(
            [
                gate_logit_grad(attn_prob, attn_pick, attn_gate_grad),
                gate_logit_grad(ffn_prob, ffn_pick, ffn_gate_grad),
            ],
            axis=-1,
        )
        grad_router = grad_router + jnp.dot(
            logit_grad.T, normed_low.astype(jnp.float32), precision=HIGHEST
        )
        router_part = jnp.dot(logit_grad, router_wide, precision=HIGHEST)
        normed_grad = lax.psum(normed_part, "tp") + router_part
        grad_gain_one = grad_gain_one + jnp.sum(normed_grad * scaled_one, axis=0)
        grad_shift_one = grad_shift_one + jnp.sum(normed_grad, axis=0)
        input_grads.append(
            resid_grad + norm_backward(normed_grad, scaled_one, inverse_one, gain_one_f)
        )
    reduced = (
        lax.psum_scatter(grad_gain_one, "seq", scatter_dimension=0, tiled=True),
        lax.psum_scatter(grad_shift_one, "seq", scatter_dimension=0, tiled=True),
        lax.psum_scatter(grad_router, "seq", scatter_dimension=1, tiled=True),
        lax.psum_scatter(
            grad_in.reshape(width, 3, local_heads, head_dim), "seq", scatter_dimension=0, tiled=True
        ),
        lax.psum_scatter(grad_in_bias, "seq", scatter_dimension=2, tiled=True),
        lax.psum_scatter(
            grad_out.reshape(local_heads, head_dim, width), "seq", scatter_dimension=2, tiled=True
        ),
        lax.psum_scatter(grad_out_bias, "seq", scatter_dimension=0, tiled=True),
        lax.psum_scatter(grad_gain_two, "seq", scatter_dimension=0, tiled=True),
        lax.psum_scatter(grad_shift_two, "seq", scatter_dimension=0, tiled=True),
        lax.psum_scatter(grad_up, "seq", scatter_dimension=0, tiled=True),
        lax.psum_scatter(
            grad_up_bias.reshape(up_bias_full.shape), "seq", scatter_dimension=1, tiled=True
        ),
        lax.psum_scatter(grad_down, "seq", scatter_dimension=1, tiled=True),
        lax.psum_scatter(grad_down_bias, "seq", scatter_dimension=0, tiled=True),
    )
    return (
        jnp.stack(outputs),
        jnp.stack(input_grads),
        reduced[0],
        reduced[1],
        reduced[2],
        reduced[3],
        reduced[4],
        reduced[5],
        reduced[6],
        reduced[7],
        reduced[8],
        reduced[9],
        reduced[10],
        reduced[11],
        reduced[12],
    )


ROWS = ("zh", "zl", "x", "c")
GROUP = ("c", "zl", "y")
PARTS = ("zh", "x")
LOW = jnp.bfloat16
WIDE = jnp.float32


def swap(value, axis):
    return lax.ppermute(value, axis, [(0, 1), (1, 0)])


def flip_where(bit, value, axis):
    return jnp.where(bit == 1, jnp.flip(value, axis), value)


def to_own_order(value, zh, x):
    lead, width = value.shape[:-1], value.shape[-1]
    value = value.reshape(lead + (2, 2, 2, 2, width // 16))
    value = jnp.swapaxes(value, -4, -3)
    value = flip_where(zh, value, -5)
    value = flip_where(x, value, -4)
    return value.reshape(lead + (width,))


def from_own_order(value, zh, x):
    lead, width = value.shape[:-1], value.shape[-1]
    value = value.reshape(lead + (2, 2, 2, 2, width // 16))
    value = flip_where(zh, value, -5)
    value = flip_where(x, value, -4)
    value = jnp.swapaxes(value, -4, -3)
    return value.reshape(lead + (width,))


def tie(*values):
    return lax.optimization_barrier(values)


def dot_to(left, right, dims):
    return lax.dot_general(left, right, (dims, ((), ())), preferred_element_type=WIDE)


def gather_over(value, axes, bits):
    for axis, bit in zip(axes, bits):
        other = swap(value, axis)
        value = jnp.where(
            bit == 0,
            jnp.concatenate([value, other], axis=0),
            jnp.concatenate([other, value], axis=0),
        )
    return value


def reduce_rows(value, zh, zl, x, c):
    value = value.reshape(2, 2, 2, 2, -1)
    for axis, at, bit in (("c", 3, c), ("zl", 1, zl), ("x", 1, x), ("zh", 0, zh)):
        keep = lax.dynamic_index_in_dim(value, bit, at, keepdims=False)
        send = lax.dynamic_index_in_dim(value, 1 - bit, at, keepdims=False)
        value = keep + swap(send, axis)
    return value


BLOCK_Q = 256
BLOCK_A = 512
NEVER = -1e30


def chunks(bits_ref, width):
    run = width // 8
    for at in range(8):
        zh, x, zl = at // 4, at // 2 % 2, at % 2
        theirs = ((zh ^ bits_ref[0]) * 2 + zl) * 2 + (x ^ bits_ref[1])
        yield at * run, pl.multiple_of(theirs * run, run)


def norm_kernel(bits_ref, x_ref, gain_ref, shift_ref, router_ref, out_ref, logits_ref):
    width = x_ref.shape[1]
    rows = x_ref[...].astype(WIDE)
    mean = jnp.mean(rows, axis=-1, keepdims=True)
    center = rows - mean
    inverse = lax.rsqrt(jnp.mean(center * center, axis=-1, keepdims=True) + EPSILON)
    logits = None
    for mine, theirs in chunks(bits_ref, width):
        at = slice(mine, mine + width // 8)
        part = (x_ref[:, pl.ds(theirs, width // 8)].astype(WIDE) - mean) * inverse
        low = (part * gain_ref[:, at] + shift_ref[:, at]).astype(LOW)
        out_ref[:, at] = low
        got = dot_to(low, router_ref[:, at], ((1,), (1,)))
        logits = got if logits is None else logits + got
    logits_ref[...] = logits


def norm_rows(bits, rows, gain, shift, router):
    length, width = rows.shape
    n = router.shape[0]
    return pl.pallas_call(
        norm_kernel,
        grid_spec=pltpu.PrefetchScalarGridSpec(
            num_scalar_prefetch=1,
            grid=(length // BLOCK_Q,),
            in_specs=[
                pl.BlockSpec((BLOCK_Q, width), lambda i, bits: (i, 0)),
                pl.BlockSpec((1, width), lambda i, bits: (0, 0)),
                pl.BlockSpec((1, width), lambda i, bits: (0, 0)),
                pl.BlockSpec((n, width), lambda i, bits: (0, 0)),
            ],
            out_specs=[
                pl.BlockSpec((BLOCK_Q, width), lambda i, bits: (i, 0)),
                pl.BlockSpec((BLOCK_Q, n), lambda i, bits: (i, 0)),
            ],
        ),
        out_shape=[
            jax.ShapeDtypeStruct((length, width), LOW),
            jax.ShapeDtypeStruct((length, n), WIDE),
        ],
        name="norm_rows",
    )(bits, rows, gain, shift, router)


def gate_kernel(bits_ref, x_ref, gate_ref, out_ref):
    width = x_ref.shape[1]
    gate = gate_ref[...]
    for mine, theirs in chunks(bits_ref, width):
        part = x_ref[:, pl.ds(theirs, width // 8)].astype(WIDE) * gate
        out_ref[:, mine : mine + width // 8] = part.astype(LOW)


def gate_rows(bits, rows, gate):
    length, width = rows.shape
    return pl.pallas_call(
        gate_kernel,
        grid_spec=pltpu.PrefetchScalarGridSpec(
            num_scalar_prefetch=1,
            grid=(length // BLOCK_Q,),
            in_specs=[
                pl.BlockSpec((BLOCK_Q, width), lambda i, bits: (i, 0)),
                pl.BlockSpec((BLOCK_Q, 1), lambda i, bits: (i, 0)),
            ],
            out_specs=pl.BlockSpec((BLOCK_Q, width), lambda i, bits: (i, 0)),
        ),
        out_shape=jax.ShapeDtypeStruct((length, width), LOW),
        name="gate_rows",
    )(bits, rows, gate)


def add_dots(left_ref, pieces, start=None):
    at, total = 0, start
    for piece in pieces:
        n = piece.shape[0]
        part = dot_to(left_ref[:, at : at + n], piece[...], ((1,), (0,)))
        total = part if total is None else total + part
        at += n
    return total


def row_spec(steps, rows, width):
    half = steps // 2
    return pl.BlockSpec((rows, width), lambda i, bit: ((i + (1 - bit[0]) * half) % steps, 0))


def fixed(value):
    return pl.BlockSpec(value.shape, lambda *_: (0, 0))


def hidden_kernel(cuts, h_ref, active_ref, bias_ref, *refs):
    pieces, (relu_ref, hidden_ref) = refs[:-2], refs[-2:]
    at, used = 0, 0
    for n in cuts:
        group = pieces[used : used + n]
        used += n
        width = group[0].shape[1]
        total = add_dots(h_ref, group, bias_ref[:, at : at + width])
        relu = jnp.maximum(total, 0.0) * active_ref[...]
        relu_ref[:, at : at + width] = relu
        hidden_ref[:, at : at + width] = (relu * relu).astype(LOW)
        at += width


def hidden_rows(normed, active, bias, groups):
    length, width = normed.shape
    units = bias.shape[1]
    rows = BLOCK_Q
    pieces = [p for group in groups for p in group]
    return pl.pallas_call(
        functools.partial(hidden_kernel, tuple(len(g) for g in groups)),
        grid=(length // rows,),
        in_specs=[
            pl.BlockSpec((rows, width), lambda i: (i, 0)),
            pl.BlockSpec((rows, 1), lambda i: (i, 0)),
            fixed(bias),
        ]
        + [fixed(p) for p in pieces],
        out_specs=[pl.BlockSpec((rows, units), lambda i: (i, 0))] * 2,
        out_shape=[
            jax.ShapeDtypeStruct((length, units), WIDE),
            jax.ShapeDtypeStruct((length, units), LOW),
        ],
        name="hidden_rows",
    )(normed, active, bias, *pieces)


def ffn_kernel(cuts_down, cuts_up, bit_ref, dz_ref, relu_ref, *refs):
    du_ref, dh_ref = refs[-2:]
    n_down = sum(cuts_down)
    downs, ups = refs[:n_down], refs[n_down:-2]
    at, used = 0, 0
    parts = []
    for n in cuts_down:
        group = downs[used : used + n]
        used += n
        grad, col = None, 0
        for piece in group:
            k = piece.shape[1]
            part = dot_to(dz_ref[:, col : col + k], piece[...], ((1,), (1,)))
            grad = part if grad is None else grad + part
            col += k
        m = grad.shape[1]
        du = (grad * 2.0 * relu_ref[:, at : at + m]).astype(LOW)
        du_ref[:, at : at + m] = du
        parts.append((at, m, du))
        at += m
    for j in range(cuts_up[0]):
        total, used = None, 0
        for g, n in enumerate(cuts_up):
            piece = ups[used + j]
            used += n
            part = dot_to(parts[g][2], piece[...], ((1,), (1,)))
            total = part if total is None else total + part
        k = total.shape[1]
        dh_ref[:, j * k : (j + 1) * k] = total.astype(LOW)


def ffn_rows(bit, down_grad, relu, down_groups, up_groups):
    length, width = down_grad.shape
    units = relu.shape[1]
    rows = BLOCK_Q
    steps = length // rows
    downs = [p for group in down_groups for p in group]
    ups = [p for group in up_groups for p in group]
    return pl.pallas_call(
        functools.partial(
            ffn_kernel, tuple(len(g) for g in down_groups), tuple(len(g) for g in up_groups)
        ),
        grid_spec=pltpu.PrefetchScalarGridSpec(
            num_scalar_prefetch=1,
            grid=(steps,),
            in_specs=[row_spec(steps, rows, width), row_spec(steps, rows, units)]
            + [fixed(p) for p in downs]
            + [fixed(p) for p in ups],
            out_specs=[
                row_spec(steps, rows, units),
                pl.BlockSpec((rows, width), lambda i, bit: (i, 0)),
            ],
        ),
        out_shape=[
            jax.ShapeDtypeStruct((length, units), LOW),
            jax.ShapeDtypeStruct((length, width), LOW),
        ],
        name="ffn_rows",
    )(bit, down_grad, relu, *downs, *ups)


def wide_kernel(cuts, left_ref, *refs):
    pieces, out_ref = refs[:-1], refs[-1]
    for j in range(cuts[0]):
        total, used, at = None, 0, 0
        for n in cuts:
            piece = pieces[used + j]
            used += n
            k = piece.shape[0]
            part = dot_to(left_ref[:, at : at + k], piece[...], ((1,), (0,)))
            total = part if total is None else total + part
            at += k
        m = total.shape[1]
        out_ref[:, j * m : (j + 1) * m] = total.astype(LOW)


def wide_rows(left, groups):
    length, depth = left.shape
    rows = BLOCK_Q
    pieces = [p for group in groups for p in group]
    width = sum(p.shape[1] for p in groups[0])
    return pl.pallas_call(
        functools.partial(wide_kernel, tuple(len(g) for g in groups)),
        grid=(length // rows,),
        in_specs=[pl.BlockSpec((rows, depth), lambda i: (i, 0))] + [fixed(p) for p in pieces],
        out_specs=pl.BlockSpec((rows, width), lambda i: (i, 0)),
        out_shape=jax.ShapeDtypeStruct((length, width), LOW),
        name="wide_rows",
    )(left, *pieces)


def own_kernel(bits_ref, a_ref, b_ref, a_out, b_out):
    width = a_ref.shape[1]
    for mine, theirs in chunks(bits_ref, width):
        at = slice(mine, mine + width // 8)
        a_out[:, at] = a_ref[:, pl.ds(theirs, width // 8)].astype(WIDE)
        b_out[:, at] = b_ref[:, pl.ds(theirs, width // 8)].astype(WIDE)


def own_rows(bits, a, b):
    shape = jax.ShapeDtypeStruct(a.shape, WIDE)
    whole = pl.BlockSpec(a.shape, lambda i, bits: (0, 0))
    return pl.pallas_call(
        own_kernel,
        grid_spec=pltpu.PrefetchScalarGridSpec(
            num_scalar_prefetch=1, grid=(1,), in_specs=[whole, whole], out_specs=[whole, whole]
        ),
        out_shape=[shape, shape],
        name="own_rows",
    )(bits, a, b)


def home_kernel(bits_ref, a_ref, out_ref):
    width = a_ref.shape[1]
    for mine, theirs in chunks(bits_ref, width):
        part = a_ref[:, mine : mine + width // 8]
        out_ref[:, pl.ds(theirs, width // 8)] = part.astype(LOW)


def home_rows(bits, a):
    whole = pl.BlockSpec(a.shape, lambda i, bits: (0, 0))
    return pl.pallas_call(
        home_kernel,
        grid_spec=pltpu.PrefetchScalarGridSpec(
            num_scalar_prefetch=1, grid=(1,), in_specs=[whole], out_specs=whole
        ),
        out_shape=jax.ShapeDtypeStruct(a.shape, LOW),
        name="home_rows",
    )(bits, a)


def first_kernel(
    bits_ref, sum_ref, router_ref, rows_ref, resid_ref, gain_ref, out_ref, sums_ref
):
    grad = sum_ref[...] + router_ref[...]
    rows = rows_ref[...]
    gain = gain_ref[...]
    _, scaled, inverse = norm_forward(rows, gain, 0.0)
    sums_ref[0:1, :] = jnp.sum(grad * scaled, axis=0, keepdims=True)
    sums_ref[1:2, :] = jnp.sum(grad, axis=0, keepdims=True)
    out = (resid_ref[...] + norm_backward(grad, scaled, inverse, gain)).astype(LOW)
    width = out.shape[1]
    for mine, theirs in chunks(bits_ref, width):
        out_ref[:, pl.ds(theirs, width // 8)] = out[:, mine : mine + width // 8]


def first_back(bits, normed_sum, router_part, rows, resid_grad, gain):
    whole = pl.BlockSpec(rows.shape, lambda i, bits: (0, 0))
    width = rows.shape[1]
    return pl.pallas_call(
        first_kernel,
        grid_spec=pltpu.PrefetchScalarGridSpec(
            num_scalar_prefetch=1,
            grid=(1,),
            in_specs=[whole] * 4 + [pl.BlockSpec((1, width), lambda i, bits: (0, 0))],
            out_specs=[whole, pl.BlockSpec((2, width), lambda i, bits: (0, 0))],
        ),
        out_shape=[
            jax.ShapeDtypeStruct(rows.shape, LOW),
            jax.ShapeDtypeStruct((2, width), WIDE),
        ],
        name="first_back",
    )(bits, normed_sum, router_part, rows, resid_grad, gain)


def qkv_kernel(h_ref, *refs):
    pieces, (bias_ref, cos_ref, sin_ref, out_ref) = refs[:-4], refs[-4:]
    total = add_dots(h_ref, pieces, bias_ref[...])
    turned = out_ref.shape[1] // HEAD_DIM * 2 // 3
    cosine, sine = cos_ref[...], sin_ref[...]
    for j in range(out_ref.shape[1] // HEAD_DIM):
        at = slice(j * HEAD_DIM, (j + 1) * HEAD_DIM)
        part = total[:, at]
        if j < turned:
            part = part * cosine + pltpu.roll(part, HEAD_DIM // 2, 1) * sine
        out_ref[:, at] = part.astype(LOW)


def qkv_rows(normed, pieces, bias, cosine, sine):
    length, width = normed.shape
    out = bias.shape[1]
    rows = BLOCK_Q
    return pl.pallas_call(
        qkv_kernel,
        grid=(length // rows,),
        in_specs=[pl.BlockSpec((rows, width), lambda i: (i, 0))]
        + [fixed(p) for p in pieces]
        + [
            fixed(bias),
            pl.BlockSpec((rows, HEAD_DIM), lambda i: (i, 0)),
            pl.BlockSpec((rows, HEAD_DIM), lambda i: (i, 0)),
        ],
        out_specs=pl.BlockSpec((rows, out), lambda i: (i, 0)),
        out_shape=jax.ShapeDtypeStruct((length, out), LOW),
        name="qkv_rows",
    )(normed, *pieces, bias, cosine, sine)


def attend_kernel(q_ref, k_ref, v_ref, key_ref, span_ref, active_ref, out_ref, lse_ref):
    scores = dot_to(k_ref[...], q_ref[...], ((1,), (1,))) * (HEAD_DIM**-0.5)
    key = key_ref[...]
    allowed = (key >= span_ref[0:1, :]) & (key <= span_ref[1:2, :])
    scores = jnp.where(allowed, scores, NEVER)
    top = jnp.max(scores, axis=0, keepdims=True)
    weights = jnp.exp(scores - top)
    total = jnp.sum(weights, axis=0, keepdims=True)
    probs = (weights * (1.0 / total)).astype(LOW)
    mixed = dot_to(probs, v_ref[...], ((0,), (0,)))
    out_ref[...] = (mixed * active_ref[0]).astype(LOW)
    lse_ref[0] = top + jnp.log(total)


def turn_back(grad, cosine, sine):
    lane = lax.broadcasted_iota(jnp.int32, grad.shape, 1)
    moved = pltpu.roll(grad * sine, HEAD_DIM // 2, 1)
    return grad * cosine + jnp.where(lane < HEAD_DIM // 2, moved, -moved)


def attend_back_kernel(
    q_ref, k_ref, v_ref, da_ref, w_ref, active_ref, lse_ref,
    key_ref, span_ref, cos_ref, sin_ref, out_ref, dk_sum, dv_sum,
):
    head, step = pl.program_id(0), pl.program_id(1)
    inner = out_ref.shape[1] // 3

    @pl.when(step == 0)
    def _():
        dk_sum[...] = jnp.zeros_like(dk_sum)
        dv_sum[...] = jnp.zeros_like(dv_sum)

    scale = HEAD_DIM**-0.5
    query, key = q_ref[...], k_ref[...]
    grad = dot_to(da_ref[...], w_ref[...], ((1,), (1,)))
    grad = (grad * active_ref[0]).astype(LOW)
    scores = dot_to(key, query, ((1,), (1,))) * scale
    place = key_ref[...]
    allowed = (place >= span_ref[0:1, :]) & (place <= span_ref[1:2, :])
    probs = jnp.exp(jnp.where(allowed, scores, NEVER) - lse_ref[0])
    prob_grad = dot_to(v_ref[...], grad, ((1,), (1,)))
    delta = jnp.sum(probs * prob_grad, axis=0, keepdims=True)
    score_grad = (probs * (prob_grad - delta) * scale).astype(LOW)
    dv_sum[...] += dot_to(probs.astype(LOW), grad, ((1,), (0,)))
    dk_sum[...] += dot_to(score_grad, query, ((1,), (0,)))
    dq = dot_to(score_grad, key, ((0,), (0,)))
    at = pl.ds(pl.multiple_of(step * BLOCK_A, BLOCK_A), BLOCK_A)
    col = pl.multiple_of(head * HEAD_DIM, HEAD_DIM)
    dq = turn_back(dq, cos_ref[at, :], sin_ref[at, :])
    out_ref[at, pl.ds(col, HEAD_DIM)] = dq.astype(LOW)

    @pl.when(step == pl.num_programs(1) - 1)
    def _():
        dk = turn_back(dk_sum[...], cos_ref[...], sin_ref[...])
        out_ref[:, pl.ds(inner + col, HEAD_DIM)] = dk.astype(LOW)
        out_ref[:, pl.ds(2 * inner + col, HEAD_DIM)] = dv_sum[...].astype(LOW)


def attend(qkv, key_place, span, active, heads):
    length = qkv.shape[0]
    d = HEAD_DIM
    n = heads
    return pl.pallas_call(
        attend_kernel,
        grid=(heads, length // BLOCK_A),
        in_specs=[
            pl.BlockSpec((BLOCK_A, d), lambda h, i: (i, h)),
            pl.BlockSpec((length, d), lambda h, i: (0, n + h)),
            pl.BlockSpec((length, d), lambda h, i: (0, 2 * n + h)),
            pl.BlockSpec((length, 1), lambda h, i: (0, 0)),
            pl.BlockSpec((2, BLOCK_A), lambda h, i: (0, i)),
            pl.BlockSpec((1, BLOCK_A, 1), lambda h, i: (h, i, 0)),
        ],
        out_specs=[
            pl.BlockSpec((BLOCK_A, d), lambda h, i: (i, h)),
            pl.BlockSpec((1, 1, BLOCK_A), lambda h, i: (h, 0, i)),
        ],
        out_shape=[
            jax.ShapeDtypeStruct((length, heads * d), LOW),
            jax.ShapeDtypeStruct((heads, 1, length), WIDE),
        ],
        name="attend",
    )(qkv, qkv, qkv, key_place, span, active)


def attend_back(qkv, out_grad, w_out, active, lse, key_place, span, cosine, sine, heads):
    length, width = out_grad.shape
    d = HEAD_DIM
    n = heads
    return pl.pallas_call(
        attend_back_kernel,
        grid=(heads, length // BLOCK_A),
        in_specs=[
            pl.BlockSpec((BLOCK_A, d), lambda h, i: (i, h)),
            pl.BlockSpec((length, d), lambda h, i: (0, n + h)),
            pl.BlockSpec((length, d), lambda h, i: (0, 2 * n + h)),
            pl.BlockSpec((BLOCK_A, width), lambda h, i: (i, 0)),
            pl.BlockSpec((d, width), lambda h, i: (h, 0)),
            pl.BlockSpec((1, BLOCK_A, 1), lambda h, i: (h, i, 0)),
            pl.BlockSpec((1, 1, BLOCK_A), lambda h, i: (h, 0, i)),
            pl.BlockSpec((length, 1), lambda h, i: (0, 0)),
            pl.BlockSpec((2, BLOCK_A), lambda h, i: (0, i)),
            pl.BlockSpec((length, d), lambda h, i: (0, 0)),
            pl.BlockSpec((length, d), lambda h, i: (0, 0)),
        ],
        out_specs=pl.BlockSpec((length, 3 * heads * d), lambda h, i: (0, 0)),
        out_shape=jax.ShapeDtypeStruct((length, 3 * heads * d), LOW),
        scratch_shapes=[pltpu.VMEM((length, d), WIDE), pltpu.VMEM((length, d), WIDE)],
        name="attend_back",
    )(qkv, qkv, qkv, out_grad, w_out, active, lse, key_place, span, cosine, sine)


def grouped(
    tokens,
    cotangent,
    head_groups,
    ffn_widths,
    doc_lengths,
    first_gain,
    first_shift,
    router_weight,
    in_weight,
    in_bias,
    out_weight,
    out_bias,
    second_gain,
    second_shift,
    up_weight,
    up_bias,
    down_weight,
    down_bias,
):
    zh, zl, x, c, y = (lax.axis_index(a) for a in ("zh", "zl", "x", "c", "y"))
    micro, tok_dev, width = tokens.shape
    half = tok_dev // 2
    own = 4 * half
    length = 16 * tok_dev
    block = width // 16
    tp_heads, head_dim = in_weight.shape[2:]
    heads = tp_heads // 4
    inner = heads * head_dim
    tp_units = up_weight.shape[1]
    units = tp_units // 4
    batch = zh * 2 + x
    part = zl * 2 + c
    place = (c * 2 + zl) * 2 + y

    def exchange(value):
        return lax.all_to_all(value, ("zl", "c"), 0, 0, tiled=True)

    def keep_and_send(value, bit, at):
        return (
            lax.dynamic_index_in_dim(value, bit, at, keepdims=False),
            lax.dynamic_index_in_dim(value, 1 - bit, at, keepdims=False),
        )

    def across(pieces):
        return (
            pieces[0],
            swap(pieces[1], "x"),
            swap(pieces[2], "zh"),
            lax.ppermute(pieces[3], PARTS, [(i, i ^ 3) for i in range(4)]),
        )

    def to_batch(value):
        value = lax.dynamic_slice_in_dim(value, y * half, half, 1)
        return across(
            [lax.dynamic_index_in_dim(value, batch ^ k, 0, keepdims=False) for k in range(4)]
        )

    bits = jnp.stack([zh, x]).astype(jnp.int32)
    core = c.reshape(1).astype(jnp.int32)
    e_in = exchange(jnp.moveaxis(in_weight.reshape(block, 3, 4, heads, head_dim), 2, 0))
    e_in = e_in.reshape(4 * block, 3 * inner)

    def rows_of_block(value):
        value = value.astype(LOW).reshape(-1)
        return jnp.pad(value, (0, -value.shape[0] % block)).reshape(-1, block)

    small = jnp.concatenate(
        [
            rows_of_block(v)
            for v in (
                first_gain,
                first_shift,
                second_gain,
                second_shift,
                out_bias,
                down_bias,
                router_weight,
                up_bias,
                head_groups,
                ffn_widths,
                in_bias,
            )
        ],
        axis=0,
    )
    n_small = small.shape[0]
    small_rows = -(-n_small * block // width)
    small = jnp.pad(small.reshape(-1), (0, small_rows * width - n_small * block))
    small = small.reshape(small_rows, width)
    mine_of = lax.dynamic_slice_in_dim(tokens, y * half, half, 1)
    token_pieces = across(
        [
            jnp.concatenate(
                [lax.dynamic_index_in_dim(mine_of, batch ^ k, 0, keepdims=False), small], axis=0
            )
            for k in range(4)
        ]
    )
    small = jnp.stack([p[half:].reshape(-1)[: n_small * block] for p in token_pieces])
    small = gather_over(small[None], ("c", "zl"), (c, zl))
    tokens_own = jnp.concatenate([p[:half] for p in token_pieces], axis=0)

    index = jnp.arange(length, dtype=jnp.int32).reshape(2, 2, 2, 2, 2, half)

    def by_place(value):
        lead = tuple(range(value.ndim - 6))
        at = value.ndim - 6
        value = jnp.transpose(value, lead + tuple(at + i for i in (3, 1, 4, 0, 2, 5)))
        return value.reshape(value.shape[: value.ndim - 6] + (length,))

    positions = by_place(index) ^ (zh * (8 * tok_dev) + x * (2 * tok_dev))
    ends = jnp.cumsum(lax.dynamic_index_in_dim(doc_lengths, batch, 0, keepdims=False))
    first = jnp.max(jnp.where(ends[:, None] <= positions[None, :], ends[:, None], 0), axis=0)
    span = jnp.stack([first, positions])
    key_place = positions[:, None]
    cosine, sine = rotary_tables(positions)
    lane = jnp.arange(HEAD_DIM)[None, :]
    signed = jnp.where(lane < HEAD_DIM // 2, -sine, sine)
    tokens_own, small, e_in, cosine, sine, signed, span, key_place = tie(
        tokens_own, small, e_in, cosine, sine, signed, span, key_place
    )

    tokens_all = lax.all_gather(tokens_own, GROUP, axis=0, tiled=True)
    in_z = swap(e_in, "zh")
    in_x = swap(e_in, "x")
    e_out = exchange(out_weight.reshape(4, inner, block))
    e_out = jnp.moveaxis(e_out, 0, 1).reshape(inner, 4 * block)
    small_own = small.reshape(2, 2, 2, 2, n_small * block).astype(WIDE)
    small_own = jnp.transpose(small_own, (2, 0, 3, 1, 4)).reshape(16, n_small * block)
    n_vec = 6 + 2 * GROUPS
    rows_of = jnp.arange(16) ^ (zh * 8 + x * 2)
    pick = (rows_of[:, None] == jnp.arange(16)[None, :]).astype(WIDE)
    small_all = jnp.dot(pick, small_own[:, n_vec * block :], precision=HIGHEST)
    vectors_f = small_own[:, : n_vec * block].reshape(2, 2, 2, 2, n_vec, block)
    vectors_f = jnp.transpose(vectors_f, (4, 0, 2, 1, 3, 5)).reshape(n_vec, width)
    router = vectors_f[6:].astype(LOW)
    size = up_bias.size
    bias_up = small_all[:, :size].reshape((16,) + up_bias.shape)
    bias_up = jnp.moveaxis(bias_up, 0, 1).reshape(4, units)
    bias_up = lax.dynamic_index_in_dim(bias_up, part, 0, keepdims=True)
    at = size
    size = 2 * micro * tok_dev
    widths = small_own[:, n_vec * block + at : n_vec * block + at + size]
    widths = widths.reshape(16, 2, micro, tok_dev)
    widths = lax.dynamic_index_in_dim(widths, batch, 2, keepdims=False).astype(jnp.int32)
    widths = jnp.swapaxes(widths, 0, 1).reshape(2, 2, 2, 2, 2, 2, half)
    at += size
    bias_in = small_all[:, at : at + in_bias.size].reshape((16,) + in_bias.shape)
    bias_in = jnp.moveaxis(bias_in, 0, 2).reshape(3, 4, heads, head_dim)
    bias_in = lax.dynamic_index_in_dim(bias_in, part, 1, keepdims=False)
    bias_in = bias_in.reshape(1, 3 * inner)
    heads_row, units_row = by_place(widths)
    head_ids = (y * 4 + part) * heads + jnp.arange(heads, dtype=jnp.int32)
    head_active = (head_ids[:, None] // (HEADS // GROUPS) < heads_row[None, :]).astype(WIDE)
    head_active = head_active[:, :, None]
    unit_group = (y * 4 + part) * units // (FF // GROUPS)
    unit_active = (unit_group < units_row).astype(WIDE)[:, None]
    (
        in_z, in_x, e_out, vectors_f, router, bias_in, bias_up, head_active, unit_active,
        cotangent, up_weight,
    ) = tie(
        in_z, in_x, e_out, vectors_f, router, bias_in, bias_up, head_active, unit_active,
        cotangent, up_weight,
    )
    gain_one, shift_one, gain_two, shift_two, bias_out, bias_down = (
        vectors_f[i : i + 1] for i in range(6)
    )

    in_zx = swap(in_z, "x")
    out_z = swap(e_out, "zh")
    cotangent_pieces = to_batch(cotangent)
    e_up = exchange(jnp.moveaxis(up_weight.reshape(block, 4, units), 1, 0))
    e_up = e_up.reshape(4 * block, units)
    normed_low, logits = norm_rows(bits, tokens_all, gain_one, shift_one, router)
    normed_low, in_zx, out_z, e_up, down_weight, logits, e_out, *cotangent_pieces = tie(
        normed_low, in_zx, out_z, e_up, down_weight, logits, e_out, *cotangent_pieces
    )
    cotangent_own = jnp.concatenate(cotangent_pieces, axis=0)
    cotangent_all = lax.all_gather(cotangent_own, GROUP, axis=0, tiled=True)
    def mine(value):
        return lax.dynamic_slice_in_dim(value, place * own, own, 0)

    cut_units = units // 2
    out_zx = swap(out_z, "x")
    out_x = swap(e_out, "x")
    up_x1 = swap(e_up[:, :cut_units], "x")
    up_z1 = swap(e_up[:, :cut_units], "zh")
    e_down = exchange(down_weight.reshape(4, units, block))
    e_down = jnp.moveaxis(e_down, 0, 1).reshape(units, 4 * block)
    w_in = (e_in, in_x, in_z, in_zx)
    qkv = qkv_rows(normed_low, w_in, bias_in, cosine, signed)
    mixed, lse = attend(qkv, key_place, span, head_active, heads)
    w_out = jnp.concatenate([e_out, out_x, out_z, out_zx], axis=1)
    mixed, w_out, e_up, up_x1, up_z1, tokens_own, logits = tie(
        mixed, w_out, e_up, up_x1, up_z1, tokens_own, logits
    )

    part_own = own // 2

    def halves(value):
        return (
            lax.dynamic_slice_in_dim(value, c * (length // 2), length // 2, 0),
            lax.dynamic_slice_in_dim(value, (1 - c) * (length // 2), length // 2, 0),
        )

    def group_second(total):
        total = total.reshape(2, 2, own, width)
        a_keep, a_send = keep_and_send(total[:, :, :part_own], zl, 0)
        b_keep, b_send = keep_and_send(total[:, :, part_own:], y, 1)
        a_got = swap(a_send.astype(LOW), "zl")
        b_got = swap(b_send.astype(LOW), "y")
        return a_keep, b_keep, a_got, b_got

    def group_third(a_keep, b_keep, a_got, b_got):
        a_keep, a_send = keep_and_send(a_keep + a_got.astype(WIDE), y, 0)
        b_keep, b_send = keep_and_send(b_keep + b_got.astype(WIDE), zl, 0)
        a_got = swap(a_send.astype(LOW), "y")
        b_got = swap(b_send.astype(LOW), "zl")
        return jnp.concatenate([a_keep + a_got.astype(WIDE), b_keep + b_got.astype(WIDE)], axis=0)

    attn_here, attn_away = halves(mixed)
    attn_away = dot_to(attn_away, w_out, ((1,), (0,))).astype(LOW)
    attn_away, attn_here, tokens_own, cotangent_own, logits = tie(
        attn_away, attn_here, tokens_own, cotangent_own, logits
    )
    attn_got = swap(attn_away, "c")
    up_x2 = swap(e_up[:, cut_units:], "x")
    up_z2 = swap(e_up[:, cut_units:], "zh")
    up_zx1 = swap(up_z1, "x")
    options = jnp.arange(GROUPS, dtype=jnp.int32)
    attn_prob = jax.nn.softmax(logits[:, :GROUPS], axis=-1)
    ffn_prob = jax.nn.softmax(logits[:, GROUPS:], axis=-1)
    attn_pick = (options[None, :] == heads_row[:, None] - 1).astype(WIDE)
    ffn_pick = (options[None, :] == units_row[:, None] - 1).astype(WIDE)
    attn_gate = GROUPS * jnp.sum(attn_prob * attn_pick, axis=-1, keepdims=True)
    ffn_gate = GROUPS * jnp.sum(ffn_prob * ffn_pick, axis=-1, keepdims=True)
    attn_total = dot_to(attn_here, w_out, ((1,), (0,))) + attn_got.astype(WIDE)
    attn_total, attn_gate, ffn_gate, tokens_own, cotangent_own = tie(
        attn_total, attn_gate, ffn_gate, tokens_own, cotangent_own
    )
    attn_total = attn_total.reshape(2, 2, own, width)
    attn_keep, attn_send = keep_and_send(attn_total, y, 1)
    attn_got = swap(attn_send.astype(LOW), "y")
    rows, upstream = own_rows(bits, tokens_own, cotangent_own)
    attn_keep, attn_got, rows, upstream, up_x2, up_z2, cotangent_all, e_down = tie(
        attn_keep, attn_got, rows, upstream, up_x2, up_z2, cotangent_all, e_down
    )
    attn_keep, attn_send = keep_and_send(attn_keep + attn_got.astype(WIDE), zl, 0)
    attn_sum = attn_keep + swap(attn_send.astype(LOW), "zl").astype(WIDE)
    down_x1 = swap(e_down[:cut_units], "x")
    attn_sum, down_x1, e_down = tie(attn_sum, down_x1, e_down)

    attn_branch = attn_sum + bias_out
    attn_gate_own = mine(attn_gate)
    ffn_gate_own = mine(ffn_gate)
    resid = rows + attn_gate_own * attn_branch
    normed_two, scaled_two, inverse_two = norm_forward(resid, gain_two, shift_two)
    normed_two_low = normed_two.astype(LOW)
    normed_two_low, e_down, cotangent_all, up_z2 = tie(
        normed_two_low, e_down, cotangent_all, up_z2
    )
    normed_two_low = lax.all_gather(normed_two_low, GROUP, axis=0, tiled=True)
    down_z1 = swap(e_down[:cut_units], "zh")
    up_zx2 = swap(up_z2, "x")
    down_x2 = swap(e_down[cut_units:], "x")
    down_grad = gate_rows(bits, cotangent_all, ffn_gate)
    down_grad, down_z1, up_zx2, down_x2, e_down = tie(
        down_grad, down_z1, up_zx2, down_x2, e_down
    )
    down_z2 = swap(e_down[cut_units:], "zh")
    down_zx1 = swap(down_z1, "x")
    normed_two_low, down_z2, down_zx1, up_zx1 = tie(normed_two_low, down_z2, down_zx1, up_zx1)

    def columns(value, k):
        return value[:, k * 4 * block : (k + 1) * 4 * block]

    down_zx2 = swap(down_z2, "x")
    w_up = (
        (e_up[:, :cut_units], up_x1, up_z1, up_zx1),
        (e_up[:, cut_units:], up_x2, up_z2, up_zx2),
    )
    relu_part, hidden = hidden_rows(normed_two_low, unit_active, bias_up, w_up)

    def down_piece(k):
        return dot_to(hidden, columns(down_grad, k), ((0,), (0,)))

    relu_part, hidden, down_zx2 = tie(relu_part, hidden, down_zx2)
    w_down = (
        (e_down[:cut_units], down_x1, down_z1, down_zx1),
        (e_down[cut_units:], down_x2, down_z2, down_zx2),
    )
    up_grad, two_part = ffn_rows(core, down_grad, relu_part, w_down, w_up)
    two_away, two_here = two_part[: length // 2], two_part[length // 2 :]
    two_got = swap(two_away, "c")

    def up_piece(k):
        return dot_to(columns(normed_two_low, k), up_grad, ((0,), (0,)))

    down_got3 = swap(down_piece(3).astype(LOW), "x")
    two_total = two_here.astype(WIDE) + two_got.astype(WIDE)
    two_total, hidden, up_grad = tie(two_total, hidden, up_grad)
    two_parts = group_second(two_total)
    up_send3 = up_piece(3).astype(LOW)
    down_send1 = down_piece(1).astype(LOW)
    *two_parts, down_send1, up_send3, up_grad = tie(*two_parts, down_send1, up_send3, up_grad)
    normed_two_grad = group_third(*two_parts)
    up_got3 = swap(up_send3, "x")
    normed_two_grad, hidden, down_grad, up_grad, down_got3 = tie(
        normed_two_grad, hidden, down_grad, up_grad, down_got3
    )
    down_send2 = (down_piece(2) + down_got3.astype(WIDE)).astype(LOW)

    resid_grad = upstream + norm_backward(normed_two_grad, scaled_two, inverse_two, gain_two)
    gated_attn = attn_gate_own * resid_grad
    gated_low = gated_attn.astype(LOW)
    gated_low, hidden, down_grad, up_grad, normed_two_grad, resid_grad, down_send2 = tie(
        gated_low, hidden, down_grad, up_grad, normed_two_grad, resid_grad, down_send2
    )
    attn_out_grad = lax.all_gather(gated_low, GROUP, axis=0, tiled=True)
    down_far1 = swap(down_send2[:cut_units], "zh")
    down_got1 = swap(down_send1, "x")
    w_in = jnp.concatenate(w_in, axis=0)
    ffn_part = wide_rows(hidden, w_down)
    grad_gain_two = jnp.sum(normed_two_grad * scaled_two, axis=0)
    grad_shift_two = jnp.sum(normed_two_grad, axis=0)
    attn_gate_grad = jnp.sum(resid_grad * attn_branch, axis=-1)
    grad_out_bias = jnp.sum(attn_gate_own * resid_grad, axis=0)
    up_send1 = up_piece(1).astype(LOW)
    up_send2 = (up_piece(2) + up_got3.astype(WIDE)).astype(LOW)
    (
        attn_out_grad, ffn_part, up_send1, up_send2, grad_out_bias, grad_gain_two, w_in,
        down_far1, down_send2,
    ) = tie(
        attn_out_grad, ffn_part, up_send1, up_send2, grad_out_bias, grad_gain_two, w_in,
        down_far1, down_send2,
    )
    down_far2 = swap(down_send2[cut_units:], "zh")

    def out_piece(k):
        return dot_to(mixed, columns(attn_out_grad, k), ((0,), (0,)))

    ffn_sum = lax.psum_scatter(ffn_part, GROUP, scatter_dimension=0, tiled=True)
    out_got = swap(jnp.stack([out_piece(1), out_piece(3)]).astype(LOW), "x")
    proj_grad = attend_back(
        qkv, attn_out_grad, w_out, head_active, lse, key_place, span, cosine, sine, heads
    )
    proj_grad, attn_out_grad, down_got1, down_far2, hidden, up_send1, up_send2, out_got = tie(
        proj_grad, attn_out_grad, down_got1, down_far2, hidden, up_send1, up_send2, out_got
    )

    def in_piece(k):
        return dot_to(columns(normed_low, k), proj_grad, ((0,), (0,)))

    one_here, one_away = halves(proj_grad)
    one_away = dot_to(one_away, w_in, ((1,), (1,))).astype(LOW)
    one_away, one_here, proj_grad, hidden, out_got, up_send2 = tie(
        one_away, one_here, proj_grad, hidden, out_got, up_send2
    )
    one_got = swap(one_away, "c")
    up_far = swap(up_send2, "zh")
    in_send3 = in_piece(3).astype(LOW)
    in_got3 = swap(in_send3, "x")
    one_total = dot_to(one_here, w_in, ((1,), (1,))) + one_got.astype(WIDE)
    one_total, proj_grad, in_send3, out_got, up_send1, hidden = tie(
        one_total, proj_grad, in_send3, out_got, up_send1, hidden
    )
    one_parts = group_second(one_total)
    in_send1 = in_piece(1).astype(LOW)
    out_send2 = (out_piece(2) + out_got[1].astype(WIDE)).astype(LOW)
    *one_parts, in_send1, out_send2, in_got3, ffn_sum, up_send1, hidden = tie(
        *one_parts, in_send1, out_send2, in_got3, ffn_sum, up_send1, hidden
    )
    normed_sum = group_third(*one_parts)
    in_got1 = swap(in_send1, "x")
    up_got1 = swap(up_send1, "x")
    out_far = swap(out_send2, "zh")
    in_send2 = (in_piece(2) + in_got3.astype(WIDE)).astype(LOW)
    ffn_branch = ffn_sum.astype(WIDE) + bias_down
    ffn_gate_grad = jnp.sum(upstream * ffn_branch, axis=-1)
    logit_grad = jnp.concatenate(
        [
            gate_logit_grad(mine(attn_prob), mine(attn_pick), attn_gate_grad),
            gate_logit_grad(mine(ffn_prob), mine(ffn_pick), ffn_gate_grad),
        ],
        axis=-1,
    )
    router_part = jnp.dot(logit_grad, vectors_f[6:], precision=HIGHEST)

    def both_halves(value, other):
        def batches(v):
            v = v.reshape(2, 2, half, width)
            return flip_where(x, flip_where(zh, v, 0), 1).reshape(4, half, width)

        value, other = batches(value), batches(other)
        return jnp.where(
            y == 0,
            jnp.concatenate([value, other], axis=1),
            jnp.concatenate([other, value], axis=1),
        )

    def spread(rows, cut):
        rows = from_own_order(rows, zh, x)
        return jnp.swapaxes(rows.reshape(cut, 16, block), 0, 1).reshape(16, cut * block)

    normed_sum, in_send2, router_part, ffn_branch, logit_grad, up_far, hidden = tie(
        normed_sum, in_send2, router_part, ffn_branch, logit_grad, up_far, hidden
    )

    in_far = swap(in_send2, "zh")
    tokens_low, last = first_back(bits, normed_sum, router_part, rows, resid_grad, gain_one)
    tokens_low = tokens_low.reshape(4, half, width)
    tokens_low, last, ffn_branch, logit_grad, up_grad, out_far, up_far, hidden = tie(
        tokens_low, last, ffn_branch, logit_grad, up_grad, out_far, up_far, hidden
    )
    tokens_pieces = across([tokens_low[k] for k in range(4)])
    block_low = home_rows(bits, resid + ffn_gate_own * ffn_branch).reshape(4, half, width)
    normed_own = mine(normed_low)
    grad_router = jnp.dot(logit_grad.T, normed_own.astype(WIDE), precision=HIGHEST)
    grad_down_bias = jnp.sum(ffn_gate_own * upstream, axis=0)
    grad_up_bias = jnp.sum(up_grad.astype(WIDE), axis=0)
    grad_in_bias = jnp.sum(proj_grad.astype(WIDE), axis=0).reshape(3, heads, head_dim)
    sums = jnp.stack([grad_out_bias, grad_gain_two, grad_shift_two, grad_down_bias])
    sums = spread(jnp.concatenate([last, sums, grad_router], axis=0), n_vec)
    chosen = (jnp.arange(4) == part).astype(WIDE)
    spread_in = (grad_in_bias[:, None] * chosen[None, :, None, None]).reshape(
        3, tp_heads, 16, head_dim // 16
    )
    spread_in = jnp.moveaxis(spread_in, 2, 0).reshape(16, -1)
    spread_up = (grad_up_bias[None, :] * chosen[:, None]).reshape(up_bias.shape[0], 16, block)
    spread_up = jnp.moveaxis(spread_up, 1, 0).reshape(16, -1)
    total = jnp.concatenate([sums, spread_in, spread_up], axis=1)
    down_far = jnp.concatenate([down_far1, down_far2], axis=0)
    down_home = (down_piece(0) + down_got1.astype(WIDE) + down_far.astype(WIDE)).astype(LOW)
    down_home = exchange(jnp.moveaxis(down_home.reshape(units, 4, block), 1, 0))
    up_home = (up_piece(0) + up_got1.astype(WIDE) + up_far.astype(WIDE)).astype(LOW)
    up_home = exchange(up_home.reshape(4, block, units))
    out_home = (out_piece(0) + out_got[0].astype(WIDE) + out_far.astype(WIDE)).astype(LOW)
    *tokens_pieces, total, block_low, up_home, out_home, in_got1, down_home, in_far = tie(
        *tokens_pieces, total, block_low, up_home, out_home, in_got1, down_home, in_far
    )
    total = reduce_rows(total, zh, zl, x, c)
    tokens_grad = jnp.stack(tokens_pieces)
    tokens_other = swap(tokens_grad, "y")
    block_out = jnp.stack(across([block_low[k] for k in range(4)]))
    out_home = exchange(jnp.moveaxis(out_home.reshape(inner, 4, block), 1, 0))
    in_home = (in_piece(0) + in_got1.astype(WIDE) + in_far.astype(WIDE)).astype(LOW)
    tokens_other, block_out, in_home, out_home, total = tie(
        tokens_other, block_out, in_home, out_home, total
    )
    block_other = swap(block_out, "y")
    in_home = exchange(in_home.reshape(4, block, 3 * inner)).reshape(4, block, 3, heads, head_dim)
    at = n_vec * block
    shared = total[:at]
    shared = (shared + swap(shared, "y")).reshape(n_vec, block)
    early = total[at:]
    return (
        both_halves(block_out, block_other),
        both_halves(tokens_grad, tokens_other).astype(WIDE),
        shared[0],
        shared[1],
        shared[6:],
        jnp.transpose(in_home, (1, 2, 0, 3, 4)).reshape(in_weight.shape).astype(WIDE),
        early[: in_bias.size].reshape(in_bias.shape),
        out_home.reshape(out_weight.shape).astype(WIDE),
        shared[2],
        shared[3],
        shared[4],
        jnp.swapaxes(up_home, 0, 1).reshape(up_weight.shape).astype(WIDE),
        early[in_bias.size :].reshape(up_bias.shape),
        down_home.reshape(down_weight.shape).astype(WIDE),
        shared[5],
    )


def solution(mesh):
    body, seq, tp = local, "seq", "tp"
    if mesh.shape["seq"] == 16 and mesh.shape["tp"] == 2:
        mesh = Mesh(mesh.devices.reshape(2, 2, 2, 2, 2), ROWS + ("y",))
        body, seq, tp = grouped, ROWS, "y"
    return jax.shard_map(
        body,
        mesh=mesh,
        in_specs=(
            P(None, seq, None),
            P(None, seq, None),
            P(None, seq),
            P(None, seq),
            P(),
            P(seq),
            P(seq),
            P(None, seq),
            P(seq, None, tp, None),
            P(None, tp, seq),
            P(tp, None, seq),
            P(seq),
            P(seq),
            P(seq),
            P(seq, tp),
            P(tp, seq),
            P(tp, seq),
            P(seq),
        ),
        out_specs=(
            P(None, seq, None),
            P(None, seq, None),
            P(seq),
            P(seq),
            P(None, seq),
            P(seq, None, tp, None),
            P(None, tp, seq),
            P(tp, None, seq),
            P(seq),
            P(seq),
            P(seq),
            P(seq, tp),
            P(tp, seq),
            P(tp, seq),
            P(seq),
        ),
        check_vma=False,
    )
```
